256 devices in a mesh: seq: 64 (over x, z, y_lo), tp: 4 (over y_hi, core).
Axes of the slice: x: 4, y: 4 (y_hi: 2, y_lo: 2; y = y_hi * 2 + y_lo), z: 8, core: 2. Of those that a mesh axis runs over, the one named last changes fastest.
Arguments:
- state: bfloat16 [18432, 3072], P('seq', 'tp'), may hold values from -40 to 40
- latent: float32 [9216, 64], P('seq'), may hold values from -6 to 6
- w_mod: bfloat16 [3072, 9216], P('tp', 'seq'), may hold values from -0.109375 to 0.109375
- w_qkv: bfloat16 [3072, 3, 1536], P(None, None, 'tp'), may hold values from -1 to 1
- w_mlp_in: bfloat16 [3072, 6144], P('seq', 'tp'), may hold values from -0.109375 to 0.109375
- q_gain: float32 [12, 128], P('tp'), may hold values from 1.4 to 6.6
- k_gain: float32 [12, 128], P('tp'), may hold values from 1.4 to 6.6
- w_out: bfloat16 [1536, 3072], P('tp'), may hold values from -0.15625 to 0.15625
- w_mlp_down: bfloat16 [3072, 6144], P('seq', 'tp'), may hold values from -0.078125 to 0.078125
- w_final: bfloat16 [3072, 64], P('tp'), may hold values from -0.109375 to 0.109375
- text_len: int32 [2, 2], replicated, may hold values from 64 to 512, as said below
- rope_ids: int32 [3, 18432], P(None, 'seq'), may hold values from 0 to 126, as said below
- guidance: int32 [2], replicated, may hold values from 2 to 12
- step_index: int32 [2], replicated, may hold values from 0 to 27
Outputs:
- new_state: bfloat16 [18432, 3072], P('seq', 'tp')
- next_latent: float32 [9216, 64], P('seq')
- state_norm: float32 [2], replicated
- top_score: float32 [2], replicated
The draws below stay inside these ranges and needn't reach their ends.
Inputs may be any that keep to these rules, and one draw needn't show every extreme that they name: `text_len`: one of the entries equals 512, a different one from draw to draw. `rope_ids`: text positions have ids (0, 0, 0); image position p >= 512 has (frame, row offset + (p - 512) // 64, column offset + (p - 512) % 64), with a frame of 0 or 1 and offsets of 0 to 63 for each request, the same in both halves; one request has row offset 63 and one has column offset 63.
All inputs are finite; a program needn't handle non-finite values.
Results may differ from the reference program's by a relative error of at most 0.008.
Values may be sent and summed in bfloat16 or wider, within the bound.
No kernel may reach another device: no remote copies, remote signals or barrier semaphores. Data moves between devices by JAX's collectives and lax.ppermute only.
A program may use at most 192 MiB of HBM per device.

```python
import math
import jax
import jax.numpy as jnp
from jax import lax

D = 3072
HD = 128
CH = 64
HEADS = 12
FF = 6144
REQ = 2
TOK_DEV = 288
TXT = 512
IMG_W = 64
STEPS = 28
BLOCKS = 16
SEQ_LEN = 4608
SEQ_ROWS = 18432


def draw_state(key, part):
    ramp = jnp.arange(SEQ_ROWS, dtype=jnp.float32) / SEQ_ROWS
    rough = jnp.clip(jax.random.normal(jax.random.fold_in(key, 1), (SEQ_ROWS, D), jnp.float32), -5.0, 5.0)
    values = rough * (0.5 + ramp)[:, None]
    return values.astype(jnp.bfloat16)


def draw_w_qkv(key, part):
    base = jnp.clip(jax.random.normal(jax.random.fold_in(key, 1), (D, 3, HEADS * HD), jnp.float32), -5.0, 5.0) / math.sqrt(D)
    return base.astype(jnp.bfloat16)


def gain_table(key, salt):
    return jax.random.uniform(jax.random.fold_in(key, salt), (HEADS, HD), jnp.float32, 1.4, 2.6)


def draw_q_gain(key, part):
    return gain_table(key, 11)


def draw_k_gain(key, part):
    return gain_table(key, 21)


def draw_text_len(key, part):
    lengths = jax.random.randint(jax.random.fold_in(key, 1), (REQ * 2,), TXT // 8, TXT + 1)
    chosen = jax.random.randint(jax.random.fold_in(key, 2), (), 0, REQ * 2)
    lengths = jnp.where(jnp.arange(REQ * 2) == chosen, TXT, lengths)
    return lengths.reshape(REQ, 2).astype(jnp.int32)


def offset_pair(key, salt):
    free_value = jax.random.randint(jax.random.fold_in(key, salt), (), 0, 64)
    flipped = jax.random.randint(jax.random.fold_in(key, salt + 1), (), 0, 2)
    first_req = jnp.where(flipped == 1, free_value, 63)
    second_req = jnp.where(flipped == 1, 63, free_value)
    return jnp.stack([first_req, second_req] + [free_value] * (REQ - 2)).astype(jnp.int32)


def draw_rope_ids(key, part):
    row_index = jnp.arange(SEQ_ROWS, dtype=jnp.int32)
    within = row_index % TOK_DEV
    block_id = row_index // (2 * TOK_DEV) % BLOCKS
    request_id = row_index // (2 * TOK_DEV * BLOCKS)
    position = block_id * TOK_DEV + within
    image_part = position >= TXT
    relative = jnp.maximum(position - TXT, 0)
    row_offsets = offset_pair(key, 10)
    col_offsets = offset_pair(key, 20)
    frames = jax.random.randint(jax.random.fold_in(key, 30), (REQ,), 0, 2)
    picker = (request_id[:, None] == jnp.arange(REQ, dtype=jnp.int32)[None, :]).astype(jnp.int32)
    frame_tok = jnp.sum(picker * frames[None, :], axis=1)
    row_tok = jnp.sum(picker * row_offsets[None, :], axis=1) + relative // IMG_W
    col_tok = jnp.sum(picker * col_offsets[None, :], axis=1) + relative % IMG_W
    stacked = jnp.stack([frame_tok, row_tok, col_tok], axis=0)
    return jnp.where(image_part[None, :], stacked, 0).astype(jnp.int32)


def levels(stream_key, extent, shards, smallest, high):
    def one(dim, blocks):
        draws = jax.random.uniform(jax.random.fold_in(jax.random.fold_in(stream_key, 6), dim), (blocks,), jnp.float32, smallest / len(shards), high / len(shards))
        return jnp.repeat(jnp.exp(draws), extent[dim] // blocks).reshape((-1,) + (1,) * (len(extent) - dim - 1))

    loudness = one(*shards[0])
    for cut in shards[1:]:
        loudness = loudness * one(*cut)
    return loudness


def scatter_about(stream_key, extent, scale, bound, split=(), held_as=jnp.bfloat16):
    values = scale * jax.random.normal(stream_key, extent, jnp.float32)
    if split:
        values = values * levels(stream_key, extent, split, -0.22, 0.18)
    return jnp.clip(values, -bound, bound).astype(held_as)


def setup_inputs(seed: int = 0) -> dict:
    seeds = jax.random.split(jax.random.key(seed), 15)
    state = draw_state(jax.random.fold_in(seeds[14], 71), 0)
    latent = scatter_about(seeds[1], (REQ * SEQ_LEN, CH), 1.0, 6.0, ((0, 64),), jnp.float32)
    w_mod = scatter_about(seeds[2], (D, 3 * D), D ** -0.5, 0.109375, ((0, 4), (1, 64)))
    w_qkv = draw_w_qkv(jax.random.fold_in(seeds[14], 71), 0)
    w_mlp_in = scatter_about(seeds[4], (D, FF), D ** -0.5, 0.109375, ((0, 64), (1, 4)))
    q_gain = draw_q_gain(jax.random.fold_in(seeds[14], 71), 0)
    k_gain = draw_k_gain(jax.random.fold_in(seeds[14], 71), 0)
    w_out = scatter_about(seeds[7], (HEADS * HD, D), (HEADS * HD) ** -0.5, 0.15625, ((0, 4),))
    w_mlp_down = scatter_about(seeds[8], (D, FF), FF ** -0.5, 0.078125, ((0, 64), (1, 4)))
    w_final = scatter_about(seeds[9], (D, CH), D ** -0.5, 0.109375, ((0, 4),))
    text_len = draw_text_len(jax.random.fold_in(seeds[14], 71), 0)
    rope_ids = draw_rope_ids(jax.random.fold_in(seeds[14], 71), 0)
    guidance = jax.random.randint(seeds[12], (REQ,), 2, 13).astype(jnp.int32)
    step_index = jax.random.randint(seeds[13], (REQ,), 0, STEPS).astype(jnp.int32)
    return dict(state=state, latent=latent, w_mod=w_mod, w_qkv=w_qkv, w_mlp_in=w_mlp_in, q_gain=q_gain, k_gain=k_gain, w_out=w_out, w_mlp_down=w_mlp_down, w_final=w_final, text_len=text_len, rope_ids=rope_ids, guidance=guidance, step_index=step_index)


TIME_SHIFT = 1.15
ROPE_THETA = 10000.0
NORM_EPS = 1e-06
MASKED_SCORE = -1e+30

def sigma_of(step_count):
    fraction = 1.0 - step_count.astype(jnp.float32) / STEPS
    boosted = math.exp(TIME_SHIFT) * fraction
    return boosted / (boosted + 1.0 - fraction)

def time_embedding(sigma_vals):
    half_width = D // 2
    frequency = jnp.exp(-math.log(10000.0) * jnp.arange(half_width, dtype=jnp.float32) / half_width)
    phases = 1000.0 * sigma_vals[:, None] * frequency[None, :]
    return jnp.concatenate([jnp.cos(phases), jnp.sin(phases)], axis=1)

def layer_norm(rows):
    center = lax.optimization_barrier(jnp.mean(rows, axis=-1, keepdims=True))
    spread = lax.optimization_barrier(jnp.mean(jnp.square(rows - center), axis=-1, keepdims=True))
    return (rows - center) * lax.rsqrt(spread + NORM_EPS)

def rms_norm(rows):
    return rows * lax.rsqrt(lax.optimization_barrier(jnp.mean(jnp.square(rows), axis=-1, keepdims=True)) + NORM_EPS)

def rope_angles(id_rows):
    pieces = []
    for component, width in enumerate((HD // 8, 7 * HD // 16, 7 * HD // 16)):
        index_vec = jnp.arange(width // 2, dtype=jnp.float32)
        omega = jnp.exp(-math.log(ROPE_THETA) * 2.0 * index_vec / width)
        pieces.append(id_rows[component].astype(jnp.float32)[:, None] * omega[None, :])
    return jnp.concatenate(pieces, axis=1)

def rotate(rows, angles):
    count, heads_here, size = rows.shape
    paired = rows.reshape(count, heads_here, size // 2, 2)
    cosine = jnp.cos(angles)[:, None, :]
    sine = jnp.sin(angles)[:, None, :]
    first = paired[..., 0]
    second = paired[..., 1]
    turned = jnp.stack([first * cosine - second * sine, first * sine + second * cosine], axis=-1)
    return turned.reshape(count, heads_here, size)

def reference(state, latent, w_mod, w_qkv, w_mlp_in, q_gain, k_gain, w_out, w_mlp_down, w_final, text_len, rope_ids, guidance, step_index):
    sigma_now = sigma_of(step_index)
    step_size = sigma_of(step_index + 1) - sigma_now
    time_vec = jax.nn.silu(time_embedding(sigma_now)).astype(jnp.bfloat16)
    modulation = jnp.dot(time_vec, w_mod, preferred_element_type=jnp.float32)
    grouped = state.reshape(REQ, BLOCKS, 2, TOK_DEV, D).transpose(0, 2, 1, 3, 4).reshape(REQ, 2, SEQ_LEN, D)
    id_grid = rope_ids.reshape(3, REQ, BLOCKS, 2, TOK_DEV).transpose(0, 1, 3, 2, 4).reshape(3, REQ, 2, SEQ_LEN)
    positions = jnp.arange(SEQ_LEN, dtype=jnp.int32)
    weight_flat = w_qkv.reshape(D, 3 * HEADS * HD)
    score_scale = 1.0 / math.sqrt(HD)
    latent_rows = latent.reshape(REQ, SEQ_LEN, CH)
    state_parts = []
    latent_parts = []
    square_list = []
    peak_list = []
    for request in range(REQ):
        shift_vec = modulation[request, :D]
        scale_vec = modulation[request, D:2 * D]
        gate_vec = modulation[request, 2 * D:]
        half_states = []
        half_velocity = []
        square_total = jnp.zeros((), jnp.float32)
        peak_total = jnp.full((), MASKED_SCORE, jnp.float32)
        for guided_half in range(2):
            rows = grouped[request, guided_half].astype(jnp.float32)
            modded = ((1.0 + scale_vec) * layer_norm(rows) + shift_vec).astype(jnp.bfloat16)
            projected = jnp.dot(modded, weight_flat, preferred_element_type=jnp.float32).reshape(SEQ_LEN, 3, HEADS, HD)
            mlp_pre = jnp.dot(modded, w_mlp_in, preferred_element_type=jnp.float32)
            mlp_hidden = jax.nn.gelu(mlp_pre, approximate=True).astype(jnp.bfloat16)
            angles = rope_angles(id_grid[:, request, guided_half])
            queries = rotate(rms_norm(projected[:, 0]) * q_gain[None], angles).astype(jnp.bfloat16)
            key_rows = rotate(rms_norm(projected[:, 1]) * k_gain[None], angles).astype(jnp.bfloat16)
            value_rows = projected[:, 2].astype(jnp.bfloat16)
            live = (positions >= TXT) | (positions < text_len[request, guided_half])

            def one_head(operands):
                head_queries, head_keys, head_values = operands
                scores = jnp.dot(head_queries, head_keys.T, preferred_element_type=jnp.float32) * score_scale
                scores = jnp.where(live[None, :], scores, MASKED_SCORE)
                row_max = lax.optimization_barrier(jnp.max(scores, axis=1, keepdims=True))
                weights = jnp.exp(scores - row_max)
                weights = (weights / lax.optimization_barrier(jnp.sum(weights, axis=1, keepdims=True))).astype(jnp.bfloat16)
                result = jnp.dot(weights, head_values, preferred_element_type=jnp.float32).astype(jnp.bfloat16)
                return (result, jnp.max(row_max))
            attended, head_peaks = lax.map(one_head, (queries.transpose(1, 0, 2), key_rows.transpose(1, 0, 2), value_rows.transpose(1, 0, 2)))
            attended = attended.transpose(1, 0, 2).reshape(SEQ_LEN, HEADS * HD)
            update = jnp.dot(attended, w_out, preferred_element_type=jnp.float32) + jnp.dot(mlp_hidden, w_mlp_down.T, preferred_element_type=jnp.float32)
            new_half = (rows + gate_vec * update).astype(jnp.bfloat16)
            new_values = new_half.astype(jnp.float32)
            normed_out = layer_norm(new_values).astype(jnp.bfloat16)
            half_velocity.append(jnp.dot(normed_out, w_final, preferred_element_type=jnp.float32))
            half_states.append(new_half)
            square_total = square_total + jnp.sum(new_values * new_values)
            peak_total = jnp.maximum(peak_total, jnp.max(head_peaks))
        guide_scale = guidance[request].astype(jnp.float32) / 2.0
        guided = half_velocity[1] + guide_scale * (half_velocity[0] - half_velocity[1])
        latent_parts.append(latent_rows[request] + step_size[request] * guided)
        state_parts.append(jnp.stack(half_states, axis=0))
        square_list.append(square_total)
        peak_list.append(peak_total)
    new_state = jnp.stack(state_parts, axis=0).reshape(REQ, 2, BLOCKS, TOK_DEV, D).transpose(0, 2, 1, 3, 4).reshape(SEQ_ROWS, D)
    next_latent = jnp.stack(latent_parts, axis=0).reshape(REQ * SEQ_LEN, CH)
    state_norm = jnp.sqrt(jnp.stack(square_list) / (2.0 * SEQ_LEN * D))
    top_score = jnp.stack(peak_list)
    return (new_state, next_latent, state_norm, top_score)
```

```python
import functools
import math

import jax
import jax.numpy as jnp
from jax import lax
from jax.experimental import pallas as pl
from jax.experimental.pallas import tpu as pltpu
from jax.sharding import Mesh
from jax.sharding import PartitionSpec as P


D = 3072
HD = 128
REQ = 2
TOK = 288
HALF = 144
TXT = 512
STEPS = 28
WID = 768
SEQ_LEN = 4608
TIME_SHIFT = 1.15
ROPE_THETA = 10000.0
EPS = 1e-06
MASKED = -1e30
ALL = ("xh", "xl", "z", "yl", "yh", "c")
SEQ = ("xh", "xl", "z", "yl")
XZ = ("xh", "xl", "z")
TP = ("yh", "c")
Y8 = ("yl", "yh", "c")
F32 = jnp.float32
BF16 = jnp.bfloat16
EXP2_SCALE = math.log2(math.e) / math.sqrt(HD)
SCORE_SCALE = 1.0 / math.sqrt(HD)


def flip(value, axis, bits):
    return lax.ppermute(value, axis, [(i, i ^ bits) for i in range(lax.axis_size(axis))])


def turn(value, axis, by):
    count = lax.axis_size(axis)
    return lax.ppermute(value, axis, [(i, (i + by) % count) for i in range(count)])


def sigma_of(step_count):
    fraction = 1.0 - step_count.astype(F32) / STEPS
    boosted = math.exp(TIME_SHIFT) * fraction
    return boosted / (boosted + 1.0 - fraction)


def time_embedding(sigma_vals, start, width):
    half_width = D // 2
    entry = start + jnp.arange(width, dtype=jnp.int32)
    in_cos = entry < half_width
    index = jnp.where(in_cos, entry, entry - half_width).astype(F32)
    frequency = jnp.exp(-math.log(10000.0) * index / half_width)
    phases = 1000.0 * sigma_vals[:, None] * frequency[None, :]
    return jnp.where(in_cos[None, :], jnp.cos(phases), jnp.sin(phases))


def rope_tables(id_rows):
    lane = jnp.arange(HD, dtype=jnp.int32)
    width = jnp.where(lane < 16, 16.0, 56.0).astype(F32)
    first = jnp.where(lane < 16, 0, jnp.where(lane < 72, 16, 72))
    index = ((lane - first) // 2).astype(F32)
    omega = jnp.exp(-math.log(ROPE_THETA) * 2.0 * index / width)
    ids = id_rows.astype(F32)[:, :, None]
    chosen = jnp.where(lane < 16, ids[0], jnp.where(lane < 72, ids[1], ids[2]))
    angle = chosen * omega
    sign = jnp.where(lane % 2 == 0, -1.0, 1.0)
    return jnp.cos(angle), jnp.sin(angle) * sign


def whole(shape):
    return pl.BlockSpec(shape, lambda *_: (0,) * len(shape))


SMEM = pl.BlockSpec(memory_space=pltpu.SMEM)


def cost(flops, moved, exps=0):
    return pl.CostEstimate(flops=int(flops), bytes_accessed=int(moved), transcendentals=int(exps))


def flatten_kernel(parts_ref, out_ref):
    for i in range(64):
        row = parts_ref[4 * i : 4 * i + 1, :]
        for j in range(1, 4):
            row = row + parts_ref[4 * i + j : 4 * i + j + 1, :]
        out_ref[:, 144 * i : 144 * i + 144] = row


def flattened(parts):
    return pl.pallas_call(
        flatten_kernel,
        out_shape=jax.ShapeDtypeStruct((1, 3 * D), F32),
        cost_estimate=cost(3 * D * 4, 300000),
        name="flatten_mod",
    )(parts)


def modulate_kernel(at_ref, own_ref, oc_ref, far_ref, foc_ref, mod_ref, out_ref):
    yh = at_ref[0] == 1
    core = at_ref[1] == 1
    own, oc, far, foc = (r[...].astype(F32) for r in (own_ref, oc_ref, far_ref, foc_ref))
    total = own.sum(-1, keepdims=True) + oc.sum(-1, keepdims=True)
    total = total + far.sum(-1, keepdims=True) + foc.sum(-1, keepdims=True)
    mean = total / D
    pieces = [p - mean for p in (own, oc, far, foc)]
    spread = sum(jnp.sum(p * p, -1, keepdims=True) for p in pieces) / D
    scale = lax.rsqrt(spread + EPS)
    own, oc, far, foc = (p * scale for p in pieces)
    near = (jnp.where(core, oc, own), jnp.where(core, own, oc))
    away = (jnp.where(core, foc, far), jnp.where(core, far, foc))
    for a in range(2):
        for b in range(2):
            at = (2 * a + b) * WID
            piece = jnp.where(yh, away[b], near[b]) if a == 0 else jnp.where(yh, near[b], away[b])
            gain = 1.0 + mod_ref[:, D + at : D + at + WID]
            out_ref[:, at : at + WID] = (gain * piece + mod_ref[:, at : at + WID]).astype(BF16)


def modulated(at, pieces, mod):
    rows = 96
    piece = pl.BlockSpec((rows, WID), lambda i: (i, 0))
    return pl.pallas_call(
        modulate_kernel,
        grid=(TOK // rows,),
        in_specs=[SMEM, piece, piece, piece, piece, whole((1, 3 * D))],
        out_specs=pl.BlockSpec((rows, D), lambda i: (i, 0)),
        out_shape=jax.ShapeDtypeStruct((TOK, D), BF16),
        cost_estimate=cost(TOK * D * 12, TOK * D * 4),
        name="modulate",
    )(at, *pieces, mod)


def heads_kernel(at_ref, q_ref, k_ref, v_ref, qg_ref, kg_ref, cos_ref, sin_ref, *outs):
    own_ref, give_ref, mine_ref = outs
    high = at_ref[2] == 1
    cosine, sine = cos_ref[...], sin_ref[...]
    even = lax.broadcasted_iota(jnp.int32, (TOK, HD), 1) % 2 == 0

    def turned(ref, gains, head):
        x = ref[:, head * HD : head * HD + HD]
        x = x * lax.rsqrt(jnp.mean(x * x, -1, keepdims=True) + EPS)
        x = x * gains[head : head + 1, :]
        swapped = jnp.where(even, pltpu.roll(x, HD - 1, 1), pltpu.roll(x, 1, 1))
        return x * cosine + swapped * sine

    def value(head):
        return v_ref[:, head * HD : head * HD + HD]

    def halves(low_head, high_head):
        mine = jnp.where(high, high_head, low_head).astype(BF16)
        return mine, jnp.where(high, low_head, high_head).astype(BF16)

    own_ref[1] = turned(k_ref, kg_ref, 1).astype(BF16)
    give_ref[1] = own_ref[1]
    own_ref[3] = value(1).astype(BF16)
    give_ref[3] = own_ref[3]
    own_ref[0], give_ref[0] = halves(turned(k_ref, kg_ref, 0), turned(k_ref, kg_ref, 2))
    own_ref[2], give_ref[2] = halves(value(0), value(2))
    mine_ref[0], give_ref[4] = halves(turned(q_ref, qg_ref, 0), turned(q_ref, qg_ref, 2))
    mine_ref[1] = turned(q_ref, qg_ref, 1).astype(BF16)


def heads_of(at, projected, q_gain, k_gain, cosine, sine):
    def out(n):
        return jax.ShapeDtypeStruct((n, TOK, HD), BF16)

    vmem = pl.BlockSpec(memory_space=pltpu.VMEM)
    return pl.pallas_call(
        heads_kernel,
        in_specs=[SMEM] + [vmem] * 7,
        out_shape=(out(4), out(5), out(2)),
        cost_estimate=cost(TOK * 1152 * 12, TOK * 1152 * 6),
        name="heads",
    )(at, *projected, q_gain, k_gain, cosine, sine)


def attend_kernel(first, last, chunks, *refs):
    q_ref, bias_ref = refs[:2]
    kv = refs[2 : 2 + 2 * chunks]
    keys = jnp.concatenate([kv[2 * n][...] for n in range(chunks)], axis=0)
    values = jnp.concatenate([kv[2 * n + 1][...] for n in range(chunks)], axis=0)
    rest = refs[2 + 2 * chunks :]
    if not first:
        stat_in, acc_in = rest[:2]
        rest = rest[2:]
    scores = lax.dot_general(
        q_ref[...], keys, (((1,), (1,)), ((), ())), preferred_element_type=F32
    )
    scores = scores + bias_ref[...]
    peak = jnp.max(scores, axis=1, keepdims=True)
    if not first:
        peak = jnp.maximum(peak, stat_in[:, 0:1])
    weights = jnp.exp2((scores - peak) * EXP2_SCALE)
    total = jnp.sum(weights, axis=1, keepdims=True)
    acc = jnp.dot(weights.astype(BF16), values, preferred_element_type=F32)
    if not first:
        fade = jnp.exp2((stat_in[:, 0:1] - peak) * EXP2_SCALE)
        total = total + fade * stat_in[:, 64:65]
        acc = acc + fade * acc_in[...]
    if last:
        out_ref, top_ref = rest
        out_ref[...] = (acc / total).astype(BF16)
        top_ref[...] = jnp.broadcast_to(jnp.max(peak, axis=0, keepdims=True) * SCORE_SCALE, (8, HD))
    else:
        stat_ref, acc_ref = rest
        lane = lax.broadcasted_iota(jnp.int32, (TOK, HD), 1)
        stat_ref[...] = jnp.where(lane < 64, peak, total)
        acc_ref[...] = acc


def attended_more(queries, biases, chunks, carry, last):
    count = len(chunks)
    first = carry is None
    unit = pl.BlockSpec((None, TOK, HD), lambda u: (u, 0, 0))
    key = pl.BlockSpec((None, TOK, HD), lambda u: (u // 2, 0, 0))
    val = pl.BlockSpec((None, TOK, HD), lambda u: (2 + u // 2, 0, 0))
    width = TOK * count
    specs = [unit, whole((1, width))] + [key, val] * count
    args = [queries, jnp.concatenate(biases, axis=1) if count > 1 else biases[0]]
    for chunk in chunks:
        args += [chunk, chunk]
    if not first:
        specs += [unit, unit]
        args += list(carry)
    state = jax.ShapeDtypeStruct((3, TOK, HD), F32)
    if last:
        outs = (jax.ShapeDtypeStruct((3, TOK, HD), BF16), jax.ShapeDtypeStruct((3, 8, HD), F32))
        out_specs = (unit, pl.BlockSpec((None, 8, HD), lambda u: (u, 0, 0)))
    else:
        outs, out_specs = (state, state), (unit, unit)
    return pl.pallas_call(
        functools.partial(attend_kernel, first, last, count),
        grid=(3,),
        in_specs=specs,
        out_specs=out_specs,
        out_shape=outs,
        cost_estimate=cost(3 * TOK * width * HD * 4, 4e6, 3 * TOK * width),
        name="attend",
    )(*args)


def finish_kernel(*refs):
    state_ref, gate_ref, wf_ref, top_ref = refs[:4]
    parts = refs[4:8]
    heads = refs[8:12]
    wout = refs[12:16]
    new_ref, stat_ref = refs[16:]
    update = parts[0][...].astype(F32)
    for r in parts[1:]:
        update = update + r[...].astype(F32)
    for h, w in zip(heads, wout):
        update = update + jnp.dot(h[...], w[...], preferred_element_type=F32)
    new = (state_ref[...].astype(F32) + gate_ref[...] * update).astype(BF16)
    new_ref[...] = new
    wide = new.astype(F32)
    squares = jnp.sum(wide * wide, axis=1, keepdims=True)
    lane = lax.broadcasted_iota(jnp.int32, (TOK, HD), 1)
    stats = jnp.dot(new, wf_ref[...], preferred_element_type=F32)
    stats = jnp.where(lane == 65, squares, stats)
    total = jnp.sum(squares, axis=0, keepdims=True)
    ones = jnp.ones((16, WID), BF16)
    extra = jnp.dot(ones, wf_ref[...], preferred_element_type=F32)[:8]
    lane8 = lax.broadcasted_iota(jnp.int32, (8, HD), 1)
    top = jnp.max(top_ref[...], axis=0)
    extra = jnp.where(lane8 == 66, total, jnp.where(lane8 == 67, top, extra))
    for h in range(8):
        half = h // 4
        stat_ref[h, :HALF, :] = stats[half * HALF : (half + 1) * HALF]
        stat_ref[h, HALF:, :] = extra


def finished(state, gate, wf, top, parts, heads, wout):
    return pl.pallas_call(
        finish_kernel,
        out_shape=(
            jax.ShapeDtypeStruct((TOK, WID), BF16),
            jax.ShapeDtypeStruct((8, HALF + 8, HD), F32),
        ),
        cost_estimate=cost(2 * TOK * 1536 * WID, 6e6),
        name="finish",
    )(state, gate, wf, top, *parts, *heads, *wout)


def sums_kernel(got_ref, sums_ref):
    total, top = got_ref[0, HALF : HALF + 1, :], got_ref[0, HALF : HALF + 1, :]
    for i in range(1, 8):
        total = total + got_ref[i, HALF : HALF + 1, :]
        top = jnp.maximum(top, got_ref[i, HALF : HALF + 1, :])
    lane = lax.broadcasted_iota(jnp.int32, (1, HD), 1)
    row = jnp.where(lane == 67, top, total)
    for i in range(32):
        sums_ref[i] = row


def latent_kernel(guide_ref, got_ref, latent_ref, next_ref):
    def velocity(h):
        total = got_ref[4 * h] + got_ref[4 * h + 1] + got_ref[4 * h + 2] + got_ref[4 * h + 3]
        mean = total[:HALF, 64:65] / D
        spread = total[:HALF, 65:66] / D - mean * mean
        product = total[:HALF, :64] - mean * total[HALF : HALF + 1, :64]
        return product * lax.rsqrt(spread + EPS)

    cond, uncond = velocity(0), velocity(1)
    step, scale = guide_ref[0], guide_ref[1]
    next_ref[...] = latent_ref[...] + step * (uncond + scale * (cond - uncond))


def block_sums(got):
    return pl.pallas_call(
        sums_kernel,
        in_specs=[pl.BlockSpec((8, HALF + 8, HD), lambda *_: (0, 0, 0))],
        out_shape=jax.ShapeDtypeStruct((32, 1, HD), F32),
        cost_estimate=cost(1e4, 7e5),
        name="block_sums",
    )(got)


def next_latents(guide, got, latent):
    return pl.pallas_call(
        latent_kernel,
        in_specs=[SMEM, whole(got.shape), whole(latent.shape)],
        out_specs=whole(latent.shape),
        out_shape=jax.ShapeDtypeStruct(latent.shape, F32),
        cost_estimate=cost(4e5, 7e5),
        name="next_latent",
    )(guide, got, latent)


def body(
    state,
    latent,
    w_mod,
    w_qkv,
    w_mlp_in,
    q_gain,
    k_gain,
    w_out,
    w_mlp_down,
    w_final,
    text_len,
    rope_ids,
    guidance,
    step_index,
):
    xh, xl, z, yl, yh, core = (lax.axis_index(a) for a in ALL)
    tp = 2 * yh + core
    at = jnp.stack([yh, core, xl]).astype(jnp.int32)

    both = jnp.stack([w_mlp_in, w_mlp_down])
    keep = lax.dynamic_slice_in_dim(both, yl * WID, WID, 2)
    give = lax.dynamic_slice_in_dim(both, (1 - yl) * WID, WID, 2)
    taken = flip(give, "yl", 1)
    low = jnp.where(yl == 0, keep, taken)
    high = jnp.where(yl == 0, taken, keep)
    rows96 = jnp.concatenate([low, high], axis=1)
    rows96 = jnp.concatenate([rows96[0], rows96[1]], axis=1)
    weights = lax.all_gather(rows96, XZ, axis=0, tiled=True)
    w_in, w_down = weights[:, :WID], weights[:, WID:]

    s_oc = flip(state, "c", 1)
    s_far = flip(state, "yh", 1)
    s_foc = flip(s_far, "c", 1)
    t_own = flip(state, "yl", 1)
    t_far = flip(state, ("yl", "yh"), 3)
    t_pair = flip(jnp.stack([t_own, t_far]), "c", 1)

    sigma_now = sigma_of(step_index)
    step_size = sigma_of(step_index + 1) - sigma_now
    time_rows = jax.nn.silu(time_embedding(sigma_now, tp * WID, WID)).astype(BF16)
    partial_mod = jnp.dot(time_rows, w_mod, preferred_element_type=F32)
    sent = jnp.repeat(partial_mod, 128, axis=0)[:, None, :]
    got = lax.all_to_all(sent, ALL, 0, 0, tiled=True)
    mod = flattened(got.reshape(256, 144))
    gate = lax.dynamic_slice_in_dim(mod, 2 * D + tp * WID, WID, 1)

    modded = modulated(at, (state, s_oc, s_far, s_foc), mod)

    cosine, sine = rope_tables(rope_ids)
    w_kinds = w_qkv.transpose(1, 0, 2)
    projected = [jnp.dot(modded, w_kinds[k], preferred_element_type=F32) for k in range(3)]
    own_kv, give_kv, own_q = heads_of(at, projected, q_gain, k_gain, cosine, sine)
    taken_kv = flip(give_kv, "xl", 1)
    queries = jnp.concatenate([own_q[:1], taken_kv[4:], own_q[1:]], axis=0)
    taken_kv = taken_kv[:4]

    flat_len = text_len.reshape(2 * REQ)
    own_len = jnp.sum(
        jnp.where(jnp.arange(2 * REQ, dtype=jnp.int32) == xh * 2 + yl, flat_len, 0)
    )

    def bias_of(made_at, taken):
        token = jnp.arange(TOK, dtype=jnp.int32)
        side = 1 - xl if taken else xl
        positions = (side * 8 + made_at) * TOK + token
        live = (positions >= TXT) | (positions < own_len)
        return jnp.where(live, 0.0, MASKED).astype(F32)[None, :]

    def pair_bias(made_at):
        return [bias_of(made_at, False), bias_of(made_at, True)]

    carry = attended_more(queries, pair_bias(z), [own_kv, taken_kv], None, False)
    ups, dns = [own_kv, taken_kv], [own_kv, taken_kv]
    for k in range(1, 4):
        for ring in range(2):
            ups[ring] = turn(ups[ring], "z", 1)
            dns[ring] = turn(dns[ring], "z", -1)
        biases = pair_bias((z + 8 - k) % 8) + pair_bias((z + k) % 8)
        carry = attended_more(queries, biases, ups + dns, carry, False)
    final = []
    for ring in range(2):
        low = turn(ups[ring][:2], "z", 1)
        high = turn(dns[ring][2:], "z", -1)
        final.append(jnp.concatenate([low, high], axis=0))
    out, top = attended_more(queries, pair_bias((z + 4) % 8), final, carry, True)

    others = modulated(at, (t_own, t_pair[0], t_far, t_pair[1]), mod)
    both_rows = jnp.concatenate([modded, others], axis=0)
    mlp_pre = jnp.dot(both_rows, w_in, preferred_element_type=F32)
    hidden = jax.nn.gelu(mlp_pre, approximate=True).astype(BF16)

    def features_of(r):
        rows = lax.dynamic_slice_in_dim(w_down, (tp ^ r) * WID, WID, 0)
        return lax.dot_general(
            hidden, rows, (((1,), (1,)), ((), ())), preferred_element_type=F32
        )

    mine = [features_of(0), features_of(2)]
    theirs = jnp.stack([features_of(1).astype(BF16), features_of(3).astype(BF16)])
    crossed = flip(theirs, "c", 1).astype(F32)
    summed = [(mine[i] + crossed[i]).astype(BF16) for i in range(2)]
    part_own = summed[0][:TOK]
    part_yl = flip(summed[0][TOK:], "yl", 1)
    part_far = flip(summed[1][:TOK], "yh", 1)
    part_both = flip(summed[1][TOK:], ("yl", "yh"), 3)

    def wout_for(r):
        return lax.dynamic_slice_in_dim(w_out, (tp ^ r) * WID, WID, 1)

    wout = [
        wout_for(0),
        flip(wout_for(1), "c", 1),
        flip(wout_for(2), "yh", 1),
        flip(wout_for(3), ("yh", "c"), 3),
    ]
    returned = flip(out[1], "xl", 1)
    low_head = jnp.where(xl == 0, out[0], returned)
    high_head = jnp.where(xl == 0, returned, out[0])
    heads = jnp.concatenate([low_head, out[2], high_head], axis=1)
    h_oc = flip(heads, "c", 1)
    h_far = flip(heads, "yh", 1)
    h_foc = flip(h_far, "c", 1)

    wf = jnp.concatenate(
        [w_final, jnp.ones((WID, 1), BF16), jnp.zeros((WID, HD - 65), BF16)], axis=1
    )
    new_state, stats = finished(
        state,
        gate,
        wf,
        top,
        (part_own, part_yl, part_far, part_both),
        (heads, h_oc, h_far, h_foc),
        wout,
    )

    got_rows = lax.all_to_all(stats, Y8, 0, 0, tiled=True)
    request_pick = jnp.arange(REQ, dtype=jnp.int32) == xh
    guide_scale = jnp.sum(jnp.where(request_pick, guidance, 0)).astype(F32) / 2.0
    own_step = jnp.sum(jnp.where(request_pick, step_size, 0.0))
    guide = jnp.stack([own_step, guide_scale])
    every = lax.all_to_all(block_sums(got_rows), XZ, 0, 0, tiled=True)
    next_latent = next_latents(guide, got_rows, latent)
    every = every.reshape(2, 16, HD)
    state_norm = jnp.sqrt(jnp.sum(every[:, :, 66], axis=1) / (2.0 * SEQ_LEN * D))
    top_score = jnp.max(every[:, :, 67], axis=1)
    return (new_state, next_latent, state_norm, top_score)


def solution(mesh):
    split = Mesh(mesh.devices.reshape(2, 2, 8, 2, 2, 2), ALL)
    return jax.shard_map(
        body,
        mesh=split,
        in_specs=(
            P(SEQ, TP),
            P(SEQ, None),
            P(TP, SEQ),
            P(None, None, TP),
            P(SEQ, TP),
            P(TP, None),
            P(TP, None),
            P(TP, None),
            P(SEQ, TP),
            P(TP, None),
            P(),
            P(None, SEQ),
            P(),
            P(),
        ),
        out_specs=(P(SEQ, TP), P(SEQ, None), P(), P()),
        check_vma=False,
    )
```

```python
import functools
import math

import jax
import jax.numpy as jnp
from jax import lax
from jax.experimental import pallas as pl
from jax.experimental.pallas import tpu as pltpu
from jax.sharding import Mesh
from jax.sharding import PartitionSpec as P


D = 3072
HD = 128
REQ = 2
TOK = 288
HALF = 144
TXT = 512
STEPS = 28
WID = 768
SEQ_LEN = 4608
TIME_SHIFT = 1.15
ROPE_THETA = 10000.0
EPS = 1e-06
MASKED = -1e30
ALL = ("xh", "xl", "z", "yl", "yh", "c")
SEQ = ("xh", "xl", "z", "yl")
XZ = ("xh", "xl", "z")
TP = ("yh", "c")
Y8 = ("yl", "yh", "c")
F32 = jnp.float32
BF16 = jnp.bfloat16
EXP2_SCALE = math.log2(math.e) / math.sqrt(HD)
SCORE_SCALE = 1.0 / math.sqrt(HD)


def flip(value, axis, bits):
    return lax.ppermute(value, axis, [(i, i ^ bits) for i in range(lax.axis_size(axis))])


def turn(value, axis, by):
    count = lax.axis_size(axis)
    return lax.ppermute(value, axis, [(i, (i + by) % count) for i in range(count)])


def sigma_of(step_count):
    fraction = 1.0 - step_count.astype(F32) / STEPS
    boosted = math.exp(TIME_SHIFT) * fraction
    return boosted / (boosted + 1.0 - fraction)


def time_embedding(sigma_vals, start, width):
    half_width = D // 2
    entry = start + jnp.arange(width, dtype=jnp.int32)
    in_cos = entry < half_width
    index = jnp.where(in_cos, entry, entry - half_width).astype(F32)
    frequency = jnp.exp(-math.log(10000.0) * index / half_width)
    phases = 1000.0 * sigma_vals[:, None] * frequency[None, :]
    return jnp.where(in_cos[None, :], jnp.cos(phases), jnp.sin(phases))


def rope_tables(id_rows):
    lane = jnp.arange(HD, dtype=jnp.int32)
    width = jnp.where(lane < 16, 16.0, 56.0).astype(F32)
    first = jnp.where(lane < 16, 0, jnp.where(lane < 72, 16, 72))
    index = ((lane - first) // 2).astype(F32)
    omega = jnp.exp(-math.log(ROPE_THETA) * 2.0 * index / width)
    ids = id_rows.astype(F32)[:, :, None]
    chosen = jnp.where(lane < 16, ids[0], jnp.where(lane < 72, ids[1], ids[2]))
    angle = chosen * omega
    sign = jnp.where(lane % 2 == 0, -1.0, 1.0)
    return jnp.cos(angle), jnp.sin(angle) * sign


def whole(shape):
    return pl.BlockSpec(shape, lambda *_: (0,) * len(shape))


SMEM = pl.BlockSpec(memory_space=pltpu.SMEM)


def cost(flops, moved, exps=0):
    return pl.CostEstimate(flops=int(flops), bytes_accessed=int(moved), transcendentals=int(exps))


def flatten_kernel(parts_ref, out_ref):
    for i in range(64):
        row = parts_ref[4 * i : 4 * i + 1, :]
        for j in range(1, 4):
            row = row + parts_ref[4 * i + j : 4 * i + j + 1, :]
        out_ref[:, 144 * i : 144 * i + 144] = row


def flattened(parts):
    return pl.pallas_call(
        flatten_kernel,
        out_shape=jax.ShapeDtypeStruct((1, 3 * D), F32),
        cost_estimate=cost(3 * D * 4, 300000),
        name="flatten_mod",
    )(parts)


def modulate_rows(at_ref, pieces, mod_ref, out_ref, begin, rows):
    here = pl.ds(begin, rows)
    values = [r[here, :].astype(F32) for r in pieces]
    mean = sum(jnp.sum(v, -1, keepdims=True) for v in values) / D
    values = [v - mean for v in values]
    spread = sum(jnp.sum(v * v, -1, keepdims=True) for v in values) / D
    scale = lax.rsqrt(spread + EPS)
    for r, v in enumerate(values):
        lanes = pl.ds(pl.multiple_of(at_ref[3 + r], WID), WID)
        gains = pl.ds(pl.multiple_of(at_ref[3 + r] + D, WID), WID)
        out_ref[here, lanes] = (
            (1.0 + mod_ref[:, gains]) * (v * scale) + mod_ref[:, lanes]
        ).astype(BF16)


def modulate_kernel(at_ref, own_ref, oc_ref, far_ref, foc_ref, mod_ref, out_ref):
    pieces = (own_ref, oc_ref, far_ref, foc_ref)

    @pl.loop(0, 6)
    def _(i):
        modulate_rows(at_ref, pieces, mod_ref, out_ref, pl.multiple_of(i * 48, 48), 48)


VMEM = pl.BlockSpec(memory_space=pltpu.VMEM)


def modulated(at, pieces, mod):
    return pl.pallas_call(
        modulate_kernel,
        in_specs=[SMEM] + [VMEM] * 5,
        out_shape=jax.ShapeDtypeStruct((TOK, D), BF16),
        cost_estimate=cost(TOK * D * 12, TOK * D * 4),
        name="modulate",
    )(at, *pieces, mod)


def project_kernel(
    at_ref, own_ref, oc_ref, far_ref, foc_ref, mod_ref, w_ref, gain_ref, cos_ref, sin_ref,
    modded_ref, keep_ref, give_ref, mine_ref, lent_ref,
):
    kind = pl.program_id(0)

    @pl.when(kind == 0)
    def _():
        modulate_kernel(at_ref, own_ref, oc_ref, far_ref, foc_ref, mod_ref, modded_ref)

    high = at_ref[2] == 1
    even = lax.broadcasted_iota(jnp.int32, (TOK, HD), 1) % 2 == 0
    heads = jnp.dot(modded_ref[...], w_ref[...], preferred_element_type=F32)
    heads = [heads[:, h * HD : h * HD + HD] for h in range(3)]

    def turned():
        out = []
        for h, x in enumerate(heads):
            x = x * lax.rsqrt(jnp.mean(x * x, -1, keepdims=True) + EPS)
            x = x * gain_ref[h : h + 1, :]
            swapped = jnp.where(even, pltpu.roll(x, HD - 1, 1), pltpu.roll(x, 1, 1))
            out.append((x * cos_ref[...] + swapped * sin_ref[...]).astype(BF16))
        return out

    def dealt(three):
        mine = jnp.where(high, three[2].astype(F32), three[0].astype(F32)).astype(BF16)
        other = jnp.where(high, three[0].astype(F32), three[2].astype(F32)).astype(BF16)
        return mine, three[1], other

    @pl.when(kind == 0)
    def _():
        mine_ref[0], mine_ref[1], lent_ref[...] = dealt(turned())

    @pl.when(kind == 1)
    def _():
        keep_ref[0], shared, give_ref[0] = dealt(turned())
        keep_ref[1] = shared
        give_ref[1] = shared

    @pl.when(kind == 2)
    def _():
        keep_ref[2], shared, give_ref[2] = dealt([h.astype(BF16) for h in heads])
        keep_ref[3] = shared
        give_ref[3] = shared


def projected(at, pieces, mod, w_kinds, gains, cosine, sine):
    def out(n):
        return jax.ShapeDtypeStruct((n, TOK, HD), BF16)

    return pl.pallas_call(
        project_kernel,
        grid=(3,),
        in_specs=[SMEM]
        + [VMEM] * 5
        + [
            pl.BlockSpec((None, D, 3 * HD), lambda k: (k, 0, 0)),
            pl.BlockSpec((None, 3, HD), lambda k: (jnp.minimum(k, 1), 0, 0)),
            VMEM,
            VMEM,
        ],
        out_specs=(
            whole((TOK, D)),
            whole((4, TOK, HD)),
            whole((4, TOK, HD)),
            whole((2, TOK, HD)),
            whole((TOK, HD)),
        ),
        out_shape=(
            jax.ShapeDtypeStruct((TOK, D), BF16),
            out(4),
            out(4),
            out(2),
            jax.ShapeDtypeStruct((TOK, HD), BF16),
        ),
        cost_estimate=cost(2 * TOK * D * 9 * HD, 11e6),
        name="project",
    )(at, *pieces, mod, w_kinds, gains, cosine, sine)


def assemble_kernel(at_ref, *refs):
    out_ref = refs[-1]
    z = at_ref[7]
    for k in range(7):
        spot = lax.rem(z + (0, 7, 1, 6, 2, 5, 3)[k], 8) * 96
        out_ref[pl.ds(pl.multiple_of(spot, 32), 96), :] = refs[k][...]
    spot = lax.rem(z + 4, 8) * 96
    out_ref[pl.ds(pl.multiple_of(spot, 32), 48), :] = refs[7][...]
    out_ref[pl.ds(pl.multiple_of(spot + 48, 16), 48), :] = refs[8][...]


def assembled(at, parts):
    return pl.pallas_call(
        assemble_kernel,
        in_specs=[SMEM] + [VMEM] * 9,
        out_shape=jax.ShapeDtypeStruct((WID, 2 * WID), BF16),
        cost_estimate=cost(1e5, 5e6),
        name="assemble",
    )(at, *parts)


def hidden_part(at_ref, rows_ref, j, w_ref):
    x = lax.rem(at_ref[8] + j, 4)
    lanes = pl.ds(pl.multiple_of(x * WID, WID), WID)
    return jnp.dot(rows_ref[:, lanes], w_ref[...], preferred_element_type=F32)


def early_kernel(at_ref, mine_ref, other_ref, w0_ref, w1_ref, w3_ref, out_ref):
    for half, rows_ref in enumerate((mine_ref, other_ref)):
        total = hidden_part(at_ref, rows_ref, 0, w0_ref)
        total = total + hidden_part(at_ref, rows_ref, 1, w1_ref)
        out_ref[half] = total + hidden_part(at_ref, rows_ref, 3, w3_ref)


def late_kernel(
    at_ref, pre_ref, mine_ref, other_ref, wl_ref, wh_ref, d0_ref, d1_ref, dl_ref, dh_ref, d3_ref,
    out_ref,
):
    def block(j):
        return at_ref[3 + 6 + j]

    far = lax.rem(at_ref[8] + 2, 4) * WID
    for half, rows_ref in enumerate((mine_ref, other_ref)):
        total = pre_ref[half]
        for n, w_ref in enumerate((wl_ref, wh_ref)):
            lanes = pl.ds(pl.multiple_of(far + n * (WID // 2), WID // 2), WID // 2)
            total = total + jnp.dot(rows_ref[:, lanes], w_ref[...], preferred_element_type=F32)
        cubic = total + 0.044715 * (total * total * total)
        hidden = total * (0.5 + 0.5 * jnp.tanh(math.sqrt(2.0 / math.pi) * cubic))
        hidden = hidden.astype(BF16)

        def down(w):
            return lax.dot_general(
                hidden, w[...], (((1,), (1,)), ((), ())), preferred_element_type=F32
            ).astype(BF16)

        for j, w_ref in ((0, d0_ref), (1, d1_ref), (3, d3_ref)):
            out_ref[block(j), half] = down(w_ref)
        out_ref[block(2), half, :, : WID // 2] = down(dl_ref)
        out_ref[block(2), half, :, WID // 2 :] = down(dh_ref)


def mlp(at, mine, other, w0, w1, w2, w3):
    def left(rows=WID):
        return pl.BlockSpec((rows, WID), lambda i: (0, 0))

    def right(rows=WID):
        return pl.BlockSpec((rows, WID), lambda i: (0, 1))

    half = WID // 2
    pre = pl.pallas_call(
        early_kernel,
        grid=(1,),
        in_specs=[SMEM, VMEM, VMEM, left(), left(), left()],
        out_specs=whole((2, TOK, WID)),
        out_shape=jax.ShapeDtypeStruct((2, TOK, WID), F32),
        cost_estimate=cost(6 * 2 * TOK * WID * WID, 9e6),
        name="mlp_early",
    )(at, mine, other, w0, w1, w3)
    return pl.pallas_call(
        late_kernel,
        grid=(1,),
        in_specs=[SMEM, VMEM, VMEM, VMEM, left(half), left(half)]
        + [right(), right(), right(half), right(half), right()],
        out_specs=whole((4, 2, TOK, WID)),
        out_shape=jax.ShapeDtypeStruct((4, 2, TOK, WID), BF16),
        cost_estimate=cost(10 * 2 * TOK * WID * WID, 16e6),
        name="mlp_late",
    )(at, pre, mine, other, *w2, w0, w1, *w2, w3)


def attend_kernel(first, last, makers, *refs):
    count = len(makers)
    at_ref, own_ref, taken_ref = refs[:3]
    kv = refs[3 : 3 + 2 * count]
    rest = refs[3 + 2 * count :]
    if not first:
        stat_in, acc_in = rest[:2]
        rest = rest[2:]
    taken = jnp.full((TOK, HD), pl.program_id(0), jnp.int32) == 1
    queries = jnp.where(taken, taken_ref[...].astype(F32), own_ref[...].astype(F32)).astype(BF16)
    keys = jnp.concatenate([r[...] for r in kv[:count]], axis=0)
    values = jnp.concatenate([r[...] for r in kv[count:]], axis=0)
    token = lax.broadcasted_iota(jnp.int32, (1, count * TOK), 1)
    place = jnp.zeros((1, count * TOK), jnp.int32)
    for n, (by, side) in enumerate(makers):
        row = at_ref[2] if side == 0 else 1 - at_ref[2]
        start = (row * 8 + lax.rem(at_ref[7] + by, 8) - n) * TOK
        place = jnp.where(token >= n * TOK, token + start, place)
    live = (place >= TXT) | (place < at_ref[13])
    bias = jnp.where(live, 0.0, MASKED).astype(F32)
    scores = lax.dot_general(
        queries, keys, (((1,), (1,)), ((), ())), preferred_element_type=F32
    )
    scores = scores + bias
    peak = jnp.max(scores, axis=1, keepdims=True)
    if not first:
        peak = jnp.maximum(peak, stat_in[:, 0:1])
    weights = jnp.exp2((scores - peak) * EXP2_SCALE)
    total = jnp.sum(weights, axis=1, keepdims=True)
    acc = jnp.dot(weights.astype(BF16), values, preferred_element_type=F32)
    if not first:
        fade = jnp.exp2((stat_in[:, 0:1] - peak) * EXP2_SCALE)
        total = total + fade * stat_in[:, 64:65]
        acc = acc + fade * acc_in[...]
    if last:
        out_ref, top_ref = rest
        out_ref[...] = (acc / total).astype(BF16)
        top_ref[...] = jnp.broadcast_to(jnp.max(peak, axis=0, keepdims=True) * SCORE_SCALE, (8, HD))
    else:
        stat_ref, acc_ref = rest
        lane = lax.broadcasted_iota(jnp.int32, (TOK, HD), 1)
        stat_ref[...] = jnp.where(lane < 64, peak, total)
        acc_ref[...] = acc


def attended_more(at, own_q, taken_q, makers, keys, values, carry, last):
    count = len(makers)
    first = carry is None
    unit = pl.BlockSpec((None, TOK, HD), lambda u: (u, 0, 0))
    shared = pl.BlockSpec((None, TOK, HD), lambda u: (u // 2, 0, 0))
    later = pl.BlockSpec((None, TOK, HD), lambda u: (2 + u // 2, 0, 0))
    specs = [SMEM, shared, whole((TOK, HD))] + [shared] * count
    specs += [later if v.shape[0] == 4 else shared for v in values]
    args = [at, own_q, taken_q, *keys, *values]
    if not first:
        specs += [unit, unit]
        args += list(carry)
    state = jax.ShapeDtypeStruct((3, TOK, HD), F32)
    if last:
        outs = (jax.ShapeDtypeStruct((3, TOK, HD), BF16), jax.ShapeDtypeStruct((3, 8, HD), F32))
        out_specs = (unit, pl.BlockSpec((None, 8, HD), lambda u: (u, 0, 0)))
    else:
        outs, out_specs = (state, state), (unit, unit)
    width = count * TOK
    return pl.pallas_call(
        functools.partial(attend_kernel, first, last, makers),
        grid=(3,),
        in_specs=specs,
        out_specs=out_specs,
        out_shape=outs,
        cost_estimate=cost(3 * TOK * width * HD * 4, 4e6, 3 * TOK * width),
        name="attend",
    )(*args)


def finish_kernel(*refs):
    state_ref, gate_ref, wf_ref, top_ref = refs[:4]
    parts = refs[4:8]
    heads = refs[8:12]
    wout = refs[12:16]
    new_ref, stat_ref = refs[16:]
    update = parts[0][...].astype(F32)
    for r in parts[1:]:
        update = update + r[...].astype(F32)
    for h, w in zip(heads, wout):
        update = update + jnp.dot(h[...], w[...], preferred_element_type=F32)
    new = (state_ref[...].astype(F32) + gate_ref[...] * update).astype(BF16)
    new_ref[...] = new
    wide = new.astype(F32)
    squares = jnp.sum(wide * wide, axis=1, keepdims=True)
    lane = lax.broadcasted_iota(jnp.int32, (TOK, HD), 1)
    stats = jnp.dot(new, wf_ref[...], preferred_element_type=F32)
    stats = jnp.where(lane == 65, squares, stats)
    total = jnp.sum(squares, axis=0, keepdims=True)
    ones = jnp.ones((16, WID), BF16)
    extra = jnp.dot(ones, wf_ref[...], preferred_element_type=F32)[:8]
    lane8 = lax.broadcasted_iota(jnp.int32, (8, HD), 1)
    top = jnp.max(top_ref[...], axis=0)
    extra = jnp.where(lane8 == 66, total, jnp.where(lane8 == 67, top, extra))
    for h in range(8):
        half = h // 4
        stat_ref[h, :HALF, :] = stats[half * HALF : (half + 1) * HALF]
        stat_ref[h, HALF:, :] = extra


def finished(state, gate, wf, top, parts, heads, wout):
    return pl.pallas_call(
        finish_kernel,
        out_shape=(
            jax.ShapeDtypeStruct((TOK, WID), BF16),
            jax.ShapeDtypeStruct((8, HALF + 8, HD), F32),
        ),
        cost_estimate=cost(2 * TOK * 1536 * WID, 6e6),
        name="finish",
    )(state, gate, wf, top, *parts, *heads, *wout)


def sums_kernel(got_ref, sums_ref):
    total, top = got_ref[0, HALF : HALF + 1, :], got_ref[0, HALF : HALF + 1, :]
    for i in range(1, 8):
        total = total + got_ref[i, HALF : HALF + 1, :]
        top = jnp.maximum(top, got_ref[i, HALF : HALF + 1, :])
    lane = lax.broadcasted_iota(jnp.int32, (1, HD), 1)
    row = jnp.where(lane == 67, top, total)
    for i in range(32):
        sums_ref[i] = row


def latent_kernel(guide_ref, got_ref, latent_ref, next_ref):
    def velocity(h):
        total = got_ref[4 * h] + got_ref[4 * h + 1] + got_ref[4 * h + 2] + got_ref[4 * h + 3]
        mean = total[:HALF, 64:65] / D
        spread = total[:HALF, 65:66] / D - mean * mean
        product = total[:HALF, :64] - mean * total[HALF : HALF + 1, :64]
        return product * lax.rsqrt(spread + EPS)

    cond, uncond = velocity(0), velocity(1)
    step, scale = guide_ref[0], guide_ref[1]
    next_ref[...] = latent_ref[...] + step * (uncond + scale * (cond - uncond))


def block_sums(got):
    return pl.pallas_call(
        sums_kernel,
        in_specs=[pl.BlockSpec((8, HALF + 8, HD), lambda *_: (0, 0, 0))],
        out_shape=jax.ShapeDtypeStruct((32, 1, HD), F32),
        cost_estimate=cost(1e4, 7e5),
        name="block_sums",
    )(got)


def next_latents(guide, got, latent):
    return pl.pallas_call(
        latent_kernel,
        in_specs=[SMEM, whole(got.shape), whole(latent.shape)],
        out_specs=whole(latent.shape),
        out_shape=jax.ShapeDtypeStruct(latent.shape, F32),
        cost_estimate=cost(4e5, 7e5),
        name="next_latent",
    )(guide, got, latent)


def body(
    state,
    latent,
    w_mod,
    w_qkv,
    w_mlp_in,
    q_gain,
    k_gain,
    w_out,
    w_mlp_down,
    w_final,
    text_len,
    rope_ids,
    guidance,
    step_index,
):
    xh, xl, z, yl, yh, core = (lax.axis_index(a) for a in ALL)
    tp = 2 * yh + core
    x = 2 * xh + xl
    blocks = [(tp ^ r) * WID for r in range(4)]
    owners = [((x + j) % 4) ^ tp for j in range(4)]
    flat_len = text_len.reshape(2 * REQ)
    own_len = jnp.sum(
        jnp.where(jnp.arange(2 * REQ, dtype=jnp.int32) == xh * 2 + yl, flat_len, 0)
    )
    at = jnp.stack([yh, core, xl, *blocks, z, x, *owners, own_len]).astype(jnp.int32)

    both = jnp.stack([w_mlp_in, w_mlp_down])
    keep = lax.dynamic_slice_in_dim(both, yl * WID, WID, 2)
    give = lax.dynamic_slice_in_dim(both, (1 - yl) * WID, WID, 2)
    taken = flip(give, "yl", 1)
    low = jnp.where(yl == 0, keep, taken)
    high = jnp.where(yl == 0, taken, keep)
    rows96 = jnp.concatenate([low, high], axis=1)
    rows96 = jnp.concatenate([rows96[0], rows96[1]], axis=1)
    w_up1 = turn(rows96, "z", 1)
    w_dn1 = turn(rows96, "z", -1)
    w_up2 = turn(rows96, "z", 2)
    w_dn2 = turn(rows96, "z", -2)
    w_up3 = turn(w_up2, "z", 1)
    w_dn3 = turn(w_dn2, "z", -1)
    w_up4 = turn(w_up2[:48], "z", 2)
    w_dn4 = turn(w_dn2[48:], "z", -2)
    w_parts = [rows96, w_up1, w_dn1, w_up2, w_dn2, w_up3, w_dn3, w_up4, w_dn4]
    w_here = assembled(at, w_parts)
    w_before = turn(w_here, ("xh", "xl"), 1)
    w_after = turn(w_here, ("xh", "xl"), -1)
    w_far_low = turn(w_before[: WID // 2], ("xh", "xl"), 1)
    w_far_high = turn(w_after[WID // 2 :], ("xh", "xl"), -1)

    s_oc = flip(state, "c", 1)
    s_far = flip(state, "yh", 1)
    s_foc = flip(s_far, "c", 1)
    t_own = flip(state, "yl", 1)
    t_far = flip(state, ("yl", "yh"), 3)
    t_pair = flip(jnp.stack([t_own, t_far]), "c", 1)

    sigma_now = sigma_of(step_index)
    step_size = sigma_of(step_index + 1) - sigma_now
    time_rows = jax.nn.silu(time_embedding(sigma_now, tp * WID, WID)).astype(BF16)
    partial_mod = jnp.dot(time_rows, w_mod, preferred_element_type=F32)
    sent = jnp.repeat(partial_mod, 128, axis=0)[:, None, :]
    got = lax.all_to_all(sent, ALL, 0, 0, tiled=True)
    mod = flattened(got.reshape(256, 144))
    gate = lax.dynamic_slice_in_dim(mod, 2 * D + tp * WID, WID, 1)

    cosine, sine = rope_tables(rope_ids)
    w_kinds = w_qkv.transpose(1, 0, 2)
    gains = jnp.stack([q_gain, k_gain])
    modded, own_kv, give_kv, own_q, give_q = projected(
        at, (state, s_oc, s_far, s_foc), mod, w_kinds, gains, cosine, sine
    )
    taken_kv = flip(give_kv, "xl", 1)
    taken_q = flip(give_q, "xl", 1)

    ups, dns = [own_kv, taken_kv], [own_kv, taken_kv]
    makers = ((0, 0), (0, 1))
    carry = attended_more(at, own_q, taken_q, makers, ups, ups, None, False)
    for k in range(1, 4):
        for ring in range(2):
            ups[ring] = turn(ups[ring], "z", 1)
            dns[ring] = turn(dns[ring], "z", -1)
        makers = ((8 - k, 0), (8 - k, 1), (k, 0), (k, 1))
        blocks4 = ups + dns
        carry = attended_more(at, own_q, taken_q, makers, blocks4, blocks4, carry, False)
    lows, highs = [], []
    for ring in range(2):
        lows.append(turn(ups[ring][:2], "z", 1))
        highs.append(turn(dns[ring][2:], "z", -1))
    makers = ((4, 0), (4, 1))
    out, top = attended_more(at, own_q, taken_q, makers, lows, highs, carry, True)

    others = modulated(at, (t_own, t_pair[0], t_far, t_pair[1]), mod)
    products = mlp(at, modded, others, w_here, w_after, (w_far_low, w_far_high), w_before)
    crossed = flip(jnp.stack([products[1], products[3]]), "c", 1)
    summed = [
        (products[2 * i].astype(F32) + crossed[i].astype(F32)).astype(BF16) for i in range(2)
    ]
    part_own = summed[0][0]
    part_yl = flip(summed[0][1], "yl", 1)
    part_far = flip(summed[1][0], "yh", 1)
    part_both = flip(summed[1][1], ("yl", "yh"), 3)

    def wout_for(r):
        return lax.dynamic_slice_in_dim(w_out, (tp ^ r) * WID, WID, 1)

    wout = [wout_for(0)]
    wout.append(flip(wout_for(1), "c", 1))
    wout.append(flip(wout_for(2), "yh", 1))
    wout.append(flip(wout_for(3), ("yh", "c"), 3))
    returned = flip(out[1], "xl", 1)
    low_head = jnp.where(xl == 0, out[0], returned)
    high_head = jnp.where(xl == 0, returned, out[0])
    heads = jnp.concatenate([low_head, out[2], high_head], axis=1)
    h_oc = flip(heads, "c", 1)
    h_far = flip(heads, "yh", 1)
    h_foc = flip(h_far, "c", 1)

    wf = jnp.concatenate(
        [w_final, jnp.ones((WID, 1), BF16), jnp.zeros((WID, HD - 65), BF16)], axis=1
    )
    new_state, stats = finished(
        state,
        gate,
        wf,
        top,
        (part_own, part_yl, part_far, part_both),
        (heads, h_oc, h_far, h_foc),
        wout,
    )

    got_rows = lax.all_to_all(stats, Y8, 0, 0, tiled=True)
    request_pick = jnp.arange(REQ, dtype=jnp.int32) == xh
    guide_scale = jnp.sum(jnp.where(request_pick, guidance, 0)).astype(F32) / 2.0
    own_step = jnp.sum(jnp.where(request_pick, step_size, 0.0))
    guide = jnp.stack([own_step, guide_scale])
    every = lax.all_to_all(block_sums(got_rows), XZ, 0, 0, tiled=True)
    next_latent = next_latents(guide, got_rows, latent)
    every = every.reshape(2, 16, HD)
    state_norm = jnp.sqrt(jnp.sum(every[:, :, 66], axis=1) / (2.0 * SEQ_LEN * D))
    top_score = jnp.max(every[:, :, 67], axis=1)
    return (new_state, next_latent, state_norm, top_score)


def solution(mesh):
    split = Mesh(mesh.devices.reshape(2, 2, 8, 2, 2, 2), ALL)
    return jax.shard_map(
        body,
        mesh=split,
        in_specs=(
            P(SEQ, TP),
            P(SEQ, None),
            P(TP, SEQ),
            P(None, None, TP),
            P(SEQ, TP),
            P(TP, None),
            P(TP, None),
            P(TP, None),
            P(SEQ, TP),
            P(TP, None),
            P(),
            P(None, SEQ),
            P(),
            P(),
        ),
        out_specs=(P(SEQ, TP), P(SEQ, None), P(), P()),
        check_vma=False,
    )
```

```python
import functools
import math

import jax
import jax.numpy as jnp
from jax import lax
from jax.experimental import pallas as pl
from jax.experimental.pallas import tpu as pltpu
from jax.sharding import Mesh
from jax.sharding import PartitionSpec as P


D = 3072
HD = 128
REQ = 2
TOK = 288
HALF = 144
TXT = 512
STEPS = 28
WID = 768
SEQ_LEN = 4608
TIME_SHIFT = 1.15
ROPE_THETA = 10000.0
EPS = 1e-06
MASKED = -1e30
ALL = ("xh", "xl", "z", "yl", "yh", "c")
SEQ = ("xh", "xl", "z", "yl")
XZ = ("xh", "xl", "z")
TP = ("yh", "c")
Y8 = ("yl", "yh", "c")
X = ("xh", "xl")
YY = ("yl", "yh")
F32 = jnp.float32
BF16 = jnp.bfloat16
EXP2_SCALE = math.log2(math.e) / math.sqrt(HD)
SCORE_SCALE = 1.0 / math.sqrt(HD)


def flip(value, axis, bits):
    return lax.ppermute(value, axis, [(i, i ^ bits) for i in range(lax.axis_size(axis))])


def turn(value, axis, by):
    count = lax.axis_size(axis)
    return lax.ppermute(value, axis, [(i, (i + by) % count) for i in range(count)])


def exchange(value, axis):
    return lax.all_to_all(value, axis, 0, 0, tiled=True)


def sigma_of(step_count):
    fraction = 1.0 - step_count.astype(F32) / STEPS
    boosted = math.exp(TIME_SHIFT) * fraction
    return boosted / (boosted + 1.0 - fraction)


def time_embedding(sigma_vals, start, width):
    half_width = D // 2
    entry = start + jnp.arange(width, dtype=jnp.int32)
    in_cos = entry < half_width
    index = jnp.where(in_cos, entry, entry - half_width).astype(F32)
    frequency = jnp.exp(-math.log(10000.0) * index / half_width)
    phases = 1000.0 * sigma_vals[:, None] * frequency[None, :]
    return jnp.where(in_cos[None, :], jnp.cos(phases), jnp.sin(phases))


def rope_tables(id_rows):
    lane = jnp.arange(HD, dtype=jnp.int32)
    width = jnp.where(lane < 16, 16.0, 56.0).astype(F32)
    first = jnp.where(lane < 16, 0, jnp.where(lane < 72, 16, 72))
    index = ((lane - first) // 2).astype(F32)
    omega = jnp.exp(-math.log(ROPE_THETA) * 2.0 * index / width)
    ids = id_rows.astype(F32)[:, :, None]
    chosen = jnp.where(lane < 16, ids[0], jnp.where(lane < 72, ids[1], ids[2]))
    angle = chosen * omega
    sign = jnp.where(lane % 2 == 0, -1.0, 1.0)
    return jnp.cos(angle), jnp.sin(angle) * sign


def whole(shape):
    return pl.BlockSpec(shape, lambda *_: (0,) * len(shape))


SMEM = pl.BlockSpec(memory_space=pltpu.SMEM)


def cost(flops, moved, exps=0):
    return pl.CostEstimate(flops=int(flops), bytes_accessed=int(moved), transcendentals=int(exps))


def flatten_kernel(parts_ref, out_ref):
    for i in range(64):
        row = parts_ref[4 * i : 4 * i + 1, :]
        for j in range(1, 4):
            row = row + parts_ref[4 * i + j : 4 * i + j + 1, :]
        out_ref[:, 144 * i : 144 * i + 144] = row


def flattened(parts):
    return pl.pallas_call(
        flatten_kernel,
        out_shape=jax.ShapeDtypeStruct((1, 3 * D), F32),
        cost_estimate=cost(3 * D * 4, 300000),
        name="flatten_mod",
    )(parts)


def modulate_rows(at_ref, pieces, mod_ref, out_ref, begin, rows):
    here = pl.ds(begin, rows)
    values = [r[here, :].astype(F32) for r in pieces]
    mean = sum(jnp.sum(v, -1, keepdims=True) for v in values) / D
    values = [v - mean for v in values]
    spread = sum(jnp.sum(v * v, -1, keepdims=True) for v in values) / D
    scale = lax.rsqrt(spread + EPS)
    for r, v in enumerate(values):
        lanes = pl.ds(pl.multiple_of(at_ref[3 + r], WID), WID)
        gains = pl.ds(pl.multiple_of(at_ref[3 + r] + D, WID), WID)
        out_ref[here, lanes] = (
            (1.0 + mod_ref[:, gains]) * (v * scale) + mod_ref[:, lanes]
        ).astype(BF16)


def modulate_kernel(at_ref, own_ref, oc_ref, far_ref, foc_ref, mod_ref, out_ref):
    pieces = (own_ref, oc_ref, far_ref, foc_ref)

    @pl.loop(0, 6)
    def _(i):
        modulate_rows(at_ref, pieces, mod_ref, out_ref, pl.multiple_of(i * 48, 48), 48)


VMEM = pl.BlockSpec(memory_space=pltpu.VMEM)


def project_kernel(
    at_ref, own_ref, oc_ref, far_ref, foc_ref, mod_ref, w_ref, gain_ref, cos_ref, sin_ref,
    modded_ref, keep_ref, give_ref, mine_ref, lent_ref,
):
    kind = pl.program_id(0)

    @pl.when(kind == 0)
    def _():
        modulate_kernel(at_ref, own_ref, oc_ref, far_ref, foc_ref, mod_ref, modded_ref)

    high = at_ref[2] == 1
    even = lax.broadcasted_iota(jnp.int32, (TOK, HD), 1) % 2 == 0
    heads = jnp.dot(modded_ref[...], w_ref[...], preferred_element_type=F32)
    heads = [heads[:, h * HD : h * HD + HD] for h in range(3)]

    def turned():
        out = []
        for h, x in enumerate(heads):
            x = x * lax.rsqrt(jnp.mean(x * x, -1, keepdims=True) + EPS)
            x = x * gain_ref[h : h + 1, :]
            swapped = jnp.where(even, pltpu.roll(x, HD - 1, 1), pltpu.roll(x, 1, 1))
            out.append((x * cos_ref[...] + swapped * sin_ref[...]).astype(BF16))
        return out

    def dealt(three):
        mine = jnp.where(high, three[2].astype(F32), three[0].astype(F32)).astype(BF16)
        other = jnp.where(high, three[0].astype(F32), three[2].astype(F32)).astype(BF16)
        return mine, three[1], other

    @pl.when(kind == 0)
    def _():
        mine_ref[0], mine_ref[1], lent_ref[...] = dealt(turned())

    @pl.when(kind == 1)
    def _():
        keep_ref[0], shared, give_ref[0] = dealt(turned())
        keep_ref[1] = shared
        give_ref[1] = shared

    @pl.when(kind == 2)
    def _():
        keep_ref[2], shared, give_ref[2] = dealt([h.astype(BF16) for h in heads])
        keep_ref[3] = shared
        give_ref[3] = shared


def projected(at, pieces, mod, w_kinds, gains, cosine, sine):
    def out(n):
        return jax.ShapeDtypeStruct((n, TOK, HD), BF16)

    return pl.pallas_call(
        project_kernel,
        grid=(3,),
        in_specs=[SMEM]
        + [VMEM] * 5
        + [
            pl.BlockSpec((None, D, 3 * HD), lambda k: (k, 0, 0)),
            pl.BlockSpec((None, 3, HD), lambda k: (jnp.minimum(k, 1), 0, 0)),
            VMEM,
            VMEM,
        ],
        out_specs=(
            whole((TOK, D)),
            whole((4, TOK, HD)),
            whole((4, TOK, HD)),
            whole((2, TOK, HD)),
            whole((TOK, HD)),
        ),
        out_shape=(
            jax.ShapeDtypeStruct((TOK, D), BF16),
            out(4),
            out(4),
            out(2),
            jax.ShapeDtypeStruct((TOK, HD), BF16),
        ),
        cost_estimate=cost(2 * TOK * D * 9 * HD, 11e6),
        name="project",
    )(at, *pieces, mod, w_kinds, gains, cosine, sine)


def assemble_kernel(at_ref, *refs):
    out_ref = refs[-1]
    z = at_ref[7]
    for k in range(7):
        spot = lax.rem(z + (0, 7, 1, 6, 2, 5, 3)[k], 8) * 96
        out_ref[pl.ds(pl.multiple_of(spot, 32), 96), :] = refs[k][...]
    spot = lax.rem(z + 4, 8) * 96
    out_ref[pl.ds(pl.multiple_of(spot, 32), 48), :] = refs[7][...]
    out_ref[pl.ds(pl.multiple_of(spot + 48, 16), 48), :] = refs[8][...]


def assembled(at, parts):
    return pl.pallas_call(
        assemble_kernel,
        in_specs=[SMEM] + [VMEM] * 9,
        out_shape=jax.ShapeDtypeStruct((WID, 2 * WID), BF16),
        cost_estimate=cost(1e5, 5e6),
        name="assemble",
    )(at, *parts)


def hidden_part(at_ref, rows_ref, j, w_ref):
    x = lax.rem(at_ref[8] + j, 4)
    lanes = pl.ds(pl.multiple_of(x * WID, WID), WID)
    return jnp.dot(rows_ref[:, lanes], w_ref[...], preferred_element_type=F32)


def gathered_rows(mine_ref, low_ref, high_ref, rows_ref):
    @pl.when(pl.program_id(0) == 0)
    def _():
        rows_ref[...] = mine_ref[...]

    @pl.when(pl.program_id(0) == 1)
    def _():
        rows_ref[:HALF] = low_ref[...]
        rows_ref[HALF:] = high_ref[...]


def early_kernel(at_ref, mine_ref, low_ref, high_ref, w0_ref, w1_ref, w3_ref, out_ref, rows_ref):
    gathered_rows(mine_ref, low_ref, high_ref, rows_ref)
    total = hidden_part(at_ref, rows_ref, 0, w0_ref)
    total = total + hidden_part(at_ref, rows_ref, 1, w1_ref)
    out_ref[...] = total + hidden_part(at_ref, rows_ref, 3, w3_ref)


def late_kernel(
    at_ref, pre_ref, mine_ref, low_ref, high_ref,
    wl_ref, wh_ref, d0_ref, d1_ref, dl_ref, dh_ref, d3_ref, out_ref, rows_ref,
):
    def block(j):
        return at_ref[9 + j]

    far = lax.rem(at_ref[8] + 2, 4) * WID
    gathered_rows(mine_ref, low_ref, high_ref, rows_ref)
    total = pre_ref[...]
    for n, w_ref in enumerate((wl_ref, wh_ref)):
        lanes = pl.ds(pl.multiple_of(far + n * (WID // 2), WID // 2), WID // 2)
        total = total + jnp.dot(rows_ref[:, lanes], w_ref[...], preferred_element_type=F32)
    cubic = total + 0.044715 * (total * total * total)
    hidden = total * (0.5 + 0.5 * jnp.tanh(math.sqrt(2.0 / math.pi) * cubic))
    hidden = hidden.astype(BF16)

    def down(w):
        return lax.dot_general(
            hidden, w[...], (((1,), (1,)), ((), ())), preferred_element_type=F32
        ).astype(BF16)

    for j, w_ref in ((0, d0_ref), (1, d1_ref), (3, d3_ref)):
        out_ref[block(j)] = down(w_ref)
    out_ref[block(2), :, : WID // 2] = down(dl_ref)
    out_ref[block(2), :, WID // 2 :] = down(dh_ref)


def mlp(at, mine, low, high, w0, w1, w2, w3):
    half = WID // 2

    def left(rows=WID):
        return pl.BlockSpec((rows, WID), lambda i: (0, 0))

    def right(rows=WID):
        return pl.BlockSpec((rows, WID), lambda i: (0, 1))

    part = pl.BlockSpec((None, TOK, WID), lambda i: (i, 0, 0))
    rows = [VMEM, VMEM, VMEM]
    scratch = [pltpu.VMEM((TOK, D), BF16)]
    pre = pl.pallas_call(
        early_kernel,
        grid=(2,),
        in_specs=[SMEM, *rows, left(), left(), left()],
        out_specs=part,
        out_shape=jax.ShapeDtypeStruct((2, TOK, WID), F32),
        scratch_shapes=scratch,
        cost_estimate=cost(6 * 2 * TOK * WID * WID, 9e6),
        name="mlp_early",
    )(at, mine, low, high, w0, w1, w3)
    return pl.pallas_call(
        late_kernel,
        grid=(2,),
        in_specs=[SMEM, part, *rows, left(half), left(half)]
        + [right(), right(), right(half), right(half), right()],
        out_specs=pl.BlockSpec((4, None, TOK, WID), lambda i: (0, i, 0, 0)),
        out_shape=jax.ShapeDtypeStruct((4, 2, TOK, WID), BF16),
        scratch_shapes=scratch,
        cost_estimate=cost(10 * 2 * TOK * WID * WID, 16e6),
        name="mlp_late",
    )(at, pre, mine, low, high, *w2, w0, w1, *w2, w3)


def attend_kernel(first, last, makers, *refs):
    count = len(makers)
    at_ref, own_ref, taken_ref = refs[:3]
    kv = refs[3 : 3 + 2 * count]
    rest = refs[3 + 2 * count :]
    if not first:
        stat_in, acc_in = rest[:2]
        rest = rest[2:]
    taken = jnp.full((TOK, HD), pl.program_id(0), jnp.int32) == 1
    queries = jnp.where(taken, taken_ref[...].astype(F32), own_ref[...].astype(F32)).astype(BF16)
    keys = jnp.concatenate([r[...] for r in kv[:count]], axis=0)
    values = jnp.concatenate([r[...] for r in kv[count:]], axis=0)
    token = lax.broadcasted_iota(jnp.int32, (1, count * TOK), 1)
    place = jnp.zeros((1, count * TOK), jnp.int32)
    for n, (by, side) in enumerate(makers):
        row = at_ref[2] if side == 0 else 1 - at_ref[2]
        start = (row * 8 + lax.rem(at_ref[7] + by, 8) - n) * TOK
        place = jnp.where(token >= n * TOK, token + start, place)
    live = (place >= TXT) | (place < at_ref[13])
    bias = jnp.where(live, 0.0, MASKED).astype(F32)
    scores = lax.dot_general(
        queries, keys, (((1,), (1,)), ((), ())), preferred_element_type=F32
    )
    scores = scores + bias
    peak = jnp.max(scores, axis=1, keepdims=True)
    if not first:
        peak = jnp.maximum(peak, stat_in[:, 0:1])
    weights = jnp.exp2((scores - peak) * EXP2_SCALE)
    total = jnp.sum(weights, axis=1, keepdims=True)
    acc = jnp.dot(weights.astype(BF16), values, preferred_element_type=F32)
    if not first:
        fade = jnp.exp2((stat_in[:, 0:1] - peak) * EXP2_SCALE)
        total = total + fade * stat_in[:, 64:65]
        acc = acc + fade * acc_in[...]
    if last:
        out_ref, top_ref = rest
        out_ref[...] = (acc / total).astype(BF16)
        top_ref[...] = jnp.broadcast_to(jnp.max(peak, axis=0, keepdims=True) * SCORE_SCALE, (8, HD))
    else:
        stat_ref, acc_ref = rest
        lane = lax.broadcasted_iota(jnp.int32, (TOK, HD), 1)
        stat_ref[...] = jnp.where(lane < 64, peak, total)
        acc_ref[...] = acc


def attended_more(at, own_q, taken_q, makers, keys, values, carry, last):
    count = len(makers)
    first = carry is None
    unit = pl.BlockSpec((None, TOK, HD), lambda u: (u, 0, 0))
    shared = pl.BlockSpec((None, TOK, HD), lambda u: (u // 2, 0, 0))
    later = pl.BlockSpec((None, TOK, HD), lambda u: (2 + u // 2, 0, 0))
    specs = [SMEM, shared, whole((TOK, HD))] + [shared] * count
    specs += [later if v.shape[0] == 4 else shared for v in values]
    args = [at, own_q, taken_q, *keys, *values]
    if not first:
        specs += [unit, unit]
        args += list(carry)
    state = jax.ShapeDtypeStruct((3, TOK, HD), F32)
    if last:
        outs = (jax.ShapeDtypeStruct((3, TOK, HD), BF16), jax.ShapeDtypeStruct((3, 8, HD), F32))
        out_specs = (unit, pl.BlockSpec((None, 8, HD), lambda u: (u, 0, 0)))
    else:
        outs, out_specs = (state, state), (unit, unit)
    width = count * TOK
    return pl.pallas_call(
        functools.partial(attend_kernel, first, last, makers),
        grid=(3,),
        in_specs=specs,
        out_specs=out_specs,
        out_shape=outs,
        cost_estimate=cost(3 * TOK * width * HD * 4, 4e6, 3 * TOK * width),
        name="attend",
    )(*args)


def finish_kernel(*refs):
    state_ref, gate_ref, wf_ref, top_ref = refs[:4]
    parts = refs[4:8]
    heads = refs[8:12]
    wout = refs[12:16]
    new_ref, stat_ref = refs[16:]
    update = parts[0][...].astype(F32)
    for r in parts[1:]:
        update = update + r[...].astype(F32)
    for h, w in zip(heads, wout):
        update = update + jnp.dot(h[...], w[...], preferred_element_type=F32)
    new = (state_ref[...].astype(F32) + gate_ref[...] * update).astype(BF16)
    new_ref[...] = new
    wide = new.astype(F32)
    squares = jnp.sum(wide * wide, axis=1, keepdims=True)
    lane = lax.broadcasted_iota(jnp.int32, (TOK, HD), 1)
    stats = jnp.dot(new, wf_ref[...], preferred_element_type=F32)
    stats = jnp.where(lane == 65, squares, stats)
    total = jnp.sum(squares, axis=0, keepdims=True)
    ones = jnp.ones((16, WID), BF16)
    extra = jnp.dot(ones, wf_ref[...], preferred_element_type=F32)[:8]
    lane8 = lax.broadcasted_iota(jnp.int32, (8, HD), 1)
    top = jnp.max(top_ref[...], axis=0)
    extra = jnp.where(lane8 == 66, total, jnp.where(lane8 == 67, top, extra))
    for h in range(8):
        half = h // 4
        stat_ref[h, :HALF, :] = stats[half * HALF : (half + 1) * HALF]
        stat_ref[h, HALF:, :] = extra


def finished(state, gate, wf, top, parts, heads, wout):
    return pl.pallas_call(
        finish_kernel,
        out_shape=(
            jax.ShapeDtypeStruct((TOK, WID), BF16),
            jax.ShapeDtypeStruct((8, HALF + 8, HD), F32),
        ),
        cost_estimate=cost(2 * TOK * 1536 * WID, 6e6),
        name="finish",
    )(state, gate, wf, top, *parts, *heads, *wout)


def sums_kernel(got_ref, sums_ref):
    total, top = got_ref[0, HALF : HALF + 1, :], got_ref[0, HALF : HALF + 1, :]
    for i in range(1, 8):
        total = total + got_ref[i, HALF : HALF + 1, :]
        top = jnp.maximum(top, got_ref[i, HALF : HALF + 1, :])
    lane = lax.broadcasted_iota(jnp.int32, (1, HD), 1)
    row = jnp.where(lane == 67, top, total)
    for i in range(32):
        sums_ref[i] = row


def latent_kernel(guide_ref, got_ref, latent_ref, next_ref):
    def velocity(h):
        total = got_ref[4 * h] + got_ref[4 * h + 1] + got_ref[4 * h + 2] + got_ref[4 * h + 3]
        mean = total[:HALF, 64:65] / D
        spread = total[:HALF, 65:66] / D - mean * mean
        product = total[:HALF, :64] - mean * total[HALF : HALF + 1, :64]
        return product * lax.rsqrt(spread + EPS)

    cond, uncond = velocity(0), velocity(1)
    step, scale = guide_ref[0], guide_ref[1]
    next_ref[...] = latent_ref[...] + step * (uncond + scale * (cond - uncond))


def block_sums(got):
    return pl.pallas_call(
        sums_kernel,
        in_specs=[pl.BlockSpec((8, HALF + 8, HD), lambda *_: (0, 0, 0))],
        out_shape=jax.ShapeDtypeStruct((32, 1, HD), F32),
        cost_estimate=cost(1e4, 7e5),
        name="block_sums",
    )(got)


def next_latents(guide, got, latent):
    return pl.pallas_call(
        latent_kernel,
        in_specs=[SMEM, whole(got.shape), whole(latent.shape)],
        out_specs=whole(latent.shape),
        out_shape=jax.ShapeDtypeStruct(latent.shape, F32),
        cost_estimate=cost(4e5, 7e5),
        name="next_latent",
    )(guide, got, latent)


def body(
    state,
    latent,
    w_mod,
    w_qkv,
    w_mlp_in,
    q_gain,
    k_gain,
    w_out,
    w_mlp_down,
    w_final,
    text_len,
    rope_ids,
    guidance,
    step_index,
):
    xh, xl, z, yl, yh, core = (lax.axis_index(a) for a in ALL)
    tp = 2 * yh + core
    x = 2 * xh + xl
    blocks = [(tp ^ r) * WID for r in range(4)]
    owners = [((x + j) % 4) ^ tp for j in range(4)]
    flat_len = text_len.reshape(2 * REQ)
    own_len = jnp.sum(
        jnp.where(jnp.arange(2 * REQ, dtype=jnp.int32) == xh * 2 + yl, flat_len, 0)
    )
    at = jnp.stack([yh, core, xl, *blocks, z, x, *owners, own_len]).astype(jnp.int32)

    both = jnp.stack([w_mlp_in, w_mlp_down])
    keep = lax.dynamic_slice_in_dim(both, yl * WID, WID, 2)
    give = lax.dynamic_slice_in_dim(both, (1 - yl) * WID, WID, 2)
    taken = flip(give, "yl", 1)
    low = jnp.where(yl == 0, keep, taken)
    high = jnp.where(yl == 0, taken, keep)
    rows96 = jnp.concatenate([low, high], axis=1)
    rows96 = jnp.concatenate([rows96[0], rows96[1]], axis=1)
    w_up1 = turn(rows96, "z", 1)
    w_dn1 = turn(rows96, "z", -1)
    w_up2 = turn(rows96, "z", 2)
    w_dn2 = turn(rows96, "z", -2)
    w_up3 = turn(w_up2, "z", 1)
    w_dn3 = turn(w_dn2, "z", -1)
    w_up4 = turn(w_up2[:48], "z", 2)
    w_dn4 = turn(w_dn2[48:], "z", -2)
    w_parts = [rows96, w_up1, w_dn1, w_up2, w_dn2, w_up3, w_dn3, w_up4, w_dn4]
    w_here = assembled(at, w_parts)
    w_before = turn(w_here, X, 1)
    w_after = turn(w_here, X, -1)
    w_far_low = turn(w_before[: WID // 2], X, 1)
    w_far_high = turn(w_after[WID // 2 :], X, -1)

    s_oc = flip(state, "c", 1)
    s_far = flip(state, "yh", 1)
    s_foc = flip(s_far, "c", 1)

    sigma_now = sigma_of(step_index)
    step_size = sigma_of(step_index + 1) - sigma_now
    time_rows = jax.nn.silu(time_embedding(sigma_now, tp * WID, WID)).astype(BF16)
    partial_mod = jnp.dot(time_rows, w_mod, preferred_element_type=F32)
    sent = jnp.repeat(partial_mod, 128, axis=0)[:, None, :]
    got = exchange(sent, ALL)
    mod = flattened(got.reshape(256, 144))
    gate = lax.dynamic_slice_in_dim(mod, 2 * D + tp * WID, WID, 1)

    cosine, sine = rope_tables(rope_ids)
    w_kinds = w_qkv.transpose(1, 0, 2)
    gains = jnp.stack([q_gain, k_gain])
    pieces = (state, s_oc, s_far, s_foc)
    modded, own_kv, give_kv, own_q, give_q = projected(
        at, pieces, mod, w_kinds, gains, cosine, sine
    )
    taken_kv = flip(give_kv, "xl", 1)
    taken_q = flip(give_q, "xl", 1)
    other_low = flip(modded[:HALF], "yl", 1)
    other_high = flip(modded[HALF:], YY, 3)

    ups, dns, seen, makers = [own_kv, taken_kv], [own_kv, taken_kv], [own_kv, taken_kv], [(0, 0), (0, 1)]
    carry = None
    for k in range(1, 4):
        for side in range(2):
            ups[side] = turn(ups[side], "z", 1)
            dns[side] = turn(dns[side], "z", -1)
        seen = seen + ups + dns
        makers = makers + [(8 - k, 0), (8 - k, 1), (k, 0), (k, 1)]
        if k != 2:
            carry = attended_more(at, own_q, taken_q, tuple(makers), seen, seen, carry, False)
            seen, makers = [], []
    lows = [turn(ups[side][:2], "z", 1) for side in range(2)]
    highs = [turn(dns[side][2:], "z", -1) for side in range(2)]
    out, top = attended_more(at, own_q, taken_q, ((4, 0), (4, 1)), lows, highs, carry, True)

    products = mlp(
        at, modded, other_low, other_high, w_here, w_after, (w_far_low, w_far_high), w_before
    )
    crossed = flip(jnp.stack([products[1], products[3]]), "c", 1)

    def added(i):
        total = products[2 * i].astype(F32) + crossed[i].astype(F32)
        return total.astype(BF16)

    near, away = added(0), added(1)
    part_yl = flip(near[1], "yl", 1)
    part_far = flip(away[0], "yh", 1)
    part_both = flip(away[1], YY, 3)

    def wout_for(r):
        return lax.dynamic_slice_in_dim(w_out, (tp ^ r) * WID, WID, 1)

    wout = [
        wout_for(0), flip(wout_for(1), "c", 1), flip(wout_for(2), "yh", 1), flip(wout_for(3), TP, 3)
    ]
    returned = flip(out[1], "xl", 1)
    low_head = jnp.where(xl == 0, out[0], returned)
    high_head = jnp.where(xl == 0, returned, out[0])
    heads = jnp.concatenate([low_head, out[2], high_head], axis=1)
    h_oc = flip(heads, "c", 1)
    h_far = flip(heads, "yh", 1)
    h_foc = flip(h_far, "c", 1)

    wf = jnp.concatenate(
        [w_final, jnp.ones((WID, 1), BF16), jnp.zeros((WID, HD - 65), BF16)], axis=1
    )
    parts = (near[0], part_yl, part_far, part_both)
    new_state, stats = finished(state, gate, wf, top, parts, (heads, h_oc, h_far, h_foc), wout)

    got_rows = exchange(stats, Y8)
    request_pick = jnp.arange(REQ, dtype=jnp.int32) == xh
    guide_scale = jnp.sum(jnp.where(request_pick, guidance, 0)).astype(F32) / 2.0
    own_step = jnp.sum(jnp.where(request_pick, step_size, 0.0))
    guide = jnp.stack([own_step, guide_scale])
    every = exchange(block_sums(got_rows), XZ)
    next_latent = next_latents(guide, got_rows, latent)
    every = every.reshape(2, 16, HD)
    state_norm = jnp.sqrt(jnp.sum(every[:, :, 66], axis=1) / (2.0 * SEQ_LEN * D))
    top_score = jnp.max(every[:, :, 67], axis=1)
    return (new_state, next_latent, state_norm, top_score)


def solution(mesh):
    split = Mesh(mesh.devices.reshape(2, 2, 8, 2, 2, 2), ALL)
    return jax.shard_map(
        body,
        mesh=split,
        in_specs=(
            P(SEQ, TP),
            P(SEQ, None),
            P(TP, SEQ),
            P(None, None, TP),
            P(SEQ, TP),
            P(TP, None),
            P(TP, None),
            P(TP, None),
            P(SEQ, TP),
            P(TP, None),
            P(),
            P(None, SEQ),
            P(),
            P(),
        ),
        out_specs=(P(SEQ, TP), P(SEQ, None), P(), P()),
        check_vma=False,
    )
```

```python
import functools
import math

import jax
import jax.numpy as jnp
from jax import lax
from jax.experimental import pallas as pl
from jax.experimental.pallas import tpu as pltpu
from jax.sharding import Mesh
from jax.sharding import PartitionSpec as P


D = 3072
HD = 128
REQ = 2
TOK = 288
HALF = 144
TXT = 512
STEPS = 28
WID = 768
SEQ_LEN = 4608
TIME_SHIFT = 1.15
ROPE_THETA = 10000.0
EPS = 1e-06
MASKED = -1e30
ALL = ("xh", "xl", "z", "yl", "yh", "c")
SEQ = ("xh", "xl", "z", "yl")
XZ = ("xh", "xl", "z")
TP = ("yh", "c")
Y8 = ("yl", "yh", "c")
X = ("xh", "xl")
YY = ("yl", "yh")
F32 = jnp.float32
BF16 = jnp.bfloat16
EXP2_SCALE = math.log2(math.e) / math.sqrt(HD)
SCORE_SCALE = 1.0 / math.sqrt(HD)


def flip(value, axis, bits):
    return lax.ppermute(value, axis, [(i, i ^ bits) for i in range(lax.axis_size(axis))])


def turn(value, axis, by):
    count = lax.axis_size(axis)
    return lax.ppermute(value, axis, [(i, (i + by) % count) for i in range(count)])


def exchange(value, axis):
    return lax.all_to_all(value, axis, 0, 0, tiled=True)


def sigma_of(step_count):
    fraction = 1.0 - step_count.astype(F32) / STEPS
    boosted = math.exp(TIME_SHIFT) * fraction
    return boosted / (boosted + 1.0 - fraction)


def time_embedding(sigma_vals, start, width):
    half_width = D // 2
    entry = start + jnp.arange(width, dtype=jnp.int32)
    in_cos = entry < half_width
    index = jnp.where(in_cos, entry, entry - half_width).astype(F32)
    frequency = jnp.exp(-math.log(10000.0) * index / half_width)
    phases = 1000.0 * sigma_vals[:, None] * frequency[None, :]
    return jnp.where(in_cos[None, :], jnp.cos(phases), jnp.sin(phases))


def rope_tables(id_rows):
    lane = jnp.arange(HD, dtype=jnp.int32)
    width = jnp.where(lane < 16, 16.0, 56.0).astype(F32)
    first = jnp.where(lane < 16, 0, jnp.where(lane < 72, 16, 72))
    index = ((lane - first) // 2).astype(F32)
    omega = jnp.exp(-math.log(ROPE_THETA) * 2.0 * index / width)
    ids = id_rows.astype(F32)[:, :, None]
    chosen = jnp.where(lane < 16, ids[0], jnp.where(lane < 72, ids[1], ids[2]))
    angle = chosen * omega
    sign = jnp.where(lane % 2 == 0, -1.0, 1.0)
    return jnp.cos(angle), jnp.sin(angle) * sign


def whole(shape):
    return pl.BlockSpec(shape, lambda *_: (0,) * len(shape))


SMEM = pl.BlockSpec(memory_space=pltpu.SMEM)


def cost(flops, moved, exps=0):
    return pl.CostEstimate(flops=int(flops), bytes_accessed=int(moved), transcendentals=int(exps))


def flatten_kernel(parts_ref, out_ref):
    for i in range(64):
        row = parts_ref[4 * i : 4 * i + 1, :]
        for j in range(1, 4):
            row = row + parts_ref[4 * i + j : 4 * i + j + 1, :]
        out_ref[:, 144 * i : 144 * i + 144] = row


def flattened(parts):
    return pl.pallas_call(
        flatten_kernel,
        out_shape=jax.ShapeDtypeStruct((1, 3 * D), F32),
        cost_estimate=cost(3 * D * 4, 300000),
        name="flatten_mod",
    )(parts)


def modulate_rows(at_ref, pieces, mod_ref, out_ref, begin, rows):
    here = pl.ds(begin, rows)
    values = [r[here, :].astype(F32) for r in pieces]
    mean = sum(jnp.sum(v, -1, keepdims=True) for v in values) / D
    values = [v - mean for v in values]
    spread = sum(jnp.sum(v * v, -1, keepdims=True) for v in values) / D
    scale = lax.rsqrt(spread + EPS)
    for r, v in enumerate(values):
        lanes = pl.ds(pl.multiple_of(at_ref[3 + r], WID), WID)
        gains = pl.ds(pl.multiple_of(at_ref[3 + r] + D, WID), WID)
        out_ref[here, lanes] = (
            (1.0 + mod_ref[:, gains]) * (v * scale) + mod_ref[:, lanes]
        ).astype(BF16)


def modulate_kernel(at_ref, own_ref, oc_ref, far_ref, foc_ref, mod_ref, out_ref):
    pieces = (own_ref, oc_ref, far_ref, foc_ref)

    @pl.loop(0, 6)
    def _(i):
        modulate_rows(at_ref, pieces, mod_ref, out_ref, pl.multiple_of(i * 48, 48), 48)


VMEM = pl.BlockSpec(memory_space=pltpu.VMEM)


def project_kernel(
    at_ref, own_ref, oc_ref, far_ref, foc_ref, mod_ref, w_ref, gain_ref, cos_ref, sin_ref,
    low_ref, high_ref, keep_ref, give_ref, mine_ref, lent_ref, modded_ref,
):
    kind = pl.program_id(0)

    @pl.when(kind == 0)
    def _():
        modulate_kernel(at_ref, own_ref, oc_ref, far_ref, foc_ref, mod_ref, modded_ref)
        low_ref[...] = modded_ref[:HALF]
        high_ref[...] = modded_ref[HALF:]

    high = at_ref[2] == 1
    even = lax.broadcasted_iota(jnp.int32, (TOK, HD), 1) % 2 == 0
    heads = jnp.dot(modded_ref[...], w_ref[...], preferred_element_type=F32)
    heads = [heads[:, h * HD : h * HD + HD] for h in range(3)]

    def turned():
        out = []
        for h, x in enumerate(heads):
            x = x * lax.rsqrt(jnp.mean(x * x, -1, keepdims=True) + EPS)
            x = x * gain_ref[h : h + 1, :]
            swapped = jnp.where(even, pltpu.roll(x, HD - 1, 1), pltpu.roll(x, 1, 1))
            out.append((x * cos_ref[...] + swapped * sin_ref[...]).astype(BF16))
        return out

    def dealt(three):
        mine = jnp.where(high, three[2].astype(F32), three[0].astype(F32)).astype(BF16)
        other = jnp.where(high, three[0].astype(F32), three[2].astype(F32)).astype(BF16)
        return mine, three[1], other

    @pl.when(kind == 0)
    def _():
        mine_ref[0], mine_ref[1], lent_ref[...] = dealt(turned())

    @pl.when(kind == 1)
    def _():
        keep_ref[0], shared, give_ref[0] = dealt(turned())
        keep_ref[1] = shared
        give_ref[1] = shared

    @pl.when(kind == 2)
    def _():
        keep_ref[2], shared, give_ref[2] = dealt([h.astype(BF16) for h in heads])
        keep_ref[3] = shared
        give_ref[3] = shared


def projected(at, pieces, mod, w_kinds, gains, cosine, sine):
    def out(n):
        return jax.ShapeDtypeStruct((n, TOK, HD), BF16)

    return pl.pallas_call(
        project_kernel,
        grid=(3,),
        in_specs=[SMEM]
        + [VMEM] * 5
        + [
            pl.BlockSpec((None, D, 3 * HD), lambda k: (k, 0, 0)),
            pl.BlockSpec((None, 3, HD), lambda k: (jnp.minimum(k, 1), 0, 0)),
            VMEM,
            VMEM,
        ],
        out_specs=(
            whole((HALF, D)),
            whole((HALF, D)),
            whole((4, TOK, HD)),
            whole((4, TOK, HD)),
            whole((2, TOK, HD)),
            whole((TOK, HD)),
        ),
        out_shape=(
            jax.ShapeDtypeStruct((HALF, D), BF16),
            jax.ShapeDtypeStruct((HALF, D), BF16),
            out(4),
            out(4),
            out(2),
            jax.ShapeDtypeStruct((TOK, HD), BF16),
        ),
        scratch_shapes=[pltpu.VMEM((TOK, D), BF16)],
        cost_estimate=cost(2 * TOK * D * 9 * HD, 11e6),
        name="project",
    )(at, *pieces, mod, w_kinds, gains, cosine, sine)


def assemble_kernel(at_ref, *refs):
    z = at_ref[7]
    turns = (0, 7, 1, 6, 2, 5, 3, 4, 4)
    for k, by in enumerate(turns):
        maker = lax.rem(z + by, 8)
        offset = pl.multiple_of(lax.rem(maker, 4) * 96 + (48 if k == 8 else 0), 16)
        rows = pl.ds(offset, refs[k].shape[0])
        for side, out_ref in enumerate(refs[9:]):

            @pl.when(maker // 4 == side)
            def _():
                out_ref[rows, :] = refs[k][...]


def assembled(at, parts):
    return pl.pallas_call(
        assemble_kernel,
        in_specs=[SMEM] + [VMEM] * 9,
        out_shape=[jax.ShapeDtypeStruct((WID // 2, 2 * WID), BF16)] * 2,
        cost_estimate=cost(1e5, 5e6),
        name="assemble",
    )(at, *parts)


def gathered_rows(halves, rows_ref):
    for i in range(2):

        @pl.when(pl.program_id(0) == i)
        def _():
            rows_ref[:HALF] = halves[2 * i][...]
            rows_ref[HALF:] = halves[2 * i + 1][...]


def hidden_part(at_ref, rows_ref, j, halves):
    x = lax.rem(at_ref[8] + j, 4)
    total = None
    for n, w_ref in enumerate(halves):
        wide = w_ref.shape[0]
        lanes = pl.ds(pl.multiple_of(x * WID + n * wide, wide), wide)
        part = jnp.dot(rows_ref[:, lanes], w_ref[...], preferred_element_type=F32)
        total = part if total is None else total + part
    return total


def early_kernel(at_ref, *refs):
    rows_ref = refs[-1]
    gathered_rows(refs[:4], rows_ref)
    total = hidden_part(at_ref, rows_ref, 0, refs[4:6])
    total = total + hidden_part(at_ref, rows_ref, 1, refs[6:8])
    refs[-2][...] = total + hidden_part(at_ref, rows_ref, 3, refs[8:10])


def late_kernel(at_ref, pre_ref, *refs):
    out_ref, rows_ref = refs[-2:]
    gathered_rows(refs[:4], rows_ref)
    total = pre_ref[...] + hidden_part(at_ref, rows_ref, 2, refs[4:6])
    cubic = total + 0.044715 * (total * total * total)
    hidden = total * (0.5 + 0.5 * jnp.tanh(math.sqrt(2.0 / math.pi) * cubic))
    hidden = hidden.astype(BF16)
    for j, halves in ((0, refs[6:8]), (1, refs[8:10]), (2, refs[10:12]), (3, refs[12:14])):
        begin = 0
        for w_ref in halves:
            down = lax.dot_general(
                hidden, w_ref[...], (((1,), (1,)), ((), ())), preferred_element_type=F32
            )
            out_ref[at_ref[9 + j], :, begin : begin + down.shape[1]] = down.astype(BF16)
            begin += down.shape[1]


def mlp(at, halves, w0, w1, w2, w3):
    half = WID // 2

    def left(rows=half):
        return pl.BlockSpec((rows, WID), lambda i: (0, 0))

    def right(rows=half):
        return pl.BlockSpec((rows, WID), lambda i: (0, 1))

    part = pl.BlockSpec((None, TOK, WID), lambda i: (i, 0, 0))
    scratch = [pltpu.VMEM((TOK, D), BF16)]
    pre = pl.pallas_call(
        early_kernel,
        grid=(2,),
        in_specs=[SMEM] + [VMEM] * 4 + [left()] * 6,
        out_specs=part,
        out_shape=jax.ShapeDtypeStruct((2, TOK, WID), F32),
        scratch_shapes=scratch,
        cost_estimate=cost(6 * 2 * TOK * WID * WID, 9e6),
        name="mlp_early",
    )(at, *halves, *w0, *w1, *w3)
    return pl.pallas_call(
        late_kernel,
        grid=(2,),
        in_specs=[SMEM, part] + [VMEM] * 4 + [left()] * 2 + [right()] * 8,
        out_specs=pl.BlockSpec((4, None, TOK, WID), lambda i: (0, i, 0, 0)),
        out_shape=jax.ShapeDtypeStruct((4, 2, TOK, WID), BF16),
        scratch_shapes=scratch,
        cost_estimate=cost(10 * 2 * TOK * WID * WID, 16e6),
        name="mlp_late",
    )(at, pre, *halves, *w2, *w0, *w1, *w2, *w3)


def attend_kernel(first, last, makers, *refs):
    count = len(makers)
    at_ref, own_ref, taken_ref = refs[:3]
    kv = refs[3 : 3 + 2 * count]
    rest = refs[3 + 2 * count :]
    if not first:
        stat_in, acc_in = rest[:2]
        rest = rest[2:]
    taken = jnp.full((TOK, HD), pl.program_id(0), jnp.int32) == 1
    queries = jnp.where(taken, taken_ref[...].astype(F32), own_ref[...].astype(F32)).astype(BF16)
    keys = jnp.concatenate([r[...] for r in kv[:count]], axis=0)
    values = jnp.concatenate([r[...] for r in kv[count:]], axis=0)
    token = lax.broadcasted_iota(jnp.int32, (1, count * TOK), 1)
    place = jnp.zeros((1, count * TOK), jnp.int32)
    for n, (by, side) in enumerate(makers):
        row = at_ref[2] if side == 0 else 1 - at_ref[2]
        start = (row * 8 + lax.rem(at_ref[7] + by, 8) - n) * TOK
        place = jnp.where(token >= n * TOK, token + start, place)
    live = (place >= TXT) | (place < at_ref[13])
    bias = jnp.where(live, 0.0, MASKED).astype(F32)
    scores = lax.dot_general(
        queries, keys, (((1,), (1,)), ((), ())), preferred_element_type=F32
    )
    scores = scores + bias
    peak = jnp.max(scores, axis=1, keepdims=True)
    if not first:
        peak = jnp.maximum(peak, stat_in[:, 0:1])
    weights = jnp.exp2((scores - peak) * EXP2_SCALE)
    total = jnp.sum(weights, axis=1, keepdims=True)
    acc = jnp.dot(weights.astype(BF16), values, preferred_element_type=F32)
    if not first:
        fade = jnp.exp2((stat_in[:, 0:1] - peak) * EXP2_SCALE)
        total = total + fade * stat_in[:, 64:65]
        acc = acc + fade * acc_in[...]
    if last:
        out_ref, top_ref = rest
        out_ref[...] = (acc / total).astype(BF16)
        top_ref[...] = jnp.broadcast_to(jnp.max(peak, axis=0, keepdims=True) * SCORE_SCALE, (8, HD))
    else:
        stat_ref, acc_ref = rest
        lane = lax.broadcasted_iota(jnp.int32, (TOK, HD), 1)
        stat_ref[...] = jnp.where(lane < 64, peak, total)
        acc_ref[...] = acc


def attended_more(at, own_q, taken_q, makers, keys, values, carry, last):
    count = len(makers)
    first = carry is None
    unit = pl.BlockSpec((None, TOK, HD), lambda u: (u, 0, 0))
    shared = pl.BlockSpec((None, TOK, HD), lambda u: (u // 2, 0, 0))
    later = pl.BlockSpec((None, TOK, HD), lambda u: (2 + u // 2, 0, 0))
    specs = [SMEM, shared, whole((TOK, HD))] + [shared] * count
    specs += [later if v.shape[0] == 4 else shared for v in values]
    args = [at, own_q, taken_q, *keys, *values]
    if not first:
        specs += [unit, unit]
        args += list(carry)
    state = jax.ShapeDtypeStruct((3, TOK, HD), F32)
    if last:
        outs = (jax.ShapeDtypeStruct((3, TOK, HD), BF16), jax.ShapeDtypeStruct((3, 8, HD), F32))
        out_specs = (unit, pl.BlockSpec((None, 8, HD), lambda u: (u, 0, 0)))
    else:
        outs, out_specs = (state, state), (unit, unit)
    width = count * TOK
    return pl.pallas_call(
        functools.partial(attend_kernel, first, last, makers),
        grid=(3,),
        in_specs=specs,
        out_specs=out_specs,
        out_shape=outs,
        cost_estimate=cost(3 * TOK * width * HD * 4, 4e6, 3 * TOK * width),
        name="attend",
    )(*args)


def finish_kernel(*refs):
    state_ref, gate_ref, wf_ref, top_ref = refs[:4]
    parts = refs[4:8]
    heads = refs[8:12]
    wout = refs[12:16]
    new_ref, stat_ref = refs[16:]
    update = parts[0][...].astype(F32)
    for r in parts[1:]:
        update = update + r[...].astype(F32)
    for h, w in zip(heads, wout):
        update = update + jnp.dot(h[...], w[...], preferred_element_type=F32)
    new = (state_ref[...].astype(F32) + gate_ref[...] * update).astype(BF16)
    new_ref[...] = new
    wide = new.astype(F32)
    squares = jnp.sum(wide * wide, axis=1, keepdims=True)
    lane = lax.broadcasted_iota(jnp.int32, (TOK, HD), 1)
    stats = jnp.dot(new, wf_ref[...], preferred_element_type=F32)
    stats = jnp.where(lane == 65, squares, stats)
    total = jnp.sum(squares, axis=0, keepdims=True)
    ones = jnp.ones((16, WID), BF16)
    extra = jnp.dot(ones, wf_ref[...], preferred_element_type=F32)[:8]
    lane8 = lax.broadcasted_iota(jnp.int32, (8, HD), 1)
    top = jnp.max(top_ref[...], axis=0)
    extra = jnp.where(lane8 == 66, total, jnp.where(lane8 == 67, top, extra))
    for h in range(8):
        half = h // 4
        stat_ref[h, :HALF, :] = stats[half * HALF : (half + 1) * HALF]
        stat_ref[h, HALF:, :] = extra


def finished(state, gate, wf, top, parts, heads, wout):
    return pl.pallas_call(
        finish_kernel,
        out_shape=(
            jax.ShapeDtypeStruct((TOK, WID), BF16),
            jax.ShapeDtypeStruct((8, HALF + 8, HD), F32),
        ),
        cost_estimate=cost(2 * TOK * 1536 * WID, 6e6),
        name="finish",
    )(state, gate, wf, top, *parts, *heads, *wout)


def sums_kernel(got_ref, sums_ref):
    total, top = got_ref[0, HALF : HALF + 1, :], got_ref[0, HALF : HALF + 1, :]
    for i in range(1, 8):
        total = total + got_ref[i, HALF : HALF + 1, :]
        top = jnp.maximum(top, got_ref[i, HALF : HALF + 1, :])
    lane = lax.broadcasted_iota(jnp.int32, (1, HD), 1)
    row = jnp.where(lane == 67, top, total)
    for i in range(32):
        sums_ref[i] = row


def latent_kernel(guide_ref, got_ref, latent_ref, next_ref):
    def velocity(h):
        total = got_ref[4 * h] + got_ref[4 * h + 1] + got_ref[4 * h + 2] + got_ref[4 * h + 3]
        mean = total[:HALF, 64:65] / D
        spread = total[:HALF, 65:66] / D - mean * mean
        product = total[:HALF, :64] - mean * total[HALF : HALF + 1, :64]
        return product * lax.rsqrt(spread + EPS)

    cond, uncond = velocity(0), velocity(1)
    step, scale = guide_ref[0], guide_ref[1]
    next_ref[...] = latent_ref[...] + step * (uncond + scale * (cond - uncond))


def block_sums(got):
    return pl.pallas_call(
        sums_kernel,
        in_specs=[pl.BlockSpec((8, HALF + 8, HD), lambda *_: (0, 0, 0))],
        out_shape=jax.ShapeDtypeStruct((32, 1, HD), F32),
        cost_estimate=cost(1e4, 7e5),
        name="block_sums",
    )(got)


def next_latents(guide, got, latent):
    return pl.pallas_call(
        latent_kernel,
        in_specs=[SMEM, whole(got.shape), whole(latent.shape)],
        out_specs=whole(latent.shape),
        out_shape=jax.ShapeDtypeStruct(latent.shape, F32),
        cost_estimate=cost(4e5, 7e5),
        name="next_latent",
    )(guide, got, latent)


def body(
    state,
    latent,
    w_mod,
    w_qkv,
    w_mlp_in,
    q_gain,
    k_gain,
    w_out,
    w_mlp_down,
    w_final,
    text_len,
    rope_ids,
    guidance,
    step_index,
):
    xh, xl, z, yl, yh, core = (lax.axis_index(a) for a in ALL)
    tp = 2 * yh + core
    x = 2 * xh + xl
    blocks = [(tp ^ r) * WID for r in range(4)]
    owners = [((x + j) % 4) ^ tp for j in range(4)]
    flat_len = text_len.reshape(2 * REQ)
    own_len = jnp.sum(
        jnp.where(jnp.arange(2 * REQ, dtype=jnp.int32) == xh * 2 + yl, flat_len, 0)
    )
    at = jnp.stack([yh, core, xl, *blocks, z, x, *owners, own_len]).astype(jnp.int32)

    both = jnp.stack([w_mlp_in, w_mlp_down])
    keep = lax.dynamic_slice_in_dim(both, yl * WID, WID, 2)
    give = lax.dynamic_slice_in_dim(both, (1 - yl) * WID, WID, 2)
    taken = flip(give, "yl", 1)
    low = jnp.where(yl == 0, keep, taken)
    high = jnp.where(yl == 0, taken, keep)
    rows96 = jnp.concatenate([low, high], axis=1)
    rows96 = jnp.concatenate([rows96[0], rows96[1]], axis=1)
    w_up1 = turn(rows96, "z", 1)
    w_dn1 = turn(rows96, "z", -1)
    w_up2 = turn(rows96, "z", 2)
    w_dn2 = turn(rows96, "z", -2)
    w_up3 = turn(w_up2, "z", 1)
    w_dn3 = turn(w_dn2, "z", -1)
    w_up4 = turn(w_up2[:48], "z", 2)
    w_dn4 = turn(w_dn2[48:], "z", -2)
    w_parts = [rows96, w_up1, w_dn1, w_up2, w_dn2, w_up3, w_dn3, w_up4, w_dn4]
    w_low, w_high = assembled(at, w_parts)
    before_low = turn(w_low, X, 1)
    after_high = turn(w_high, X, -1)
    before_high = turn(w_high, X, 1)
    after_low = turn(w_low, X, -1)
    far_low = turn(before_low, X, 1)
    far_high = turn(after_high, X, -1)

    s_oc = flip(state, "c", 1)
    s_far = flip(state, "yh", 1)
    s_foc = flip(s_far, "c", 1)

    sigma_now = sigma_of(step_index)
    step_size = sigma_of(step_index + 1) - sigma_now
    time_rows = jax.nn.silu(time_embedding(sigma_now, tp * WID, WID)).astype(BF16)
    partial_mod = jnp.dot(time_rows, w_mod, preferred_element_type=F32)
    sent = jnp.repeat(partial_mod, 128, axis=0)[:, None, :]
    got = exchange(sent, ALL)
    mod = flattened(got.reshape(256, 144))
    gate = lax.dynamic_slice_in_dim(mod, 2 * D + tp * WID, WID, 1)

    cosine, sine = rope_tables(rope_ids)
    w_kinds = w_qkv.transpose(1, 0, 2)
    gains = jnp.stack([q_gain, k_gain])
    pieces = (state, s_oc, s_far, s_foc)
    mine_low, mine_high, own_kv, give_kv, own_q, give_q = projected(
        at, pieces, mod, w_kinds, gains, cosine, sine
    )
    taken_kv = flip(give_kv, "xl", 1)
    taken_q = flip(give_q, "xl", 1)
    other_low = flip(mine_low, "yl", 1)
    other_high = flip(mine_high, YY, 3)

    ups, dns, seen, makers = [own_kv, taken_kv], [own_kv, taken_kv], [own_kv, taken_kv], [(0, 0), (0, 1)]
    carry = None
    for k in range(1, 4):
        for side in range(2):
            ups[side] = turn(ups[side], "z", 1)
            dns[side] = turn(dns[side], "z", -1)
        seen = seen + ups + dns
        makers = makers + [(8 - k, 0), (8 - k, 1), (k, 0), (k, 1)]
        if k != 2:
            carry = attended_more(at, own_q, taken_q, tuple(makers), seen, seen, carry, False)
            seen, makers = [], []
    lows = [turn(ups[side][:2], "z", 1) for side in range(2)]
    highs = [turn(dns[side][2:], "z", -1) for side in range(2)]
    out, top = attended_more(at, own_q, taken_q, ((4, 0), (4, 1)), lows, highs, carry, True)

    halves = (mine_low, mine_high, other_low, other_high)
    products = mlp(
        at, halves, (w_low, w_high), (after_low, after_high), (far_low, far_high), (before_low, before_high)
    )
    crossed = flip(jnp.stack([products[1], products[3]]), "c", 1)

    def added(i):
        total = products[2 * i].astype(F32) + crossed[i].astype(F32)
        return total.astype(BF16)

    near, away = added(0), added(1)
    part_yl = flip(near[1], "yl", 1)
    part_far = flip(away[0], "yh", 1)
    part_both = flip(away[1], YY, 3)

    def wout_for(r):
        return lax.dynamic_slice_in_dim(w_out, (tp ^ r) * WID, WID, 1)

    wout = [
        wout_for(0), flip(wout_for(1), "c", 1), flip(wout_for(2), "yh", 1), flip(wout_for(3), TP, 3)
    ]
    returned = flip(out[1], "xl", 1)
    low_head = jnp.where(xl == 0, out[0], returned)
    high_head = jnp.where(xl == 0, returned, out[0])
    heads = jnp.concatenate([low_head, out[2], high_head], axis=1)
    h_oc = flip(heads, "c", 1)
    h_far = flip(heads, "yh", 1)
    h_foc = flip(h_far, "c", 1)

    wf = jnp.concatenate(
        [w_final, jnp.ones((WID, 1), BF16), jnp.zeros((WID, HD - 65), BF16)], axis=1
    )
    parts = (near[0], part_yl, part_far, part_both)
    new_state, stats = finished(state, gate, wf, top, parts, (heads, h_oc, h_far, h_foc), wout)

    got_rows = exchange(stats, Y8)
    request_pick = jnp.arange(REQ, dtype=jnp.int32) == xh
    guide_scale = jnp.sum(jnp.where(request_pick, guidance, 0)).astype(F32) / 2.0
    own_step = jnp.sum(jnp.where(request_pick, step_size, 0.0))
    guide = jnp.stack([own_step, guide_scale])
    every = exchange(block_sums(got_rows), XZ)
    next_latent = next_latents(guide, got_rows, latent)
    every = every.reshape(2, 16, HD)
    state_norm = jnp.sqrt(jnp.sum(every[:, :, 66], axis=1) / (2.0 * SEQ_LEN * D))
    top_score = jnp.max(every[:, :, 67], axis=1)
    return (new_state, next_latent, state_norm, top_score)


def solution(mesh):
    split = Mesh(mesh.devices.reshape(2, 2, 8, 2, 2, 2), ALL)
    return jax.shard_map(
        body,
        mesh=split,
        in_specs=(
            P(SEQ, TP),
            P(SEQ, None),
            P(TP, SEQ),
            P(None, None, TP),
            P(SEQ, TP),
            P(TP, None),
            P(TP, None),
            P(TP, None),
            P(SEQ, TP),
            P(TP, None),
            P(),
            P(None, SEQ),
            P(),
            P(),
        ),
        out_specs=(P(SEQ, TP), P(SEQ, None), P(), P()),
        check_vma=False,
    )
```

```python
import functools
import math

import jax
import jax.numpy as jnp
from jax import lax
from jax.experimental import pallas as pl
from jax.experimental.pallas import tpu as pltpu
from jax.sharding import Mesh
from jax.sharding import PartitionSpec as P


D = 3072
HD = 128
REQ = 2
TOK = 288
HALF = 144
TXT = 512
STEPS = 28
WID = 768
SEQ_LEN = 4608
TIME_SHIFT = 1.15
ROPE_THETA = 10000.0
EPS = 1e-06
MASKED = -1e30
ALL = ("xh", "xl", "z", "yl", "yh", "c")
SEQ = ("xh", "xl", "z", "yl")
XZ = ("xh", "xl", "z")
TP = ("yh", "c")
Y8 = ("yl", "yh", "c")
X = ("xh", "xl")
YY = ("yl", "yh")
F32 = jnp.float32
BF16 = jnp.bfloat16
EXP2_SCALE = math.log2(math.e) / math.sqrt(HD)
SCORE_SCALE = 1.0 / math.sqrt(HD)


def flip(value, axis, bits):
    return lax.ppermute(value, axis, [(i, i ^ bits) for i in range(lax.axis_size(axis))])


def turn(value, axis, by):
    count = lax.axis_size(axis)
    return lax.ppermute(value, axis, [(i, (i + by) % count) for i in range(count)])


def exchange(value, axis):
    return lax.all_to_all(value, axis, 0, 0, tiled=True)


def sigma_of(step_count):
    fraction = 1.0 - step_count.astype(F32) / STEPS
    boosted = math.exp(TIME_SHIFT) * fraction
    return boosted / (boosted + 1.0 - fraction)


def time_embedding(sigma_vals, start, width):
    half_width = D // 2
    entry = start + jnp.arange(width, dtype=jnp.int32)
    in_cos = entry < half_width
    index = jnp.where(in_cos, entry, entry - half_width).astype(F32)
    frequency = jnp.exp(-math.log(10000.0) * index / half_width)
    phases = 1000.0 * sigma_vals[:, None] * frequency[None, :]
    return jnp.where(in_cos[None, :], jnp.cos(phases), jnp.sin(phases))


def rope_tables(id_rows):
    lane = jnp.arange(HD, dtype=jnp.int32)
    width = jnp.where(lane < 16, 16.0, 56.0).astype(F32)
    first = jnp.where(lane < 16, 0, jnp.where(lane < 72, 16, 72))
    index = ((lane - first) // 2).astype(F32)
    omega = jnp.exp(-math.log(ROPE_THETA) * 2.0 * index / width)
    ids = id_rows.astype(F32)[:, :, None]
    chosen = jnp.where(lane < 16, ids[0], jnp.where(lane < 72, ids[1], ids[2]))
    angle = chosen * omega
    sign = jnp.where(lane % 2 == 0, -1.0, 1.0)
    return jnp.cos(angle), jnp.sin(angle) * sign


def whole(shape):
    return pl.BlockSpec(shape, lambda *_: (0,) * len(shape))


SMEM = pl.BlockSpec(memory_space=pltpu.SMEM)


def cost(flops, moved, exps=0):
    return pl.CostEstimate(flops=int(flops), bytes_accessed=int(moved), transcendentals=int(exps))


def flatten_kernel(parts_ref, out_ref):
    for i in range(64):
        row = parts_ref[4 * i : 4 * i + 1, :]
        for j in range(1, 4):
            row = row + parts_ref[4 * i + j : 4 * i + j + 1, :]
        out_ref[:, 144 * i : 144 * i + 144] = row


def flattened(parts):
    return pl.pallas_call(
        flatten_kernel,
        out_shape=jax.ShapeDtypeStruct((1, 3 * D), F32),
        cost_estimate=cost(3 * D * 4, 300000),
        name="flatten_mod",
    )(parts)


def modulate_rows(at_ref, pieces, mod_ref, out_ref, begin, rows):
    here = pl.ds(begin, rows)
    values = [r[here, :].astype(F32) for r in pieces]
    mean = sum(jnp.sum(v, -1, keepdims=True) for v in values) / D
    values = [v - mean for v in values]
    spread = sum(jnp.sum(v * v, -1, keepdims=True) for v in values) / D
    scale = lax.rsqrt(spread + EPS)
    for r, v in enumerate(values):
        lanes = pl.ds(pl.multiple_of(at_ref[3 + r], WID), WID)
        gains = pl.ds(pl.multiple_of(at_ref[3 + r] + D, WID), WID)
        out_ref[here, lanes] = (
            (1.0 + mod_ref[:, gains]) * (v * scale) + mod_ref[:, lanes]
        ).astype(BF16)


def modulate_kernel(at_ref, own_ref, oc_ref, far_ref, foc_ref, mod_ref, out_ref):
    pieces = (own_ref, oc_ref, far_ref, foc_ref)

    @pl.loop(0, 6)
    def _(i):
        modulate_rows(at_ref, pieces, mod_ref, out_ref, pl.multiple_of(i * 48, 48), 48)


VMEM = pl.BlockSpec(memory_space=pltpu.VMEM)


def project_kernel(
    at_ref, own_ref, oc_ref, far_ref, foc_ref, mod_ref, w_ref, gain_ref, cos_ref, sin_ref,
    low_ref, high_ref, keep_ref, give_ref, mine_ref, lent_ref, modded_ref,
):
    kind = pl.program_id(0)

    @pl.when(kind == 0)
    def _():
        modulate_kernel(at_ref, own_ref, oc_ref, far_ref, foc_ref, mod_ref, modded_ref)
        low_ref[...] = modded_ref[:HALF]
        high_ref[...] = modded_ref[HALF:]

    high = at_ref[2] == 1
    even = lax.broadcasted_iota(jnp.int32, (TOK, HD), 1) % 2 == 0
    heads = jnp.dot(modded_ref[...], w_ref[...], preferred_element_type=F32)
    heads = [heads[:, h * HD : h * HD + HD] for h in range(3)]

    def turned():
        out = []
        for h, x in enumerate(heads):
            x = x * lax.rsqrt(jnp.mean(x * x, -1, keepdims=True) + EPS)
            x = x * gain_ref[h : h + 1, :]
            swapped = jnp.where(even, pltpu.roll(x, HD - 1, 1), pltpu.roll(x, 1, 1))
            out.append((x * cos_ref[...] + swapped * sin_ref[...]).astype(BF16))
        return out

    def dealt(three):
        mine = jnp.where(high, three[2].astype(F32), three[0].astype(F32)).astype(BF16)
        other = jnp.where(high, three[0].astype(F32), three[2].astype(F32)).astype(BF16)
        return mine, three[1], other

    @pl.when(kind == 0)
    def _():
        mine_ref[0], mine_ref[1], lent_ref[...] = dealt(turned())

    @pl.when(kind == 1)
    def _():
        keep_ref[0], shared, give_ref[0] = dealt(turned())
        keep_ref[1] = shared
        give_ref[1] = shared

    @pl.when(kind == 2)
    def _():
        keep_ref[2], shared, give_ref[2] = dealt([h.astype(BF16) for h in heads])
        keep_ref[3] = shared
        give_ref[3] = shared


def projected(at, pieces, mod, w_kinds, gains, cosine, sine):
    def out(n):
        return jax.ShapeDtypeStruct((n, TOK, HD), BF16)

    return pl.pallas_call(
        project_kernel,
        grid=(3,),
        in_specs=[SMEM]
        + [VMEM] * 5
        + [
            pl.BlockSpec((None, D, 3 * HD), lambda k: (k, 0, 0)),
            pl.BlockSpec((None, 3, HD), lambda k: (jnp.minimum(k, 1), 0, 0)),
            VMEM,
            VMEM,
        ],
        out_specs=(
            whole((HALF, D)),
            whole((HALF, D)),
            whole((4, TOK, HD)),
            whole((4, TOK, HD)),
            whole((2, TOK, HD)),
            whole((TOK, HD)),
        ),
        out_shape=(
            jax.ShapeDtypeStruct((HALF, D), BF16),
            jax.ShapeDtypeStruct((HALF, D), BF16),
            out(4),
            out(4),
            out(2),
            jax.ShapeDtypeStruct((TOK, HD), BF16),
        ),
        scratch_shapes=[pltpu.VMEM((TOK, D), BF16)],
        cost_estimate=cost(2 * TOK * D * 9 * HD, 11e6),
        name="project",
    )(at, *pieces, mod, w_kinds, gains, cosine, sine)


def assemble_kernel(at_ref, *refs):
    z = at_ref[7]
    turns = (0, 7, 1, 6, 2, 5, 3, 4, 4)
    for k, by in enumerate(turns):
        maker = lax.rem(z + by, 8)
        offset = pl.multiple_of(lax.rem(maker, 4) * 96 + (48 if k == 8 else 0), 16)
        rows = pl.ds(offset, refs[k].shape[0])
        for side, out_ref in enumerate(refs[9:]):

            @pl.when(maker // 4 == side)
            def _():
                out_ref[rows, :] = refs[k][...]


def assembled(at, parts):
    return pl.pallas_call(
        assemble_kernel,
        in_specs=[SMEM] + [VMEM] * 9,
        out_shape=[jax.ShapeDtypeStruct((WID // 2, 2 * WID), BF16)] * 2,
        cost_estimate=cost(1e5, 5e6),
        name="assemble",
    )(at, *parts)


def gathered_rows(halves, rows_ref):
    for i in range(2):

        @pl.when(pl.program_id(0) == i)
        def _():
            rows_ref[:HALF] = halves[2 * i][...]
            rows_ref[HALF:] = halves[2 * i + 1][...]


def hidden_part(at_ref, rows_ref, j, halves):
    x = lax.rem(at_ref[8] + j, 4)
    total = None
    for n, w_ref in enumerate(halves):
        wide = w_ref.shape[0]
        lanes = pl.ds(pl.multiple_of(x * WID + n * wide, wide), wide)
        part = jnp.dot(rows_ref[:, lanes], w_ref[...], preferred_element_type=F32)
        total = part if total is None else total + part
    return total


def early_kernel(at_ref, *refs):
    rows_ref = refs[-1]
    gathered_rows(refs[:4], rows_ref)
    total = hidden_part(at_ref, rows_ref, 0, refs[4:6])
    total = total + hidden_part(at_ref, rows_ref, 1, refs[6:8])
    refs[-2][...] = total + hidden_part(at_ref, rows_ref, 3, refs[8:10])


def late_kernel(at_ref, pre_ref, *refs):
    same_ref, cross_ref, rows_ref = refs[-3:]
    gathered_rows(refs[:4], rows_ref)
    total = pre_ref[...] + hidden_part(at_ref, rows_ref, 2, refs[4:6])
    cubic = total + 0.044715 * (total * total * total)
    hidden = total * (0.5 + 0.5 * jnp.tanh(math.sqrt(2.0 / math.pi) * cubic))
    hidden = hidden.astype(BF16)
    for j, halves in ((0, refs[6:8]), (1, refs[8:10]), (2, refs[10:12]), (3, refs[12:14])):
        begin = 0
        for w_ref in halves:
            down = lax.dot_general(
                hidden, w_ref[...], (((1,), (1,)), ((), ())), preferred_element_type=F32
            )
            spot = at_ref[9 + j]
            for core, out_ref in enumerate((same_ref, cross_ref)):

                @pl.when(lax.rem(spot, 2) == core)
                def _():
                    out_ref[spot // 2, :, begin : begin + down.shape[1]] = down.astype(BF16)

            begin += down.shape[1]


def mlp(at, halves, w0, w1, w2, w3):
    half = WID // 2

    def left(rows=half):
        return pl.BlockSpec((rows, WID), lambda i: (0, 0))

    def right(rows=half):
        return pl.BlockSpec((rows, WID), lambda i: (0, 1))

    part = pl.BlockSpec((None, TOK, WID), lambda i: (i, 0, 0))
    scratch = [pltpu.VMEM((TOK, D), BF16)]
    pre = pl.pallas_call(
        early_kernel,
        grid=(2,),
        in_specs=[SMEM] + [VMEM] * 4 + [left()] * 6,
        out_specs=part,
        out_shape=jax.ShapeDtypeStruct((2, TOK, WID), F32),
        scratch_shapes=scratch,
        cost_estimate=cost(6 * 2 * TOK * WID * WID, 9e6),
        name="mlp_early",
    )(at, *halves, *w0, *w1, *w3)
    return pl.pallas_call(
        late_kernel,
        grid=(2,),
        in_specs=[SMEM, part] + [VMEM] * 4 + [left()] * 2 + [right()] * 8,
        out_specs=[pl.BlockSpec((2, None, TOK, WID), lambda i: (0, i, 0, 0))] * 2,
        out_shape=[jax.ShapeDtypeStruct((2, 2, TOK, WID), BF16)] * 2,
        scratch_shapes=scratch,
        cost_estimate=cost(10 * 2 * TOK * WID * WID, 16e6),
        name="mlp_late",
    )(at, pre, *halves, *w2, *w0, *w1, *w2, *w3)


def add_kernel(same_ref, crossed_ref, *outs):
    for i in range(4):
        total = same_ref[i // 2, i % 2].astype(F32) + crossed_ref[i // 2, i % 2].astype(F32)
        outs[i][...] = total.astype(BF16)


def added(same, crossed):
    rows = TOK // 3
    both = pl.BlockSpec((2, 2, rows, WID), lambda i: (0, 0, i, 0))
    return pl.pallas_call(
        add_kernel,
        grid=(3,),
        in_specs=[both, both],
        out_specs=[pl.BlockSpec((rows, WID), lambda i: (i, 0))] * 4,
        out_shape=[jax.ShapeDtypeStruct((TOK, WID), BF16)] * 4,
        cost_estimate=cost(4 * TOK * WID, 6e6),
        name="add_cores",
    )(same, crossed)


def attend_kernel(first, last, makers, *refs):
    count = len(makers)
    at_ref, own_ref, taken_ref = refs[:3]
    kv = refs[3 : 3 + 2 * count]
    rest = refs[3 + 2 * count :]
    if not first:
        stat_in, acc_in = rest[:2]
        rest = rest[2:]
    taken = jnp.full((TOK, HD), pl.program_id(0), jnp.int32) == 1
    queries = jnp.where(taken, taken_ref[...].astype(F32), own_ref[...].astype(F32)).astype(BF16)
    keys = jnp.concatenate([r[...] for r in kv[:count]], axis=0)
    values = jnp.concatenate([r[...] for r in kv[count:]], axis=0)
    token = lax.broadcasted_iota(jnp.int32, (1, count * TOK), 1)
    place = jnp.zeros((1, count * TOK), jnp.int32)
    for n, (by, side) in enumerate(makers):
        row = at_ref[2] if side == 0 else 1 - at_ref[2]
        start = (row * 8 + lax.rem(at_ref[7] + by, 8) - n) * TOK
        place = jnp.where(token >= n * TOK, token + start, place)
    live = (place >= TXT) | (place < at_ref[13])
    bias = jnp.where(live, 0.0, MASKED).astype(F32)
    scores = lax.dot_general(
        queries, keys, (((1,), (1,)), ((), ())), preferred_element_type=F32
    )
    scores = scores + bias
    peak = jnp.max(scores, axis=1, keepdims=True)
    if not first:
        peak = jnp.maximum(peak, stat_in[:, 0:1])
    weights = jnp.exp2((scores - peak) * EXP2_SCALE)
    total = jnp.sum(weights, axis=1, keepdims=True)
    acc = jnp.dot(weights.astype(BF16), values, preferred_element_type=F32)
    if not first:
        fade = jnp.exp2((stat_in[:, 0:1] - peak) * EXP2_SCALE)
        total = total + fade * stat_in[:, 64:65]
        acc = acc + fade * acc_in[...]
    if last:
        out_ref, lent_ref, top_ref = rest
        done = (acc / total).astype(BF16)

        @pl.when(pl.program_id(0) != 1)
        def _():
            out_ref[pl.program_id(0) // 2] = done

        @pl.when(pl.program_id(0) == 1)
        def _():
            lent_ref[...] = done

        top_ref[...] = jnp.broadcast_to(jnp.max(peak, axis=0, keepdims=True) * SCORE_SCALE, (8, HD))
    else:
        stat_ref, acc_ref = rest
        lane = lax.broadcasted_iota(jnp.int32, (TOK, HD), 1)
        stat_ref[...] = jnp.where(lane < 64, peak, total)
        acc_ref[...] = acc


def attended_more(at, own_q, taken_q, makers, keys, values, carry, last):
    count = len(makers)
    first = carry is None
    unit = pl.BlockSpec((None, TOK, HD), lambda u: (u, 0, 0))
    shared = pl.BlockSpec((None, TOK, HD), lambda u: (u // 2, 0, 0))
    later = pl.BlockSpec((None, TOK, HD), lambda u: (2 + u // 2, 0, 0))
    specs = [SMEM, shared, whole((TOK, HD))] + [shared] * count
    specs += [later] * count
    args = [at, own_q, taken_q, *keys, *values]
    if not first:
        specs += [unit, unit]
        args += list(carry)
    state = jax.ShapeDtypeStruct((3, TOK, HD), F32)
    if last:
        outs = (
            jax.ShapeDtypeStruct((2, TOK, HD), BF16),
            jax.ShapeDtypeStruct((TOK, HD), BF16),
            jax.ShapeDtypeStruct((3, 8, HD), F32),
        )
        out_specs = (
            whole((2, TOK, HD)),
            whole((TOK, HD)),
            pl.BlockSpec((None, 8, HD), lambda u: (u, 0, 0)),
        )
    else:
        outs, out_specs = (state, state), (unit, unit)
    width = count * TOK
    return pl.pallas_call(
        functools.partial(attend_kernel, first, last, makers),
        grid=(3,),
        in_specs=specs,
        out_specs=out_specs,
        out_shape=outs,
        cost_estimate=cost(3 * TOK * width * HD * 4, 4e6, 3 * TOK * width),
        name="attend",
    )(*args)


def finish_kernel(*refs):
    state_ref, gate_ref, wf_ref, top_ref = refs[:4]
    parts = refs[4:8]
    heads = refs[8:12]
    wout = refs[12:16]
    new_ref, stat_ref = refs[16:]
    update = parts[0][...].astype(F32)
    for r in parts[1:]:
        update = update + r[...].astype(F32)
    for h, w in zip(heads, wout):
        update = update + jnp.dot(h[...], w[...], preferred_element_type=F32)
    new = (state_ref[...].astype(F32) + gate_ref[...] * update).astype(BF16)
    new_ref[...] = new
    wide = new.astype(F32)
    squares = jnp.sum(wide * wide, axis=1, keepdims=True)
    lane = lax.broadcasted_iota(jnp.int32, (TOK, HD), 1)
    stats = jnp.dot(new, wf_ref[...], preferred_element_type=F32)
    stats = jnp.where(lane == 65, squares, stats)
    total = jnp.sum(squares, axis=0, keepdims=True)
    ones = jnp.ones((16, WID), BF16)
    extra = jnp.dot(ones, wf_ref[...], preferred_element_type=F32)[:8]
    lane8 = lax.broadcasted_iota(jnp.int32, (8, HD), 1)
    top = jnp.max(top_ref[...], axis=0)
    extra = jnp.where(lane8 == 66, total, jnp.where(lane8 == 67, top, extra))
    for h in range(8):
        half = h // 4
        stat_ref[h, :HALF, :] = stats[half * HALF : (half + 1) * HALF]
        stat_ref[h, HALF:, :] = extra


def finished(state, gate, wf, top, parts, heads, wout):
    return pl.pallas_call(
        finish_kernel,
        out_shape=(
            jax.ShapeDtypeStruct((TOK, WID), BF16),
            jax.ShapeDtypeStruct((8, HALF + 8, HD), F32),
        ),
        cost_estimate=cost(2 * TOK * 1536 * WID, 6e6),
        name="finish",
    )(state, gate, wf, top, *parts, *heads, *wout)


def sums_kernel(got_ref, sums_ref):
    total, top = got_ref[0, HALF : HALF + 1, :], got_ref[0, HALF : HALF + 1, :]
    for i in range(1, 8):
        total = total + got_ref[i, HALF : HALF + 1, :]
        top = jnp.maximum(top, got_ref[i, HALF : HALF + 1, :])
    lane = lax.broadcasted_iota(jnp.int32, (1, HD), 1)
    row = jnp.where(lane == 67, top, total)
    for i in range(32):
        sums_ref[i] = row


def latent_kernel(guide_ref, got_ref, latent_ref, next_ref):
    def velocity(h):
        total = got_ref[4 * h] + got_ref[4 * h + 1] + got_ref[4 * h + 2] + got_ref[4 * h + 3]
        mean = total[:HALF, 64:65] / D
        spread = total[:HALF, 65:66] / D - mean * mean
        product = total[:HALF, :64] - mean * total[HALF : HALF + 1, :64]
        return product * lax.rsqrt(spread + EPS)

    cond, uncond = velocity(0), velocity(1)
    step, scale = guide_ref[0], guide_ref[1]
    next_ref[...] = latent_ref[...] + step * (uncond + scale * (cond - uncond))


def block_sums(got):
    return pl.pallas_call(
        sums_kernel,
        in_specs=[pl.BlockSpec((8, HALF + 8, HD), lambda *_: (0, 0, 0))],
        out_shape=jax.ShapeDtypeStruct((32, 1, HD), F32),
        cost_estimate=cost(1e4, 7e5),
        name="block_sums",
    )(got)


def next_latents(guide, got, latent):
    return pl.pallas_call(
        latent_kernel,
        in_specs=[SMEM, whole(got.shape), whole(latent.shape)],
        out_specs=whole(latent.shape),
        out_shape=jax.ShapeDtypeStruct(latent.shape, F32),
        cost_estimate=cost(4e5, 7e5),
        name="next_latent",
    )(guide, got, latent)


def body(
    state,
    latent,
    w_mod,
    w_qkv,
    w_mlp_in,
    q_gain,
    k_gain,
    w_out,
    w_mlp_down,
    w_final,
    text_len,
    rope_ids,
    guidance,
    step_index,
):
    xh, xl, z, yl, yh, core = (lax.axis_index(a) for a in ALL)
    tp = 2 * yh + core
    x = 2 * xh + xl
    blocks = [(tp ^ r) * WID for r in range(4)]
    owners = [((x + j) % 4) ^ tp for j in range(4)]
    flat_len = text_len.reshape(2 * REQ)
    own_len = jnp.sum(
        jnp.where(jnp.arange(2 * REQ, dtype=jnp.int32) == xh * 2 + yl, flat_len, 0)
    )
    at = jnp.stack([yh, core, xl, *blocks, z, x, *owners, own_len]).astype(jnp.int32)

    both = jnp.stack([w_mlp_in, w_mlp_down])
    keep = lax.dynamic_slice_in_dim(both, yl * WID, WID, 2)
    give = lax.dynamic_slice_in_dim(both, (1 - yl) * WID, WID, 2)
    taken = flip(give, "yl", 1)
    low = jnp.where(yl == 0, keep, taken)
    high = jnp.where(yl == 0, taken, keep)
    rows96 = jnp.concatenate([low, high], axis=1)
    rows96 = jnp.concatenate([rows96[0], rows96[1]], axis=1)
    w_up1 = turn(rows96, "z", 1)
    w_dn1 = turn(rows96, "z", -1)
    w_up2 = turn(rows96, "z", 2)
    w_dn2 = turn(rows96, "z", -2)
    w_up3 = turn(w_up2, "z", 1)
    w_dn3 = turn(w_dn2, "z", -1)
    w_up4 = turn(w_up2[:48], "z", 2)
    w_dn4 = turn(w_dn2[48:], "z", -2)
    w_parts = [rows96, w_up1, w_dn1, w_up2, w_dn2, w_up3, w_dn3, w_up4, w_dn4]
    w_low, w_high = assembled(at, w_parts)
    before_low = turn(w_low, X, 1)
    after_high = turn(w_high, X, -1)
    before_high = turn(w_high, X, 1)
    after_low = turn(w_low, X, -1)
    far_low = turn(before_low, X, 1)
    far_high = turn(after_high, X, -1)

    s_oc = flip(state, "c", 1)
    s_far = flip(state, "yh", 1)
    s_foc = flip(s_far, "c", 1)

    sigma_now = sigma_of(step_index)
    step_size = sigma_of(step_index + 1) - sigma_now
    time_rows = jax.nn.silu(time_embedding(sigma_now, tp * WID, WID)).astype(BF16)
    partial_mod = jnp.dot(time_rows, w_mod, preferred_element_type=F32)
    sent = jnp.repeat(partial_mod, 128, axis=0)[:, None, :]
    got = exchange(sent, ALL)
    mod = flattened(got.reshape(256, 144))
    gate = lax.dynamic_slice_in_dim(mod, 2 * D + tp * WID, WID, 1)

    cosine, sine = rope_tables(rope_ids)
    w_kinds = w_qkv.transpose(1, 0, 2)
    gains = jnp.stack([q_gain, k_gain])
    pieces = (state, s_oc, s_far, s_foc)
    mine_low, mine_high, own_kv, give_kv, own_q, give_q = projected(
        at, pieces, mod, w_kinds, gains, cosine, sine
    )
    taken_kv = flip(give_kv, "xl", 1)
    taken_q = flip(give_q, "xl", 1)
    other_low = flip(mine_low, "yl", 1)
    other_high = flip(mine_high, YY, 3)

    ups, dns, seen, makers = [own_kv, taken_kv], [own_kv, taken_kv], [own_kv, taken_kv], [(0, 0), (0, 1)]
    carry = None
    for k in range(1, 4):
        for side in range(2):
            ups[side] = turn(ups[side], "z", 1)
            dns[side] = turn(dns[side], "z", -1)
        seen = seen + ups + dns
        makers = makers + [(8 - k, 0), (8 - k, 1), (k, 0), (k, 1)]
        if k != 2:
            carry = attended_more(at, own_q, taken_q, tuple(makers), seen, seen, carry, False)
            seen, makers = [], []
    ends = [turn(ups[0], "z", 1), turn(dns[1], "z", -1)]
    out, lent, top = attended_more(at, own_q, taken_q, ((4, 0), (4, 1)), ends, ends, carry, True)

    halves = (mine_low, mine_high, other_low, other_high)
    same, cross = mlp(
        at, halves, (w_low, w_high), (after_low, after_high), (far_low, far_high), (before_low, before_high)
    )
    crossed = flip(cross, "c", 1)
    near_own, near_yl, away_own, away_yl = added(same, crossed)
    part_yl = flip(near_yl, "yl", 1)
    part_far = flip(away_own, "yh", 1)
    part_both = flip(away_yl, YY, 3)

    def wout_for(r):
        return lax.dynamic_slice_in_dim(w_out, (tp ^ r) * WID, WID, 1)

    wout = [
        wout_for(0), flip(wout_for(1), "c", 1), flip(wout_for(2), "yh", 1), flip(wout_for(3), TP, 3)
    ]
    returned = flip(lent, "xl", 1)
    low_head = jnp.where(xl == 0, out[0], returned)
    high_head = jnp.where(xl == 0, returned, out[0])
    heads = jnp.concatenate([low_head, out[1], high_head], axis=1)
    h_oc = flip(heads, "c", 1)
    h_far = flip(heads, "yh", 1)
    h_foc = flip(h_far, "c", 1)

    wf = jnp.concatenate(
        [w_final, jnp.ones((WID, 1), BF16), jnp.zeros((WID, HD - 65), BF16)], axis=1
    )
    parts = (near_own, part_yl, part_far, part_both)
    new_state, stats = finished(state, gate, wf, top, parts, (heads, h_oc, h_far, h_foc), wout)

    got_rows = exchange(stats, Y8)
    request_pick = jnp.arange(REQ, dtype=jnp.int32) == xh
    guide_scale = jnp.sum(jnp.where(request_pick, guidance, 0)).astype(F32) / 2.0
    own_step = jnp.sum(jnp.where(request_pick, step_size, 0.0))
    guide = jnp.stack([own_step, guide_scale])
    every = exchange(block_sums(got_rows), XZ)
    next_latent = next_latents(guide, got_rows, latent)
    every = every.reshape(2, 16, HD)
    state_norm = jnp.sqrt(jnp.sum(every[:, :, 66], axis=1) / (2.0 * SEQ_LEN * D))
    top_score = jnp.max(every[:, :, 67], axis=1)
    return (new_state, next_latent, state_norm, top_score)


def solution(mesh):
    split = Mesh(mesh.devices.reshape(2, 2, 8, 2, 2, 2), ALL)
    return jax.shard_map(
        body,
        mesh=split,
        in_specs=(
            P(SEQ, TP),
            P(SEQ, None),
            P(TP, SEQ),
            P(None, None, TP),
            P(SEQ, TP),
            P(TP, None),
            P(TP, None),
            P(TP, None),
            P(SEQ, TP),
            P(TP, None),
            P(),
            P(None, SEQ),
            P(),
            P(),
        ),
        out_specs=(P(SEQ, TP), P(SEQ, None), P(), P()),
        check_vma=False,
    )
```

```python
import functools
import math

import jax
import jax.numpy as jnp
from jax import lax
from jax.experimental import pallas as pl
from jax.experimental.pallas import tpu as pltpu
from jax.sharding import Mesh
from jax.sharding import PartitionSpec as P


D = 3072
HD = 128
REQ = 2
TOK = 288
HALF = 144
TXT = 512
STEPS = 28
WID = 768
SEQ_LEN = 4608
TIME_SHIFT = 1.15
ROPE_THETA = 10000.0
EPS = 1e-06
MASKED = -1e30
ALL = ("xh", "xl", "z", "yl", "yh", "c")
SEQ = ("xh", "xl", "z", "yl")
XZ = ("xh", "xl", "z")
TP = ("yh", "c")
Y8 = ("yl", "yh", "c")
X = ("xh", "xl")
YY = ("yl", "yh")
F32 = jnp.float32
BF16 = jnp.bfloat16
EXP2_SCALE = math.log2(math.e) / math.sqrt(HD)
SCORE_SCALE = 1.0 / math.sqrt(HD)


def flip(value, axis, bits):
    return lax.ppermute(value, axis, [(i, i ^ bits) for i in range(lax.axis_size(axis))])


def turn(value, axis, by):
    count = lax.axis_size(axis)
    return lax.ppermute(value, axis, [(i, (i + by) % count) for i in range(count)])


def exchange(value, axis):
    return lax.all_to_all(value, axis, 0, 0, tiled=True)


def sigma_of(step_count):
    fraction = 1.0 - step_count.astype(F32) / STEPS
    boosted = math.exp(TIME_SHIFT) * fraction
    return boosted / (boosted + 1.0 - fraction)


def time_embedding(sigma_vals, start, width):
    half_width = D // 2
    entry = start + jnp.arange(width, dtype=jnp.int32)
    in_cos = entry < half_width
    index = jnp.where(in_cos, entry, entry - half_width).astype(F32)
    frequency = jnp.exp(-math.log(10000.0) * index / half_width)
    phases = 1000.0 * sigma_vals[:, None] * frequency[None, :]
    return jnp.where(in_cos[None, :], jnp.cos(phases), jnp.sin(phases))


def rope_tables(id_rows):
    lane = jnp.arange(HD, dtype=jnp.int32)
    width = jnp.where(lane < 16, 16.0, 56.0).astype(F32)
    first = jnp.where(lane < 16, 0, jnp.where(lane < 72, 16, 72))
    index = ((lane - first) // 2).astype(F32)
    omega = jnp.exp(-math.log(ROPE_THETA) * 2.0 * index / width)
    ids = id_rows.astype(F32)[:, :, None]
    chosen = jnp.where(lane < 16, ids[0], jnp.where(lane < 72, ids[1], ids[2]))
    angle = chosen * omega
    sign = jnp.where(lane % 2 == 0, -1.0, 1.0)
    return jnp.cos(angle), jnp.sin(angle) * sign


def whole(shape):
    return pl.BlockSpec(shape, lambda *_: (0,) * len(shape))


SMEM = pl.BlockSpec(memory_space=pltpu.SMEM)


def cost(flops, moved, exps=0):
    return pl.CostEstimate(flops=int(flops), bytes_accessed=int(moved), transcendentals=int(exps))


def flatten_kernel(parts_ref, out_ref):
    for i in range(64):
        row = parts_ref[4 * i : 4 * i + 1, :]
        for j in range(1, 4):
            row = row + parts_ref[4 * i + j : 4 * i + j + 1, :]
        out_ref[:, 144 * i : 144 * i + 144] = row


def flattened(parts):
    return pl.pallas_call(
        flatten_kernel,
        out_shape=jax.ShapeDtypeStruct((1, 3 * D), F32),
        cost_estimate=cost(3 * D * 4, 300000),
        name="flatten_mod",
    )(parts)


def modulate_rows(at_ref, pieces, mod_ref, out_ref, begin, rows):
    here = pl.ds(begin, rows)
    values = [r[here, :].astype(F32) for r in pieces]
    mean = sum(jnp.sum(v, -1, keepdims=True) for v in values) / D
    values = [v - mean for v in values]
    spread = sum(jnp.sum(v * v, -1, keepdims=True) for v in values) / D
    scale = lax.rsqrt(spread + EPS)
    for r, v in enumerate(values):
        lanes = pl.ds(pl.multiple_of(at_ref[3 + r], WID), WID)
        gains = pl.ds(pl.multiple_of(at_ref[3 + r] + D, WID), WID)
        out_ref[here, lanes] = (
            (1.0 + mod_ref[:, gains]) * (v * scale) + mod_ref[:, lanes]
        ).astype(BF16)


def modulate_kernel(at_ref, own_ref, oc_ref, far_ref, foc_ref, mod_ref, out_ref):
    pieces = (own_ref, oc_ref, far_ref, foc_ref)

    @pl.loop(0, 6)
    def _(i):
        modulate_rows(at_ref, pieces, mod_ref, out_ref, pl.multiple_of(i * 48, 48), 48)


VMEM = pl.BlockSpec(memory_space=pltpu.VMEM)


def project_kernel(
    at_ref, own_ref, oc_ref, far_ref, foc_ref, mod_ref, w_ref, gain_ref, cos_ref, sin_ref,
    low_ref, high_ref, keep_ref, give_ref, mine_ref, lent_ref, modded_ref,
):
    kind = pl.program_id(0)

    @pl.when(kind == 0)
    def _():
        modulate_kernel(at_ref, own_ref, oc_ref, far_ref, foc_ref, mod_ref, modded_ref)
        low_ref[...] = modded_ref[:HALF]
        high_ref[...] = modded_ref[HALF:]

    high = at_ref[2] == 1
    even = lax.broadcasted_iota(jnp.int32, (TOK, HD), 1) % 2 == 0
    heads = jnp.dot(modded_ref[...], w_ref[...], preferred_element_type=F32)
    heads = [heads[:, h * HD : h * HD + HD] for h in range(3)]

    def turned():
        out = []
        for h, x in enumerate(heads):
            x = x * lax.rsqrt(jnp.mean(x * x, -1, keepdims=True) + EPS)
            x = x * gain_ref[h : h + 1, :]
            swapped = jnp.where(even, pltpu.roll(x, HD - 1, 1), pltpu.roll(x, 1, 1))
            out.append((x * cos_ref[...] + swapped * sin_ref[...]).astype(BF16))
        return out

    def dealt(three):
        mine = jnp.where(high, three[2].astype(F32), three[0].astype(F32)).astype(BF16)
        other = jnp.where(high, three[0].astype(F32), three[2].astype(F32)).astype(BF16)
        return mine, three[1], other

    @pl.when(kind == 0)
    def _():
        mine_ref[0], mine_ref[1], lent_ref[...] = dealt(turned())

    @pl.when(kind == 1)
    def _():
        keep_ref[0], shared, give_ref[0] = dealt(turned())
        keep_ref[1] = shared
        give_ref[1] = shared

    @pl.when(kind == 2)
    def _():
        keep_ref[2], shared, give_ref[2] = dealt([h.astype(BF16) for h in heads])
        keep_ref[3] = shared
        give_ref[3] = shared


def projected(at, pieces, mod, w_kinds, gains, cosine, sine):
    def out(n):
        return jax.ShapeDtypeStruct((n, TOK, HD), BF16)

    return pl.pallas_call(
        project_kernel,
        grid=(3,),
        in_specs=[SMEM]
        + [VMEM] * 5
        + [
            pl.BlockSpec((None, D, 3 * HD), lambda k: (k, 0, 0)),
            pl.BlockSpec((None, 3, HD), lambda k: (jnp.minimum(k, 1), 0, 0)),
            VMEM,
            VMEM,
        ],
        out_specs=(
            whole((HALF, D)),
            whole((HALF, D)),
            whole((4, TOK, HD)),
            whole((4, TOK, HD)),
            whole((2, TOK, HD)),
            whole((TOK, HD)),
        ),
        out_shape=(
            jax.ShapeDtypeStruct((HALF, D), BF16),
            jax.ShapeDtypeStruct((HALF, D), BF16),
            out(4),
            out(4),
            out(2),
            jax.ShapeDtypeStruct((TOK, HD), BF16),
        ),
        scratch_shapes=[pltpu.VMEM((TOK, D), BF16)],
        cost_estimate=cost(2 * TOK * D * 9 * HD, 11e6),
        name="project",
    )(at, *pieces, mod, w_kinds, gains, cosine, sine)


def assemble_kernel(at_ref, *refs):
    z = at_ref[7]
    turns = (0, 7, 1, 6, 2, 5, 3, 4, 4)
    for k, by in enumerate(turns):
        begin = lax.rem(z + by, 8) * 96 + (48 if k == 8 else 0)
        rows = pl.ds(pl.multiple_of(begin, 16), refs[k].shape[0])
        refs[9][rows, :] = refs[k][:, :WID]
        refs[10][rows, :] = refs[k][:, WID:]


def assembled(at, parts):
    return pl.pallas_call(
        assemble_kernel,
        in_specs=[SMEM] + [VMEM] * 9,
        out_shape=[jax.ShapeDtypeStruct((WID, WID), BF16)] * 2,
        cost_estimate=cost(1e5, 5e6),
        name="assemble",
    )(at, *parts)


def gathered_rows(halves, rows_ref):
    for i in range(2):

        @pl.when(pl.program_id(0) == i)
        def _():
            rows_ref[:HALF] = halves[2 * i][...]
            rows_ref[HALF:] = halves[2 * i + 1][...]


def hidden_part(at_ref, rows_ref, j, halves):
    x = lax.rem(at_ref[8] + j, 4)
    total = None
    for n, w_ref in enumerate(halves):
        wide = w_ref.shape[0]
        lanes = pl.ds(pl.multiple_of(x * WID + n * wide, wide), wide)
        part = jnp.dot(rows_ref[:, lanes], w_ref[...], preferred_element_type=F32)
        total = part if total is None else total + part
    return total


def hidden_kernel(at_ref, *refs):
    out_ref, rows_ref = refs[-2:]
    gathered_rows(refs[:4], rows_ref)
    total = hidden_part(at_ref, rows_ref, 0, refs[4:5])
    total = total + hidden_part(at_ref, rows_ref, 1, refs[5:6])
    total = total + hidden_part(at_ref, rows_ref, 2, refs[6:8])
    total = total + hidden_part(at_ref, rows_ref, 3, refs[8:9])
    cubic = total + 0.044715 * (total * total * total)
    hidden = total * (0.5 + 0.5 * jnp.tanh(math.sqrt(2.0 / math.pi) * cubic))
    out_ref[...] = hidden.astype(BF16)


def down_kernel(at_ref, hidden_ref, *refs):
    out_ref = refs[-1]
    for j, halves in ((0, refs[:1]), (1, refs[1:2]), (2, refs[2:4]), (3, refs[4:5])):
        begin, spot = 0, at_ref[9 + j]
        for w_ref in halves:
            down = lax.dot_general(
                hidden_ref[...], w_ref[...], (((1,), (1,)), ((), ())), preferred_element_type=F32
            )
            lanes = slice(begin, begin + down.shape[1])
            out_ref[lax.rem(spot, 2), spot // 2, :, lanes] = down.astype(BF16)
            begin += down.shape[1]


def hidden_units(at, halves, w0, w1, w2, w3):
    return pl.pallas_call(
        hidden_kernel,
        grid=(2,),
        in_specs=[SMEM] + [VMEM] * 9,
        out_specs=pl.BlockSpec((None, TOK, WID), lambda i: (i, 0, 0)),
        out_shape=jax.ShapeDtypeStruct((2, TOK, WID), BF16),
        scratch_shapes=[pltpu.VMEM((TOK, D), BF16)],
        cost_estimate=cost(8 * 2 * TOK * WID * WID, 9e6),
        name="mlp_hidden",
    )(at, *halves, w0, w1, *w2, w3)


def down_products(at, hidden, w0, w1, w2, w3):
    return pl.pallas_call(
        down_kernel,
        grid=(2,),
        in_specs=[SMEM, pl.BlockSpec((None, TOK, WID), lambda i: (i, 0, 0))] + [VMEM] * 5,
        out_specs=pl.BlockSpec((2, 2, None, TOK, WID), lambda i: (0, 0, i, 0, 0)),
        out_shape=jax.ShapeDtypeStruct((2, 2, 2, TOK, WID), BF16),
        cost_estimate=cost(8 * 2 * TOK * WID * WID, 9e6),
        name="mlp_down",
    )(at, hidden, w0, w1, *w2, w3)


def add_kernel(same_ref, crossed_ref, *outs):
    for i in range(4):
        total = same_ref[i // 2, i % 2].astype(F32) + crossed_ref[i // 2, i % 2].astype(F32)
        outs[i][...] = total.astype(BF16)


def added(same, crossed):
    rows = TOK // 3
    both = pl.BlockSpec((2, 2, rows, WID), lambda i: (0, 0, i, 0))
    near = pl.BlockSpec((None, 2, 2, rows, WID), lambda i: (0, 0, 0, i, 0))
    return pl.pallas_call(
        add_kernel,
        grid=(3,),
        in_specs=[near, both],
        out_specs=[pl.BlockSpec((rows, WID), lambda i: (i, 0))] * 4,
        out_shape=[jax.ShapeDtypeStruct((TOK, WID), BF16)] * 4,
        cost_estimate=cost(4 * TOK * WID, 6e6),
        name="add_cores",
    )(same, crossed)


def attend_kernel(first, last, makers, *refs):
    count = len(makers)
    at_ref, own_ref, taken_ref = refs[:3]
    kv = refs[3 : 3 + 2 * count]
    rest = refs[3 + 2 * count :]
    if not first:
        stat_in, acc_in = rest[:2]
        rest = rest[2:]
    taken = jnp.full((TOK, HD), pl.program_id(0), jnp.int32) == 1
    queries = jnp.where(taken, taken_ref[...].astype(F32), own_ref[...].astype(F32)).astype(BF16)
    keys = jnp.concatenate([r[...] for r in kv[:count]], axis=0)
    values = jnp.concatenate([r[...] for r in kv[count:]], axis=0)
    token = lax.broadcasted_iota(jnp.int32, (1, count * TOK), 1)
    place = jnp.zeros((1, count * TOK), jnp.int32)
    for n, (by, side) in enumerate(makers):
        row = at_ref[2] if side == 0 else 1 - at_ref[2]
        start = (row * 8 + lax.rem(at_ref[7] + by, 8) - n) * TOK
        place = jnp.where(token >= n * TOK, token + start, place)
    live = (place >= TXT) | (place < at_ref[13])
    bias = jnp.where(live, 0.0, MASKED).astype(F32)
    scores = lax.dot_general(
        queries, keys, (((1,), (1,)), ((), ())), preferred_element_type=F32
    )
    scores = scores + bias
    peak = jnp.max(scores, axis=1, keepdims=True)
    if not first:
        peak = jnp.maximum(peak, stat_in[:, 0:1])
    weights = jnp.exp2((scores - peak) * EXP2_SCALE)
    total = jnp.sum(weights, axis=1, keepdims=True)
    acc = jnp.dot(weights.astype(BF16), values, preferred_element_type=F32)
    if not first:
        fade = jnp.exp2((stat_in[:, 0:1] - peak) * EXP2_SCALE)
        total = total + fade * stat_in[:, 64:65]
        acc = acc + fade * acc_in[...]
    if last:
        out_ref, lent_ref, top_ref = rest
        done = (acc / total).astype(BF16)

        @pl.when(pl.program_id(0) != 1)
        def _():
            out_ref[pl.program_id(0) // 2] = done

        @pl.when(pl.program_id(0) == 1)
        def _():
            lent_ref[...] = done

        top_ref[...] = jnp.broadcast_to(jnp.max(peak, axis=0, keepdims=True) * SCORE_SCALE, (8, HD))
    else:
        stat_ref, acc_ref = rest
        lane = lax.broadcasted_iota(jnp.int32, (TOK, HD), 1)
        stat_ref[...] = jnp.where(lane < 64, peak, total)
        acc_ref[...] = acc


def attended_more(at, own_q, taken_q, makers, keys, values, carry, last):
    count = len(makers)
    first = carry is None
    unit = pl.BlockSpec((None, TOK, HD), lambda u: (u, 0, 0))
    shared = pl.BlockSpec((None, TOK, HD), lambda u: (u // 2, 0, 0))
    later = pl.BlockSpec((None, TOK, HD), lambda u: (2 + u // 2, 0, 0))
    specs = [SMEM, shared, whole((TOK, HD))] + [shared] * count
    specs += [later] * count
    args = [at, own_q, taken_q, *keys, *values]
    if not first:
        specs += [unit, unit]
        args += list(carry)
    state = jax.ShapeDtypeStruct((3, TOK, HD), F32)
    if last:
        outs = (
            jax.ShapeDtypeStruct((2, TOK, HD), BF16),
            jax.ShapeDtypeStruct((TOK, HD), BF16),
            jax.ShapeDtypeStruct((3, 8, HD), F32),
        )
        out_specs = (
            whole((2, TOK, HD)),
            whole((TOK, HD)),
            pl.BlockSpec((None, 8, HD), lambda u: (u, 0, 0)),
        )
    else:
        outs, out_specs = (state, state), (unit, unit)
    width = count * TOK
    return pl.pallas_call(
        functools.partial(attend_kernel, first, last, makers),
        grid=(3,),
        in_specs=specs,
        out_specs=out_specs,
        out_shape=outs,
        cost_estimate=cost(3 * TOK * width * HD * 4, 4e6, 3 * TOK * width),
        name="attend",
    )(*args)


def finish_kernel(*refs):
    state_ref, gate_ref, wf_ref, top_ref = refs[:4]
    parts = refs[4:8]
    heads = refs[8:12]
    wout = refs[12:16]
    new_ref, stat_ref = refs[16:]
    update = parts[0][...].astype(F32)
    for r in parts[1:]:
        update = update + r[...].astype(F32)
    for h, w in zip(heads, wout):
        update = update + jnp.dot(h[...], w[...], preferred_element_type=F32)
    new = (state_ref[...].astype(F32) + gate_ref[...] * update).astype(BF16)
    new_ref[...] = new
    wide = new.astype(F32)
    squares = jnp.sum(wide * wide, axis=1, keepdims=True)
    lane = lax.broadcasted_iota(jnp.int32, (TOK, HD), 1)
    stats = jnp.dot(new, wf_ref[...], preferred_element_type=F32)
    stats = jnp.where(lane == 65, squares, stats)
    total = jnp.sum(squares, axis=0, keepdims=True)
    ones = jnp.ones((16, WID), BF16)
    extra = jnp.dot(ones, wf_ref[...], preferred_element_type=F32)[:8]
    lane8 = lax.broadcasted_iota(jnp.int32, (8, HD), 1)
    top = jnp.max(top_ref[...], axis=0)
    extra = jnp.where(lane8 == 66, total, jnp.where(lane8 == 67, top, extra))
    for h in range(8):
        half = h // 4
        stat_ref[h, :HALF, :] = stats[half * HALF : (half + 1) * HALF]
        stat_ref[h, HALF:, :] = extra


def finished(state, gate, wf, top, parts, heads, wout):
    return pl.pallas_call(
        finish_kernel,
        out_shape=(
            jax.ShapeDtypeStruct((TOK, WID), BF16),
            jax.ShapeDtypeStruct((8, HALF + 8, HD), F32),
        ),
        cost_estimate=cost(2 * TOK * 1536 * WID, 6e6),
        name="finish",
    )(state, gate, wf, top, *parts, *heads, *wout)


def sums_kernel(got_ref, sums_ref):
    total, top = got_ref[0, HALF : HALF + 1, :], got_ref[0, HALF : HALF + 1, :]
    for i in range(1, 8):
        total = total + got_ref[i, HALF : HALF + 1, :]
        top = jnp.maximum(top, got_ref[i, HALF : HALF + 1, :])
    lane = lax.broadcasted_iota(jnp.int32, (1, HD), 1)
    row = jnp.where(lane == 67, top, total)
    for i in range(32):
        sums_ref[i] = row


def latent_kernel(guide_ref, got_ref, latent_ref, next_ref):
    def velocity(h):
        total = got_ref[4 * h] + got_ref[4 * h + 1] + got_ref[4 * h + 2] + got_ref[4 * h + 3]
        mean = total[:HALF, 64:65] / D
        spread = total[:HALF, 65:66] / D - mean * mean
        product = total[:HALF, :64] - mean * total[HALF : HALF + 1, :64]
        return product * lax.rsqrt(spread + EPS)

    cond, uncond = velocity(0), velocity(1)
    step, scale = guide_ref[0], guide_ref[1]
    next_ref[...] = latent_ref[...] + step * (uncond + scale * (cond - uncond))


def block_sums(got):
    return pl.pallas_call(
        sums_kernel,
        in_specs=[pl.BlockSpec((8, HALF + 8, HD), lambda *_: (0, 0, 0))],
        out_shape=jax.ShapeDtypeStruct((32, 1, HD), F32),
        cost_estimate=cost(1e4, 7e5),
        name="block_sums",
    )(got)


def next_latents(guide, got, latent):
    return pl.pallas_call(
        latent_kernel,
        in_specs=[SMEM, whole(got.shape), whole(latent.shape)],
        out_specs=whole(latent.shape),
        out_shape=jax.ShapeDtypeStruct(latent.shape, F32),
        cost_estimate=cost(4e5, 7e5),
        name="next_latent",
    )(guide, got, latent)


def body(
    state,
    latent,
    w_mod,
    w_qkv,
    w_mlp_in,
    q_gain,
    k_gain,
    w_out,
    w_mlp_down,
    w_final,
    text_len,
    rope_ids,
    guidance,
    step_index,
):
    xh, xl, z, yl, yh, core = (lax.axis_index(a) for a in ALL)
    tp = 2 * yh + core
    x = 2 * xh + xl
    blocks = [(tp ^ r) * WID for r in range(4)]
    owners = [((x + j) % 4) ^ tp for j in range(4)]
    flat_len = text_len.reshape(2 * REQ)
    own_len = jnp.sum(
        jnp.where(jnp.arange(2 * REQ, dtype=jnp.int32) == xh * 2 + yl, flat_len, 0)
    )
    at = jnp.stack([yh, core, xl, *blocks, z, x, *owners, own_len]).astype(jnp.int32)

    both = jnp.stack([w_mlp_in, w_mlp_down])
    keep = lax.dynamic_slice_in_dim(both, yl * WID, WID, 2)
    give = lax.dynamic_slice_in_dim(both, (1 - yl) * WID, WID, 2)
    taken = flip(give, "yl", 1)
    low = jnp.where(yl == 0, keep, taken)
    high = jnp.where(yl == 0, taken, keep)
    rows96 = jnp.concatenate([low, high], axis=1)
    rows96 = jnp.concatenate([rows96[0], rows96[1]], axis=1)
    w_up1 = turn(rows96, "z", 1)
    w_dn1 = turn(rows96, "z", -1)
    w_up2 = turn(rows96, "z", 2)
    w_dn2 = turn(rows96, "z", -2)
    w_up3 = turn(w_up2, "z", 1)
    w_dn3 = turn(w_dn2, "z", -1)
    w_up4 = turn(w_up2[:48], "z", 2)
    w_dn4 = turn(w_dn2[48:], "z", -2)
    w_parts = [rows96, w_up1, w_dn1, w_up2, w_dn2, w_up3, w_dn3, w_up4, w_dn4]
    half = WID // 2
    in_here, down_here = assembled(at, w_parts)
    in_before = turn(in_here, X, 1)
    in_after = turn(in_here, X, -1)
    in_far = (turn(in_before[:half], X, 1), turn(in_after[half:], X, -1))
    down_before = turn(down_here, X, 1)
    down_after = turn(down_here, X, -1)
    down_far = (turn(down_before[:half], X, 1), turn(down_after[half:], X, -1))

    s_oc = flip(state, "c", 1)
    s_far = flip(state, "yh", 1)
    s_foc = flip(s_far, "c", 1)

    sigma_now = sigma_of(step_index)
    step_size = sigma_of(step_index + 1) - sigma_now
    time_rows = jax.nn.silu(time_embedding(sigma_now, tp * WID, WID)).astype(BF16)
    partial_mod = jnp.dot(time_rows, w_mod, preferred_element_type=F32)
    sent = jnp.repeat(partial_mod, 128, axis=0)[:, None, :]
    got = exchange(sent, ALL)
    mod = flattened(got.reshape(256, 144))
    gate = lax.dynamic_slice_in_dim(mod, 2 * D + tp * WID, WID, 1)

    cosine, sine = rope_tables(rope_ids)
    w_kinds = w_qkv.transpose(1, 0, 2)
    gains = jnp.stack([q_gain, k_gain])
    pieces = (state, s_oc, s_far, s_foc)
    mine_low, mine_high, own_kv, give_kv, own_q, give_q = projected(
        at, pieces, mod, w_kinds, gains, cosine, sine
    )
    taken_kv = flip(give_kv, "xl", 1)
    taken_q = flip(give_q, "xl", 1)
    other_low = flip(mine_low, "yl", 1)
    other_high = flip(mine_high, YY, 3)

    ups, dns, seen, makers = [own_kv, taken_kv], [own_kv, taken_kv], [own_kv, taken_kv], [(0, 0), (0, 1)]
    carry = None
    for k in range(1, 4):
        for side in range(2):
            ups[side] = turn(ups[side], "z", 1)
            dns[side] = turn(dns[side], "z", -1)
        seen = seen + ups + dns
        makers = makers + [(8 - k, 0), (8 - k, 1), (k, 0), (k, 1)]
        if k != 2:
            carry = attended_more(at, own_q, taken_q, tuple(makers), seen, seen, carry, False)
            seen, makers = [], []
    ends = [turn(ups[0], "z", 1), turn(dns[1], "z", -1)]
    out, lent, top = attended_more(at, own_q, taken_q, ((4, 0), (4, 1)), ends, ends, carry, True)

    halves = (mine_low, mine_high, other_low, other_high)
    hidden = hidden_units(at, halves, in_here, in_after, in_far, in_before)
    products = down_products(at, hidden, down_here, down_after, down_far, down_before)
    crossed = flip(products[1], "c", 1)
    near_own, near_yl, away_own, away_yl = added(products, crossed)
    part_yl = flip(near_yl, "yl", 1)
    part_far = flip(away_own, "yh", 1)
    part_both = flip(away_yl, YY, 3)

    def wout_for(r):
        return lax.dynamic_slice_in_dim(w_out, (tp ^ r) * WID, WID, 1)

    wout = [
        wout_for(0), flip(wout_for(1), "c", 1), flip(wout_for(2), "yh", 1), flip(wout_for(3), TP, 3)
    ]
    returned = flip(lent, "xl", 1)
    low_head = jnp.where(xl == 0, out[0], returned)
    high_head = jnp.where(xl == 0, returned, out[0])
    heads = jnp.concatenate([low_head, out[1], high_head], axis=1)
    h_oc = flip(heads, "c", 1)
    h_far = flip(heads, "yh", 1)
    h_foc = flip(h_far, "c", 1)

    wf = jnp.concatenate(
        [w_final, jnp.ones((WID, 1), BF16), jnp.zeros((WID, HD - 65), BF16)], axis=1
    )
    parts = (near_own, part_yl, part_far, part_both)
    new_state, stats = finished(state, gate, wf, top, parts, (heads, h_oc, h_far, h_foc), wout)

    got_rows = exchange(stats, Y8)
    request_pick = jnp.arange(REQ, dtype=jnp.int32) == xh
    guide_scale = jnp.sum(jnp.where(request_pick, guidance, 0)).astype(F32) / 2.0
    own_step = jnp.sum(jnp.where(request_pick, step_size, 0.0))
    guide = jnp.stack([own_step, guide_scale])
    every = exchange(block_sums(got_rows), XZ)
    next_latent = next_latents(guide, got_rows, latent)
    every = every.reshape(2, 16, HD)
    state_norm = jnp.sqrt(jnp.sum(every[:, :, 66], axis=1) / (2.0 * SEQ_LEN * D))
    top_score = jnp.max(every[:, :, 67], axis=1)
    return (new_state, next_latent, state_norm, top_score)


def solution(mesh):
    split = Mesh(mesh.devices.reshape(2, 2, 8, 2, 2, 2), ALL)
    return jax.shard_map(
        body,
        mesh=split,
        in_specs=(
            P(SEQ, TP),
            P(SEQ, None),
            P(TP, SEQ),
            P(None, None, TP),
            P(SEQ, TP),
            P(TP, None),
            P(TP, None),
            P(TP, None),
            P(SEQ, TP),
            P(TP, None),
            P(),
            P(None, SEQ),
            P(),
            P(),
        ),
        out_specs=(P(SEQ, TP), P(SEQ, None), P(), P()),
        check_vma=False,
    )
```

```python
import functools
import math

import jax
import jax.numpy as jnp
from jax import lax
from jax.experimental import pallas as pl
from jax.experimental.pallas import tpu as pltpu
from jax.sharding import Mesh
from jax.sharding import PartitionSpec as P


D = 3072
HD = 128
REQ = 2
TOK = 288
HALF = 144
TXT = 512
STEPS = 28
WID = 768
SEQ_LEN = 4608
TIME_SHIFT = 1.15
ROPE_THETA = 10000.0
EPS = 1e-06
MASKED = -1e30
ALL = ("xh", "xl", "z", "yl", "yh", "c")
SEQ = ("xh", "xl", "z", "yl")
XZ = ("xh", "xl", "z")
TP = ("yh", "c")
Y8 = ("yl", "yh", "c")
X = ("xh", "xl")
YY = ("yl", "yh")
F32 = jnp.float32
BF16 = jnp.bfloat16
EXP2_SCALE = math.log2(math.e) / math.sqrt(HD)
SCORE_SCALE = 1.0 / math.sqrt(HD)


def flip(value, axis, bits):
    return lax.ppermute(value, axis, [(i, i ^ bits) for i in range(lax.axis_size(axis))])


def turn(value, axis, by):
    count = lax.axis_size(axis)
    return lax.ppermute(value, axis, [(i, (i + by) % count) for i in range(count)])


def exchange(value, axis):
    return lax.all_to_all(value, axis, 0, 0, tiled=True)


def sigma_of(step_count):
    fraction = 1.0 - step_count.astype(F32) / STEPS
    boosted = math.exp(TIME_SHIFT) * fraction
    return boosted / (boosted + 1.0 - fraction)


def time_embedding(sigma_vals, start, width):
    half_width = D // 2
    entry = start + jnp.arange(width, dtype=jnp.int32)
    in_cos = entry < half_width
    index = jnp.where(in_cos, entry, entry - half_width).astype(F32)
    frequency = jnp.exp(-math.log(10000.0) * index / half_width)
    phases = 1000.0 * sigma_vals[:, None] * frequency[None, :]
    return jnp.where(in_cos[None, :], jnp.cos(phases), jnp.sin(phases))


def rope_tables(id_rows):
    lane = jnp.arange(HD, dtype=jnp.int32)
    width = jnp.where(lane < 16, 16.0, 56.0).astype(F32)
    first = jnp.where(lane < 16, 0, jnp.where(lane < 72, 16, 72))
    index = ((lane - first) // 2).astype(F32)
    omega = jnp.exp(-math.log(ROPE_THETA) * 2.0 * index / width)
    ids = id_rows.astype(F32)[:, :, None]
    chosen = jnp.where(lane < 16, ids[0], jnp.where(lane < 72, ids[1], ids[2]))
    angle = chosen * omega
    sign = jnp.where(lane % 2 == 0, -1.0, 1.0)
    return jnp.cos(angle), jnp.sin(angle) * sign


def whole(shape):
    return pl.BlockSpec(shape, lambda *_: (0,) * len(shape))


SMEM = pl.BlockSpec(memory_space=pltpu.SMEM)


def cost(flops, moved, exps=0):
    return pl.CostEstimate(flops=int(flops), bytes_accessed=int(moved), transcendentals=int(exps))


def flatten_kernel(parts_ref, out_ref):
    for i in range(64):
        row = parts_ref[4 * i : 4 * i + 1, :]
        for j in range(1, 4):
            row = row + parts_ref[4 * i + j : 4 * i + j + 1, :]
        out_ref[:, 144 * i : 144 * i + 144] = row


def flattened(parts):
    return pl.pallas_call(
        flatten_kernel,
        out_shape=jax.ShapeDtypeStruct((1, 3 * D), F32),
        cost_estimate=cost(3 * D * 4, 300000),
        name="flatten_mod",
    )(parts)


def modulate_rows(at_ref, pieces, mod_ref, out_ref, begin, rows):
    here = pl.ds(begin, rows)
    values = [r[here, :].astype(F32) for r in pieces]
    mean = sum(jnp.sum(v, -1, keepdims=True) for v in values) / D
    values = [v - mean for v in values]
    spread = sum(jnp.sum(v * v, -1, keepdims=True) for v in values) / D
    scale = lax.rsqrt(spread + EPS)
    for r, v in enumerate(values):
        lanes = pl.ds(pl.multiple_of(at_ref[3 + r], WID), WID)
        gains = pl.ds(pl.multiple_of(at_ref[3 + r] + D, WID), WID)
        out_ref[here, lanes] = (
            (1.0 + mod_ref[:, gains]) * (v * scale) + mod_ref[:, lanes]
        ).astype(BF16)


def modulate_kernel(at_ref, own_ref, oc_ref, far_ref, foc_ref, mod_ref, out_ref):
    pieces = (own_ref, oc_ref, far_ref, foc_ref)

    @pl.loop(0, 6)
    def _(i):
        modulate_rows(at_ref, pieces, mod_ref, out_ref, pl.multiple_of(i * 48, 48), 48)


VMEM = pl.BlockSpec(memory_space=pltpu.VMEM)


def project_kernel(
    at_ref, own_ref, oc_ref, far_ref, foc_ref, mod_ref, w_ref, gain_ref, cos_ref, sin_ref,
    low_ref, high_ref, keep_ref, give_ref, mine_ref, lent_ref, modded_ref,
):
    kind = pl.program_id(0)

    @pl.when(kind == 0)
    def _():
        modulate_kernel(at_ref, own_ref, oc_ref, far_ref, foc_ref, mod_ref, modded_ref)
        low_ref[...] = modded_ref[:HALF]
        high_ref[...] = modded_ref[HALF:]

    high = at_ref[2] == 1
    even = lax.broadcasted_iota(jnp.int32, (TOK, HD), 1) % 2 == 0
    heads = jnp.dot(modded_ref[...], w_ref[...], preferred_element_type=F32)
    heads = [heads[:, h * HD : h * HD + HD] for h in range(3)]

    def turned():
        out = []
        for h, x in enumerate(heads):
            x = x * lax.rsqrt(jnp.mean(x * x, -1, keepdims=True) + EPS)
            x = x * gain_ref[h : h + 1, :]
            swapped = jnp.where(even, pltpu.roll(x, HD - 1, 1), pltpu.roll(x, 1, 1))
            out.append((x * cos_ref[...] + swapped * sin_ref[...]).astype(BF16))
        return out

    def dealt(three):
        mine = jnp.where(high, three[2].astype(F32), three[0].astype(F32)).astype(BF16)
        other = jnp.where(high, three[0].astype(F32), three[2].astype(F32)).astype(BF16)
        return mine, three[1], other

    @pl.when(kind == 0)
    def _():
        mine_ref[0], mine_ref[1], lent_ref[...] = dealt(turned())

    @pl.when(kind == 1)
    def _():
        keep_ref[0], shared, give_ref[0] = dealt(turned())
        keep_ref[1] = shared
        give_ref[1] = shared

    @pl.when(kind == 2)
    def _():
        keep_ref[2], shared, give_ref[2] = dealt([h.astype(BF16) for h in heads])
        keep_ref[3] = shared
        give_ref[3] = shared


def projected(at, pieces, mod, w_kinds, gains, cosine, sine):
    def out(n):
        return jax.ShapeDtypeStruct((n, TOK, HD), BF16)

    return pl.pallas_call(
        project_kernel,
        grid=(3,),
        in_specs=[SMEM]
        + [VMEM] * 5
        + [
            pl.BlockSpec((None, D, 3 * HD), lambda k: (k, 0, 0)),
            pl.BlockSpec((None, 3, HD), lambda k: (jnp.minimum(k, 1), 0, 0)),
            VMEM,
            VMEM,
        ],
        out_specs=(
            whole((HALF, D)),
            whole((HALF, D)),
            whole((4, TOK, HD)),
            whole((4, TOK, HD)),
            whole((2, TOK, HD)),
            whole((TOK, HD)),
        ),
        out_shape=(
            jax.ShapeDtypeStruct((HALF, D), BF16),
            jax.ShapeDtypeStruct((HALF, D), BF16),
            out(4),
            out(4),
            out(2),
            jax.ShapeDtypeStruct((TOK, HD), BF16),
        ),
        scratch_shapes=[pltpu.VMEM((TOK, D), BF16)],
        cost_estimate=cost(2 * TOK * D * 9 * HD, 11e6),
        name="project",
    )(at, *pieces, mod, w_kinds, gains, cosine, sine)


def assemble_kernel(at_ref, *refs):
    z = at_ref[7]
    turns = (0, 7, 1, 6, 2, 5, 3, 4, 4)
    for k, by in enumerate(turns):
        begin = lax.rem(z + by, 8) * 96 + (48 if k == 8 else 0)
        rows = pl.ds(pl.multiple_of(begin, 16), refs[k].shape[0])
        refs[9][rows, :] = refs[k][:, :WID]
        refs[10][rows, :] = refs[k][:, WID:]


def assembled(at, parts):
    return pl.pallas_call(
        assemble_kernel,
        in_specs=[SMEM] + [VMEM] * 9,
        out_shape=[jax.ShapeDtypeStruct((WID, WID), BF16)] * 2,
        cost_estimate=cost(1e5, 5e6),
        name="assemble",
    )(at, *parts)


def gathered_rows(halves, rows_ref):
    for i in range(2):

        @pl.when(pl.program_id(0) == i)
        def _():
            rows_ref[:HALF] = halves[2 * i][...]
            rows_ref[HALF:] = halves[2 * i + 1][...]


def hidden_part(at_ref, rows_ref, j, w_ref):
    x = lax.rem(at_ref[8] + j, 4)
    lanes = pl.ds(pl.multiple_of(x * WID, WID), WID)
    return jnp.dot(rows_ref[:, lanes], w_ref[...], preferred_element_type=F32)


def hidden_kernel(at_ref, *refs):
    out_ref, rows_ref = refs[-2:]
    gathered_rows(refs[:4], rows_ref)
    total = hidden_part(at_ref, rows_ref, 0, refs[4])
    for j in range(1, 4):
        total = total + hidden_part(at_ref, rows_ref, j, refs[4 + j])
    cubic = total + 0.044715 * (total * total * total)
    hidden = total * (0.5 + 0.5 * jnp.tanh(math.sqrt(2.0 / math.pi) * cubic))
    out_ref[...] = hidden.astype(BF16)


def down_kernel(at_ref, hidden_ref, *refs):
    out_ref = refs[-1]
    for j in range(4):
        spot = at_ref[9 + j]
        down = lax.dot_general(
            hidden_ref[...], refs[j][...], (((1,), (1,)), ((), ())), preferred_element_type=F32
        )
        out_ref[lax.rem(spot, 2), spot // 2] = down.astype(BF16)


def hidden_units(at, halves, w0, w1, w2, w3):
    return pl.pallas_call(
        hidden_kernel,
        grid=(2,),
        in_specs=[SMEM] + [VMEM] * 8,
        out_specs=pl.BlockSpec((None, TOK, WID), lambda i: (i, 0, 0)),
        out_shape=jax.ShapeDtypeStruct((2, TOK, WID), BF16),
        scratch_shapes=[pltpu.VMEM((TOK, D), BF16)],
        cost_estimate=cost(8 * 2 * TOK * WID * WID, 9e6),
        name="mlp_hidden",
    )(at, *halves, w0, w1, w2, w3)


def down_products(at, hidden, w0, w1, w2, w3):
    return pl.pallas_call(
        down_kernel,
        grid=(2,),
        in_specs=[SMEM, pl.BlockSpec((None, TOK, WID), lambda i: (i, 0, 0))] + [VMEM] * 4,
        out_specs=pl.BlockSpec((2, 2, None, TOK, WID), lambda i: (0, 0, i, 0, 0)),
        out_shape=jax.ShapeDtypeStruct((2, 2, 2, TOK, WID), BF16),
        cost_estimate=cost(8 * 2 * TOK * WID * WID, 9e6),
        name="mlp_down",
    )(at, hidden, w0, w1, w2, w3)


def add_kernel(same_ref, crossed_ref, *outs):
    for i in range(4):
        total = same_ref[i // 2, i % 2].astype(F32) + crossed_ref[i // 2, i % 2].astype(F32)
        outs[i][...] = total.astype(BF16)


def added(same, crossed):
    rows = TOK // 3
    both = pl.BlockSpec((2, 2, rows, WID), lambda i: (0, 0, i, 0))
    near = pl.BlockSpec((None, 2, 2, rows, WID), lambda i: (0, 0, 0, i, 0))
    return pl.pallas_call(
        add_kernel,
        grid=(3,),
        in_specs=[near, both],
        out_specs=[pl.BlockSpec((rows, WID), lambda i: (i, 0))] * 4,
        out_shape=[jax.ShapeDtypeStruct((TOK, WID), BF16)] * 4,
        cost_estimate=cost(4 * TOK * WID, 6e6),
        name="add_cores",
    )(same, crossed)


def attend_kernel(first, last, makers, *refs):
    count = len(makers)
    at_ref, own_ref, taken_ref = refs[:3]
    kv = refs[3 : 3 + 2 * count]
    rest = refs[3 + 2 * count :]
    if not first:
        stat_in, acc_in = rest[:2]
        rest = rest[2:]
    taken = jnp.full((TOK, HD), pl.program_id(0), jnp.int32) == 1
    queries = jnp.where(taken, taken_ref[...].astype(F32), own_ref[...].astype(F32)).astype(BF16)
    keys = jnp.concatenate([r[...] for r in kv[:count]], axis=0)
    values = jnp.concatenate([r[...] for r in kv[count:]], axis=0)
    token = lax.broadcasted_iota(jnp.int32, (1, count * TOK), 1)
    place = jnp.zeros((1, count * TOK), jnp.int32)
    for n, (by, side) in enumerate(makers):
        row = at_ref[2] if side == 0 else 1 - at_ref[2]
        start = (row * 8 + lax.rem(at_ref[7] + by, 8) - n) * TOK
        place = jnp.where(token >= n * TOK, token + start, place)
    live = (place >= TXT) | (place < at_ref[13])
    bias = jnp.where(live, 0.0, MASKED).astype(F32)
    scores = lax.dot_general(
        queries, keys, (((1,), (1,)), ((), ())), preferred_element_type=F32
    )
    scores = scores + bias
    peak = jnp.max(scores, axis=1, keepdims=True)
    if not first:
        peak = jnp.maximum(peak, stat_in[:, 0:1])
    weights = jnp.exp2((scores - peak) * EXP2_SCALE)
    total = jnp.sum(weights, axis=1, keepdims=True)
    acc = jnp.dot(weights.astype(BF16), values, preferred_element_type=F32)
    if not first:
        fade = jnp.exp2((stat_in[:, 0:1] - peak) * EXP2_SCALE)
        total = total + fade * stat_in[:, 64:65]
        acc = acc + fade * acc_in[...]
    if last:
        out_ref, lent_ref, top_ref = rest
        done = (acc / total).astype(BF16)

        @pl.when(pl.program_id(0) != 1)
        def _():
            out_ref[pl.program_id(0) // 2] = done

        @pl.when(pl.program_id(0) == 1)
        def _():
            lent_ref[...] = done

        top_ref[...] = jnp.broadcast_to(jnp.max(peak, axis=0, keepdims=True) * SCORE_SCALE, (8, HD))
    else:
        stat_ref, acc_ref = rest
        lane = lax.broadcasted_iota(jnp.int32, (TOK, HD), 1)
        stat_ref[...] = jnp.where(lane < 64, peak, total)
        acc_ref[...] = acc


def attended_more(at, own_q, taken_q, makers, keys, values, carry, last):
    count = len(makers)
    first = carry is None
    unit = pl.BlockSpec((None, TOK, HD), lambda u: (u, 0, 0))
    shared = pl.BlockSpec((None, TOK, HD), lambda u: (u // 2, 0, 0))
    later = pl.BlockSpec((None, TOK, HD), lambda u: (2 + u // 2, 0, 0))
    specs = [SMEM, shared, whole((TOK, HD))] + [shared] * count
    specs += [later] * count
    args = [at, own_q, taken_q, *keys, *values]
    if not first:
        specs += [unit, unit]
        args += list(carry)
    state = jax.ShapeDtypeStruct((3, TOK, HD), F32)
    if last:
        outs = (
            jax.ShapeDtypeStruct((2, TOK, HD), BF16),
            jax.ShapeDtypeStruct((TOK, HD), BF16),
            jax.ShapeDtypeStruct((3, 8, HD), F32),
        )
        out_specs = (
            whole((2, TOK, HD)),
            whole((TOK, HD)),
            pl.BlockSpec((None, 8, HD), lambda u: (u, 0, 0)),
        )
    else:
        outs, out_specs = (state, state), (unit, unit)
    width = count * TOK
    return pl.pallas_call(
        functools.partial(attend_kernel, first, last, makers),
        grid=(3,),
        in_specs=specs,
        out_specs=out_specs,
        out_shape=outs,
        cost_estimate=cost(3 * TOK * width * HD * 4, 4e6, 3 * TOK * width),
        name="attend",
    )(*args)


def finish_kernel(*refs):
    state_ref, gate_ref, wf_ref, top_ref = refs[:4]
    parts = refs[4:8]
    heads = refs[8:12]
    wout = refs[12:16]
    new_ref, stat_ref = refs[16:]
    update = parts[0][...].astype(F32)
    for r in parts[1:]:
        update = update + r[...].astype(F32)
    for h, w in zip(heads, wout):
        update = update + jnp.dot(h[...], w[...], preferred_element_type=F32)
    new = (state_ref[...].astype(F32) + gate_ref[...] * update).astype(BF16)
    new_ref[...] = new
    wide = new.astype(F32)
    squares = jnp.sum(wide * wide, axis=1, keepdims=True)
    lane = lax.broadcasted_iota(jnp.int32, (TOK, HD), 1)
    stats = jnp.dot(new, wf_ref[...], preferred_element_type=F32)
    stats = jnp.where(lane == 65, squares, stats)
    total = jnp.sum(squares, axis=0, keepdims=True)
    ones = jnp.ones((16, WID), BF16)
    extra = jnp.dot(ones, wf_ref[...], preferred_element_type=F32)[:8]
    lane8 = lax.broadcasted_iota(jnp.int32, (8, HD), 1)
    top = jnp.max(top_ref[...], axis=0)
    extra = jnp.where(lane8 == 66, total, jnp.where(lane8 == 67, top, extra))
    for h in range(8):
        half = h // 4
        stat_ref[h, :HALF, :] = stats[half * HALF : (half + 1) * HALF]
        stat_ref[h, HALF:, :] = extra


def finished(state, gate, wf, top, parts, heads, wout):
    return pl.pallas_call(
        finish_kernel,
        out_shape=(
            jax.ShapeDtypeStruct((TOK, WID), BF16),
            jax.ShapeDtypeStruct((8, HALF + 8, HD), F32),
        ),
        cost_estimate=cost(2 * TOK * 1536 * WID, 6e6),
        name="finish",
    )(state, gate, wf, top, *parts, *heads, *wout)


def sums_kernel(got_ref, sums_ref):
    total, top = got_ref[0, HALF : HALF + 1, :], got_ref[0, HALF : HALF + 1, :]
    for i in range(1, 8):
        total = total + got_ref[i, HALF : HALF + 1, :]
        top = jnp.maximum(top, got_ref[i, HALF : HALF + 1, :])
    lane = lax.broadcasted_iota(jnp.int32, (1, HD), 1)
    row = jnp.where(lane == 67, top, total)
    for i in range(32):
        sums_ref[i] = row


def latent_kernel(guide_ref, got_ref, latent_ref, next_ref):
    def velocity(h):
        total = got_ref[4 * h] + got_ref[4 * h + 1] + got_ref[4 * h + 2] + got_ref[4 * h + 3]
        mean = total[:HALF, 64:65] / D
        spread = total[:HALF, 65:66] / D - mean * mean
        product = total[:HALF, :64] - mean * total[HALF : HALF + 1, :64]
        return product * lax.rsqrt(spread + EPS)

    cond, uncond = velocity(0), velocity(1)
    step, scale = guide_ref[0], guide_ref[1]
    next_ref[...] = latent_ref[...] + step * (uncond + scale * (cond - uncond))


def block_sums(got):
    return pl.pallas_call(
        sums_kernel,
        in_specs=[pl.BlockSpec((8, HALF + 8, HD), lambda *_: (0, 0, 0))],
        out_shape=jax.ShapeDtypeStruct((32, 1, HD), F32),
        cost_estimate=cost(1e4, 7e5),
        name="block_sums",
    )(got)


def next_latents(guide, got, latent):
    return pl.pallas_call(
        latent_kernel,
        in_specs=[SMEM, whole(got.shape), whole(latent.shape)],
        out_specs=whole(latent.shape),
        out_shape=jax.ShapeDtypeStruct(latent.shape, F32),
        cost_estimate=cost(4e5, 7e5),
        name="next_latent",
    )(guide, got, latent)


def body(
    state,
    latent,
    w_mod,
    w_qkv,
    w_mlp_in,
    q_gain,
    k_gain,
    w_out,
    w_mlp_down,
    w_final,
    text_len,
    rope_ids,
    guidance,
    step_index,
):
    xh, xl, z, yl, yh, core = (lax.axis_index(a) for a in ALL)
    tp = 2 * yh + core
    x = 2 * xh + xl
    blocks = [(tp ^ r) * WID for r in range(4)]
    owners = [((x + j) % 4) ^ tp for j in range(4)]
    flat_len = text_len.reshape(2 * REQ)
    own_len = jnp.sum(
        jnp.where(jnp.arange(2 * REQ, dtype=jnp.int32) == xh * 2 + yl, flat_len, 0)
    )
    at = jnp.stack([yh, core, xl, *blocks, z, x, *owners, own_len]).astype(jnp.int32)

    both = jnp.stack([w_mlp_in, w_mlp_down])
    keep = lax.dynamic_slice_in_dim(both, yl * WID, WID, 2)
    give = lax.dynamic_slice_in_dim(both, (1 - yl) * WID, WID, 2)
    taken = flip(give, "yl", 1)
    low = jnp.where(yl == 0, keep, taken)
    high = jnp.where(yl == 0, taken, keep)
    rows96 = jnp.concatenate([low, high], axis=1)
    rows96 = jnp.concatenate([rows96[0], rows96[1]], axis=1)
    w_up1 = turn(rows96, "z", 1)
    w_dn1 = turn(rows96, "z", -1)
    w_up2 = turn(rows96, "z", 2)
    w_dn2 = turn(rows96, "z", -2)
    w_up3 = turn(w_up2, "z", 1)
    w_dn3 = turn(w_dn2, "z", -1)
    w_up4 = turn(w_up2[:48], "z", 2)
    w_dn4 = turn(w_dn2[48:], "z", -2)
    w_parts = [rows96, w_up1, w_dn1, w_up2, w_dn2, w_up3, w_dn3, w_up4, w_dn4]
    in_here, down_here = assembled(at, w_parts)
    in_before = turn(in_here, X, 1)
    in_after = turn(in_here, X, -1)
    in_far = turn(in_before, X, 1)
    down_before = turn(down_here, X, 1)
    down_after = turn(down_here, X, -1)
    down_far = turn(down_after, X, -1)

    s_oc = flip(state, "c", 1)
    s_far = flip(state, "yh", 1)
    s_foc = flip(s_far, "c", 1)

    sigma_now = sigma_of(step_index)
    step_size = sigma_of(step_index + 1) - sigma_now
    time_rows = jax.nn.silu(time_embedding(sigma_now, tp * WID, WID)).astype(BF16)
    partial_mod = jnp.dot(time_rows, w_mod, preferred_element_type=F32)
    sent = jnp.repeat(partial_mod, 128, axis=0)[:, None, :]
    got = exchange(sent, ALL)
    mod = flattened(got.reshape(256, 144))
    gate = lax.dynamic_slice_in_dim(mod, 2 * D + tp * WID, WID, 1)

    cosine, sine = rope_tables(rope_ids)
    w_kinds = w_qkv.transpose(1, 0, 2)
    gains = jnp.stack([q_gain, k_gain])
    pieces = (state, s_oc, s_far, s_foc)
    mine_low, mine_high, own_kv, give_kv, own_q, give_q = projected(
        at, pieces, mod, w_kinds, gains, cosine, sine
    )
    taken_kv = flip(give_kv, "xl", 1)
    taken_q = flip(give_q, "xl", 1)
    other_low = flip(mine_low, "yl", 1)
    other_high = flip(mine_high, YY, 3)

    ups, dns, seen, makers = [own_kv, taken_kv], [own_kv, taken_kv], [own_kv, taken_kv], [(0, 0), (0, 1)]
    carry = None
    for k in range(1, 4):
        for side in range(2):
            ups[side] = turn(ups[side], "z", 1)
            dns[side] = turn(dns[side], "z", -1)
        seen = seen + ups + dns
        makers = makers + [(8 - k, 0), (8 - k, 1), (k, 0), (k, 1)]
        if k != 2:
            carry = attended_more(at, own_q, taken_q, tuple(makers), seen, seen, carry, False)
            seen, makers = [], []
    ends = [turn(ups[0], "z", 1), turn(dns[1], "z", -1)]
    out, lent, top = attended_more(at, own_q, taken_q, ((4, 0), (4, 1)), ends, ends, carry, True)

    halves = (mine_low, mine_high, other_low, other_high)
    hidden = hidden_units(at, halves, in_here, in_after, in_far, in_before)
    products = down_products(at, hidden, down_here, down_after, down_far, down_before)
    crossed = flip(products[1], "c", 1)
    near_own, near_yl, away_own, away_yl = added(products, crossed)
    part_yl = flip(near_yl, "yl", 1)
    part_far = flip(away_own, "yh", 1)
    part_both = flip(away_yl, YY, 3)

    def wout_for(r):
        return lax.dynamic_slice_in_dim(w_out, (tp ^ r) * WID, WID, 1)

    wout = [
        wout_for(0), flip(wout_for(1), "c", 1), flip(wout_for(2), "yh", 1), flip(wout_for(3), TP, 3)
    ]
    returned = flip(lent, "xl", 1)
    low_head = jnp.where(xl == 0, out[0], returned)
    high_head = jnp.where(xl == 0, returned, out[0])
    heads = jnp.concatenate([low_head, out[1], high_head], axis=1)
    h_oc = flip(heads, "c", 1)
    h_far = flip(heads, "yh", 1)
    h_foc = flip(h_far, "c", 1)

    wf = jnp.concatenate(
        [w_final, jnp.ones((WID, 1), BF16), jnp.zeros((WID, HD - 65), BF16)], axis=1
    )
    parts = (near_own, part_yl, part_far, part_both)
    new_state, stats = finished(state, gate, wf, top, parts, (heads, h_oc, h_far, h_foc), wout)

    got_rows = exchange(stats, Y8)
    request_pick = jnp.arange(REQ, dtype=jnp.int32) == xh
    guide_scale = jnp.sum(jnp.where(request_pick, guidance, 0)).astype(F32) / 2.0
    own_step = jnp.sum(jnp.where(request_pick, step_size, 0.0))
    guide = jnp.stack([own_step, guide_scale])
    every = exchange(block_sums(got_rows), XZ)
    next_latent = next_latents(guide, got_rows, latent)
    every = every.reshape(2, 16, HD)
    state_norm = jnp.sqrt(jnp.sum(every[:, :, 66], axis=1) / (2.0 * SEQ_LEN * D))
    top_score = jnp.max(every[:, :, 67], axis=1)
    return (new_state, next_latent, state_norm, top_score)


def solution(mesh):
    split = Mesh(mesh.devices.reshape(2, 2, 8, 2, 2, 2), ALL)
    return jax.shard_map(
        body,
        mesh=split,
        in_specs=(
            P(SEQ, TP),
            P(SEQ, None),
            P(TP, SEQ),
            P(None, None, TP),
            P(SEQ, TP),
            P(TP, None),
            P(TP, None),
            P(TP, None),
            P(SEQ, TP),
            P(TP, None),
            P(),
            P(None, SEQ),
            P(),
            P(),
        ),
        out_specs=(P(SEQ, TP), P(SEQ, None), P(), P()),
        check_vma=False,
    )
```

```python
import functools
import math

import jax
import jax.numpy as jnp
from jax import lax
from jax.experimental import pallas as pl
from jax.experimental.pallas import tpu as pltpu
from jax.sharding import Mesh
from jax.sharding import PartitionSpec as P


D = 3072
HD = 128
REQ = 2
TOK = 288
HALF = 144
TXT = 512
STEPS = 28
WID = 768
SEQ_LEN = 4608
TIME_SHIFT = 1.15
ROPE_THETA = 10000.0
EPS = 1e-06
MASKED = -1e30
ALL = ("xh", "xl", "z", "yl", "yh", "c")
SEQ = ("xh", "xl", "z", "yl")
XZ = ("xh", "xl", "z")
TP = ("yh", "c")
Y8 = ("yl", "yh", "c")
X = ("xh", "xl")
YY = ("yl", "yh")
F32 = jnp.float32
BF16 = jnp.bfloat16
EXP2_SCALE = math.log2(math.e) / math.sqrt(HD)
SCORE_SCALE = 1.0 / math.sqrt(HD)


def flip(value, axis, bits):
    return lax.ppermute(value, axis, [(i, i ^ bits) for i in range(lax.axis_size(axis))])


def turn(value, axis, by):
    count = lax.axis_size(axis)
    return lax.ppermute(value, axis, [(i, (i + by) % count) for i in range(count)])


def exchange(value, axis):
    return lax.all_to_all(value, axis, 0, 0, tiled=True)


def sigma_of(step_count):
    fraction = 1.0 - step_count.astype(F32) / STEPS
    boosted = math.exp(TIME_SHIFT) * fraction
    return boosted / (boosted + 1.0 - fraction)


def time_embedding(sigma_vals, start, width):
    half_width = D // 2
    entry = start + jnp.arange(width, dtype=jnp.int32)
    in_cos = entry < half_width
    index = jnp.where(in_cos, entry, entry - half_width).astype(F32)
    frequency = jnp.exp(-math.log(10000.0) * index / half_width)
    phases = 1000.0 * sigma_vals[:, None] * frequency[None, :]
    return jnp.where(in_cos[None, :], jnp.cos(phases), jnp.sin(phases))


def rope_tables(id_rows):
    lane = jnp.arange(HD, dtype=jnp.int32)
    width = jnp.where(lane < 16, 16.0, 56.0).astype(F32)
    first = jnp.where(lane < 16, 0, jnp.where(lane < 72, 16, 72))
    index = ((lane - first) // 2).astype(F32)
    omega = jnp.exp(-math.log(ROPE_THETA) * 2.0 * index / width)
    ids = id_rows.astype(F32)[:, :, None]
    chosen = jnp.where(lane < 16, ids[0], jnp.where(lane < 72, ids[1], ids[2]))
    angle = chosen * omega
    sign = jnp.where(lane % 2 == 0, -1.0, 1.0)
    return jnp.cos(angle), jnp.sin(angle) * sign


def whole(shape):
    return pl.BlockSpec(shape, lambda *_: (0,) * len(shape))


SMEM = pl.BlockSpec(memory_space=pltpu.SMEM)


def cost(flops, moved, exps=0):
    return pl.CostEstimate(flops=int(flops), bytes_accessed=int(moved), transcendentals=int(exps))


def flatten_kernel(parts_ref, out_ref):
    for i in range(64):
        row = parts_ref[4 * i : 4 * i + 1, :]
        for j in range(1, 4):
            row = row + parts_ref[4 * i + j : 4 * i + j + 1, :]
        out_ref[:, 144 * i : 144 * i + 144] = row


def flattened(parts):
    return pl.pallas_call(
        flatten_kernel,
        out_shape=jax.ShapeDtypeStruct((1, 3 * D), F32),
        cost_estimate=cost(3 * D * 4, 300000),
        name="flatten_mod",
    )(parts)


def modulate_rows(at_ref, pieces, mod_ref, out_ref, begin, rows):
    here = pl.ds(begin, rows)
    values = [r[here, :].astype(F32) for r in pieces]
    mean = sum(jnp.sum(v, -1, keepdims=True) for v in values) / D
    values = [v - mean for v in values]
    spread = sum(jnp.sum(v * v, -1, keepdims=True) for v in values) / D
    scale = lax.rsqrt(spread + EPS)
    for r, v in enumerate(values):
        lanes = pl.ds(pl.multiple_of(at_ref[3 + r], WID), WID)
        gains = pl.ds(pl.multiple_of(at_ref[3 + r] + D, WID), WID)
        out_ref[here, lanes] = (
            (1.0 + mod_ref[:, gains]) * (v * scale) + mod_ref[:, lanes]
        ).astype(BF16)


def modulate_kernel(at_ref, own_ref, oc_ref, far_ref, foc_ref, mod_ref, out_ref):
    pieces = (own_ref, oc_ref, far_ref, foc_ref)

    @pl.loop(0, 6)
    def _(i):
        modulate_rows(at_ref, pieces, mod_ref, out_ref, pl.multiple_of(i * 48, 48), 48)


VMEM = pl.BlockSpec(memory_space=pltpu.VMEM)


def project_kernel(
    at_ref, own_ref, oc_ref, far_ref, foc_ref, mod_ref, w_ref, gain_ref, cos_ref, sin_ref,
    low_ref, high_ref, keep_ref, give_ref, mine_ref, lent_ref, modded_ref,
):
    kind = pl.program_id(0)

    @pl.when(kind == 0)
    def _():
        modulate_kernel(at_ref, own_ref, oc_ref, far_ref, foc_ref, mod_ref, modded_ref)
        low_ref[...] = modded_ref[:HALF]
        high_ref[...] = modded_ref[HALF:]

    high = at_ref[2] == 1
    even = lax.broadcasted_iota(jnp.int32, (TOK, HD), 1) % 2 == 0
    heads = jnp.dot(modded_ref[...], w_ref[...], preferred_element_type=F32)
    heads = [heads[:, h * HD : h * HD + HD] for h in range(3)]

    def turned():
        out = []
        for h, x in enumerate(heads):
            x = x * lax.rsqrt(jnp.mean(x * x, -1, keepdims=True) + EPS)
            x = x * gain_ref[h : h + 1, :]
            swapped = jnp.where(even, pltpu.roll(x, HD - 1, 1), pltpu.roll(x, 1, 1))
            out.append((x * cos_ref[...] + swapped * sin_ref[...]).astype(BF16))
        return out

    def dealt(three):
        mine = jnp.where(high, three[2].astype(F32), three[0].astype(F32)).astype(BF16)
        other = jnp.where(high, three[0].astype(F32), three[2].astype(F32)).astype(BF16)
        return mine, three[1], other

    @pl.when(kind == 0)
    def _():
        mine_ref[0], mine_ref[1], lent_ref[...] = dealt(turned())

    @pl.when(kind == 1)
    def _():
        keep_ref[0], shared, give_ref[0] = dealt(turned())
        keep_ref[1] = shared
        give_ref[1] = shared

    @pl.when(kind == 2)
    def _():
        keep_ref[2], shared, give_ref[2] = dealt([h.astype(BF16) for h in heads])
        keep_ref[3] = shared
        give_ref[3] = shared


def projected(at, pieces, mod, w_kinds, gains, cosine, sine):
    def out(n):
        return jax.ShapeDtypeStruct((n, TOK, HD), BF16)

    return pl.pallas_call(
        project_kernel,
        grid=(3,),
        in_specs=[SMEM]
        + [VMEM] * 5
        + [
            pl.BlockSpec((None, D, 3 * HD), lambda k: (k, 0, 0)),
            pl.BlockSpec((None, 3, HD), lambda k: (jnp.minimum(k, 1), 0, 0)),
            VMEM,
            VMEM,
        ],
        out_specs=(
            whole((HALF, D)),
            whole((HALF, D)),
            whole((4, TOK, HD)),
            whole((4, TOK, HD)),
            whole((2, TOK, HD)),
            whole((TOK, HD)),
        ),
        out_shape=(
            jax.ShapeDtypeStruct((HALF, D), BF16),
            jax.ShapeDtypeStruct((HALF, D), BF16),
            out(4),
            out(4),
            out(2),
            jax.ShapeDtypeStruct((TOK, HD), BF16),
        ),
        scratch_shapes=[pltpu.VMEM((TOK, D), BF16)],
        cost_estimate=cost(2 * TOK * D * 9 * HD, 11e6),
        name="project",
    )(at, *pieces, mod, w_kinds, gains, cosine, sine)


def assemble_kernel(at_ref, *refs):
    z = at_ref[7]
    turns = (0, 7, 1, 6, 2, 5, 3, 4, 4)
    for k, by in enumerate(turns):
        begin = lax.rem(z + by, 8) * 96 + (48 if k == 8 else 0)
        rows = pl.ds(pl.multiple_of(begin, 16), refs[k].shape[0])
        refs[9][rows, :] = refs[k][:, :WID]
        refs[10][rows, :] = refs[k][:, WID:]


def assembled(at, parts):
    return pl.pallas_call(
        assemble_kernel,
        in_specs=[SMEM] + [VMEM] * 9,
        out_shape=[jax.ShapeDtypeStruct((WID, WID), BF16)] * 2,
        cost_estimate=cost(1e5, 5e6),
        name="assemble",
    )(at, *parts)


def gathered_rows(halves, rows_ref):
    for i in range(2):

        @pl.when(pl.program_id(0) == i)
        def _():
            rows_ref[:HALF] = halves[2 * i][...]
            rows_ref[HALF:] = halves[2 * i + 1][...]


def hidden_part(at_ref, rows_ref, j, w_ref):
    x = lax.rem(at_ref[8] + j, 4)
    lanes = pl.ds(pl.multiple_of(x * WID, WID), WID)
    return jnp.dot(rows_ref[:, lanes], w_ref[...], preferred_element_type=F32)


def hidden_kernel(at_ref, *refs):
    out_ref, rows_ref = refs[-2:]
    gathered_rows(refs[:4], rows_ref)
    total = hidden_part(at_ref, rows_ref, 0, refs[4])
    for j in range(1, 4):
        total = total + hidden_part(at_ref, rows_ref, j, refs[4 + j])
    cubic = total + 0.044715 * (total * total * total)
    hidden = total * (0.5 + 0.5 * jnp.tanh(math.sqrt(2.0 / math.pi) * cubic))
    out_ref[...] = hidden.astype(BF16)


def down_kernel(at_ref, hidden_ref, *refs):
    out_ref = refs[-1]
    for j in range(4):
        spot = at_ref[9 + j]
        down = lax.dot_general(
            hidden_ref[...], refs[j][...], (((1,), (1,)), ((), ())), preferred_element_type=F32
        )
        out_ref[lax.rem(spot, 2), spot // 2] = down.astype(BF16)


def hidden_units(at, halves, w0, w1, w2, w3):
    return pl.pallas_call(
        hidden_kernel,
        grid=(2,),
        in_specs=[SMEM] + [VMEM] * 8,
        out_specs=pl.BlockSpec((None, TOK, WID), lambda i: (i, 0, 0)),
        out_shape=jax.ShapeDtypeStruct((2, TOK, WID), BF16),
        scratch_shapes=[pltpu.VMEM((TOK, D), BF16)],
        cost_estimate=cost(8 * 2 * TOK * WID * WID, 9e6),
        name="mlp_hidden",
    )(at, *halves, w0, w1, w2, w3)


def down_products(at, hidden, w0, w1, w2, w3):
    return pl.pallas_call(
        down_kernel,
        grid=(2,),
        in_specs=[SMEM, pl.BlockSpec((None, TOK, WID), lambda i: (i, 0, 0))] + [VMEM] * 4,
        out_specs=pl.BlockSpec((2, 2, None, TOK, WID), lambda i: (0, 0, i, 0, 0)),
        out_shape=jax.ShapeDtypeStruct((2, 2, 2, TOK, WID), BF16),
        cost_estimate=cost(8 * 2 * TOK * WID * WID, 9e6),
        name="mlp_down",
    )(at, hidden, w0, w1, w2, w3)


def add_kernel(same_ref, crossed_ref, *outs):
    for i in range(4):
        total = same_ref[i // 2, i % 2].astype(F32) + crossed_ref[i // 2, i % 2].astype(F32)
        outs[i][...] = total.astype(BF16)


def added(same, crossed):
    rows = TOK // 3
    both = pl.BlockSpec((2, 2, rows, WID), lambda i: (0, 0, i, 0))
    near = pl.BlockSpec((None, 2, 2, rows, WID), lambda i: (0, 0, 0, i, 0))
    return pl.pallas_call(
        add_kernel,
        grid=(3,),
        in_specs=[near, both],
        out_specs=[pl.BlockSpec((rows, WID), lambda i: (i, 0))] * 4,
        out_shape=[jax.ShapeDtypeStruct((TOK, WID), BF16)] * 4,
        cost_estimate=cost(4 * TOK * WID, 6e6),
        name="add_cores",
    )(same, crossed)


def attend_kernel(first, last, makers, *refs):
    count = len(makers)
    at_ref, own_ref, taken_ref = refs[:3]
    kv = refs[3 : 3 + 2 * count]
    rest = refs[3 + 2 * count :]
    if not first:
        stat_in, acc_in = rest[:2]
        rest = rest[2:]
    taken = jnp.full((TOK, HD), pl.program_id(0), jnp.int32) == 1
    queries = jnp.where(taken, taken_ref[...].astype(F32), own_ref[...].astype(F32)).astype(BF16)
    keys = jnp.concatenate([r[...] for r in kv[:count]], axis=0)
    values = jnp.concatenate([r[...] for r in kv[count:]], axis=0)
    token = lax.broadcasted_iota(jnp.int32, (1, count * TOK), 1)
    place = jnp.zeros((1, count * TOK), jnp.int32)
    for n, (by, side) in enumerate(makers):
        row = at_ref[2] if side == 0 else 1 - at_ref[2]
        start = (row * 8 + lax.rem(at_ref[7] + by, 8) - n) * TOK
        place = jnp.where(token >= n * TOK, token + start, place)
    live = (place >= TXT) | (place < at_ref[13])
    bias = jnp.where(live, 0.0, MASKED).astype(F32)
    scores = lax.dot_general(
        queries, keys, (((1,), (1,)), ((), ())), preferred_element_type=F32
    )
    scores = scores + bias
    peak = jnp.max(scores, axis=1, keepdims=True)
    if not first:
        peak = jnp.maximum(peak, stat_in[:, 0:1])
    weights = jnp.exp2((scores - peak) * EXP2_SCALE)
    total = jnp.sum(weights, axis=1, keepdims=True)
    acc = jnp.dot(weights.astype(BF16), values, preferred_element_type=F32)
    if not first:
        fade = jnp.exp2((stat_in[:, 0:1] - peak) * EXP2_SCALE)
        total = total + fade * stat_in[:, 64:65]
        acc = acc + fade * acc_in[...]
    if last:
        out_ref, lent_ref, top_ref = rest
        done = (acc / total).astype(BF16)

        @pl.when(pl.program_id(0) != 1)
        def _():
            out_ref[pl.program_id(0) // 2] = done

        @pl.when(pl.program_id(0) == 1)
        def _():
            lent_ref[...] = done

        top_ref[...] = jnp.broadcast_to(jnp.max(peak, axis=0, keepdims=True) * SCORE_SCALE, (8, HD))
    else:
        stat_ref, acc_ref = rest
        lane = lax.broadcasted_iota(jnp.int32, (TOK, HD), 1)
        stat_ref[...] = jnp.where(lane < 64, peak, total)
        acc_ref[...] = acc


def attended_more(at, own_q, taken_q, makers, keys, values, carry, last):
    count = len(makers)
    first = carry is None
    unit = pl.BlockSpec((None, TOK, HD), lambda u: (u, 0, 0))
    shared = pl.BlockSpec((None, TOK, HD), lambda u: (u // 2, 0, 0))
    later = pl.BlockSpec((None, TOK, HD), lambda u: (2 + u // 2, 0, 0))
    specs = [SMEM, shared, whole((TOK, HD))] + [shared] * count
    specs += [later] * count
    args = [at, own_q, taken_q, *keys, *values]
    if not first:
        specs += [unit, unit]
        args += list(carry)
    state = jax.ShapeDtypeStruct((3, TOK, HD), F32)
    if last:
        outs = (
            jax.ShapeDtypeStruct((2, TOK, HD), BF16),
            jax.ShapeDtypeStruct((TOK, HD), BF16),
            jax.ShapeDtypeStruct((3, 8, HD), F32),
        )
        out_specs = (
            whole((2, TOK, HD)),
            whole((TOK, HD)),
            pl.BlockSpec((None, 8, HD), lambda u: (u, 0, 0)),
        )
    else:
        outs, out_specs = (state, state), (unit, unit)
    width = count * TOK
    return pl.pallas_call(
        functools.partial(attend_kernel, first, last, makers),
        grid=(3,),
        in_specs=specs,
        out_specs=out_specs,
        out_shape=outs,
        cost_estimate=cost(3 * TOK * width * HD * 4, 4e6, 3 * TOK * width),
        name="attend",
    )(*args)


def finish_kernel(*refs):
    state_ref, gate_ref, wf_ref, top_ref = refs[:4]
    parts = refs[4:8]
    heads = refs[8:12]
    wout = refs[12:16]
    new_ref, stat_ref = refs[16:]
    update = parts[0][...].astype(F32)
    for r in parts[1:]:
        update = update + r[...].astype(F32)
    for h, w in zip(heads, wout):
        update = update + jnp.dot(h[...], w[...], preferred_element_type=F32)
    new = (state_ref[...].astype(F32) + gate_ref[...] * update).astype(BF16)
    new_ref[...] = new
    wide = new.astype(F32)
    squares = jnp.sum(wide * wide, axis=1, keepdims=True)
    lane = lax.broadcasted_iota(jnp.int32, (TOK, HD), 1)
    stats = jnp.dot(new, wf_ref[...], preferred_element_type=F32)
    stats = jnp.where(lane == 65, squares, stats)
    total = jnp.sum(squares, axis=0, keepdims=True)
    ones = jnp.ones((16, WID), BF16)
    extra = jnp.dot(ones, wf_ref[...], preferred_element_type=F32)[:8]
    lane8 = lax.broadcasted_iota(jnp.int32, (8, HD), 1)
    top = jnp.max(top_ref[...], axis=0)
    extra = jnp.where(lane8 == 66, total, jnp.where(lane8 == 67, top, extra))
    for h in range(8):
        half = h // 4
        stat_ref[h, :HALF, :] = stats[half * HALF : (half + 1) * HALF]
        stat_ref[h, HALF:, :] = extra


def finished(state, gate, wf, top, parts, heads, wout):
    return pl.pallas_call(
        finish_kernel,
        out_shape=(
            jax.ShapeDtypeStruct((TOK, WID), BF16),
            jax.ShapeDtypeStruct((8, HALF + 8, HD), F32),
        ),
        cost_estimate=cost(2 * TOK * 1536 * WID, 6e6),
        name="finish",
    )(state, gate, wf, top, *parts, *heads, *wout)


def sums_kernel(got_ref, sums_ref):
    total, top = got_ref[0, HALF : HALF + 1, :], got_ref[0, HALF : HALF + 1, :]
    for i in range(1, 8):
        total = total + got_ref[i, HALF : HALF + 1, :]
        top = jnp.maximum(top, got_ref[i, HALF : HALF + 1, :])
    lane = lax.broadcasted_iota(jnp.int32, (1, HD), 1)
    row = jnp.where(lane == 67, top, total)
    for i in range(32):
        sums_ref[i] = row


def latent_kernel(guide_ref, got_ref, latent_ref, next_ref):
    def velocity(h):
        total = got_ref[4 * h] + got_ref[4 * h + 1] + got_ref[4 * h + 2] + got_ref[4 * h + 3]
        mean = total[:HALF, 64:65] / D
        spread = total[:HALF, 65:66] / D - mean * mean
        product = total[:HALF, :64] - mean * total[HALF : HALF + 1, :64]
        return product * lax.rsqrt(spread + EPS)

    cond, uncond = velocity(0), velocity(1)
    step, scale = guide_ref[0], guide_ref[1]
    next_ref[...] = latent_ref[...] + step * (uncond + scale * (cond - uncond))


def block_sums(got):
    return pl.pallas_call(
        sums_kernel,
        in_specs=[pl.BlockSpec((8, HALF + 8, HD), lambda *_: (0, 0, 0))],
        out_shape=jax.ShapeDtypeStruct((32, 1, HD), F32),
        cost_estimate=cost(1e4, 7e5),
        name="block_sums",
    )(got)


def next_latents(guide, got, latent):
    return pl.pallas_call(
        latent_kernel,
        in_specs=[SMEM, whole(got.shape), whole(latent.shape)],
        out_specs=whole(latent.shape),
        out_shape=jax.ShapeDtypeStruct(latent.shape, F32),
        cost_estimate=cost(4e5, 7e5),
        name="next_latent",
    )(guide, got, latent)


def body(
    state,
    latent,
    w_mod,
    w_qkv,
    w_mlp_in,
    q_gain,
    k_gain,
    w_out,
    w_mlp_down,
    w_final,
    text_len,
    rope_ids,
    guidance,
    step_index,
):
    xh, xl, z, yl, yh, core = (lax.axis_index(a) for a in ALL)
    tp = 2 * yh + core
    x = 2 * xh + xl
    blocks = [(tp ^ r) * WID for r in range(4)]
    owners = [((x + j) % 4) ^ tp for j in range(4)]
    flat_len = text_len.reshape(2 * REQ)
    own_len = jnp.sum(
        jnp.where(jnp.arange(2 * REQ, dtype=jnp.int32) == xh * 2 + yl, flat_len, 0)
    )
    at = jnp.stack([yh, core, xl, *blocks, z, x, *owners, own_len]).astype(jnp.int32)

    both = jnp.stack([w_mlp_in, w_mlp_down])
    keep = lax.dynamic_slice_in_dim(both, yl * WID, WID, 2)
    give = lax.dynamic_slice_in_dim(both, (1 - yl) * WID, WID, 2)
    taken = flip(give, "yl", 1)
    low = jnp.where(yl == 0, keep, taken)
    high = jnp.where(yl == 0, taken, keep)
    rows96 = jnp.concatenate([low, high], axis=1)
    rows96 = jnp.concatenate([rows96[0], rows96[1]], axis=1)
    w_up1 = turn(rows96, "z", 1)
    w_dn1 = turn(rows96, "z", -1)
    w_up2 = turn(rows96, "z", 2)
    w_dn2 = turn(rows96, "z", -2)
    w_up3 = turn(w_up2, "z", 1)
    w_dn3 = turn(w_dn2, "z", -1)
    w_up4 = turn(w_up2[:48], "z", 2)
    w_dn4 = turn(w_dn2[48:], "z", -2)
    w_parts = [rows96, w_up1, w_dn1, w_up2, w_dn2, w_up3, w_dn3, w_up4, w_dn4]
    in_here, down_here = assembled(at, w_parts)
    in_before = turn(in_here, X, 1)
    in_after = turn(in_here, X, -1)
    in_far = turn(in_before, X, 1)
    down_before = turn(down_here, X, 1)
    down_after = turn(down_here, X, -1)
    down_far = turn(down_after, X, -1)

    s_oc = flip(state, "c", 1)
    s_far = flip(state, "yh", 1)
    s_foc = flip(s_far, "c", 1)

    sigma_now = sigma_of(step_index)
    step_size = sigma_of(step_index + 1) - sigma_now
    time_rows = jax.nn.silu(time_embedding(sigma_now, tp * WID, WID)).astype(BF16)
    partial_mod = jnp.dot(time_rows, w_mod, preferred_element_type=F32)
    sent = jnp.repeat(partial_mod, 128, axis=0)[:, None, :]
    got = exchange(sent, ALL)
    mod = flattened(got.reshape(256, 144))
    gate = lax.dynamic_slice_in_dim(mod, 2 * D + tp * WID, WID, 1)

    cosine, sine = rope_tables(rope_ids)
    w_kinds = w_qkv.transpose(1, 0, 2)
    gains = jnp.stack([q_gain, k_gain])
    pieces = (state, s_oc, s_far, s_foc)
    mine_low, mine_high, own_kv, give_kv, own_q, give_q = projected(
        at, pieces, mod, w_kinds, gains, cosine, sine
    )
    taken_kv = flip(give_kv, "xl", 1)
    taken_q = flip(give_q, "xl", 1)
    other_low = flip(mine_low, "yl", 1)
    other_high = flip(mine_high, YY, 3)

    ups, dns, seen, makers = [own_kv, taken_kv], [own_kv, taken_kv], [own_kv, taken_kv], [(0, 0), (0, 1)]
    carry = None
    for k in range(1, 4):
        for side in range(2):
            ups[side] = turn(ups[side], "z", 1)
            dns[side] = turn(dns[side], "z", -1)
        seen = seen + ups + dns
        makers = makers + [(8 - k, 0), (8 - k, 1), (k, 0), (k, 1)]
        if k != 2:
            carry = attended_more(at, own_q, taken_q, tuple(makers), seen, seen, carry, False)
            seen, makers = [], []
    ends = [turn(ups[0], "z", 1), turn(dns[1], "z", -1)]
    out, lent, top = attended_more(at, own_q, taken_q, ((4, 0), (4, 1)), ends, ends, carry, True)

    halves = (mine_low, mine_high, other_low, other_high)
    hidden = hidden_units(at, halves, in_here, in_after, in_far, in_before)
    products = down_products(at, hidden, down_here, down_after, down_far, down_before)
    crossed = flip(products[1], "c", 1)
    near_own, near_yl, away_own, away_yl = added(products, crossed)
    part_yl = flip(near_yl, "yl", 1)
    part_far = flip(away_own, "yh", 1)
    part_both = flip(away_yl, YY, 3)

    def wout_for(r):
        return lax.dynamic_slice_in_dim(w_out, (tp ^ r) * WID, WID, 1)

    wout = [
        wout_for(0), flip(wout_for(1), "c", 1), flip(wout_for(2), "yh", 1), flip(wout_for(3), TP, 3)
    ]
    returned = flip(lent, "xl", 1)
    low_head = jnp.where(xl == 0, out[0], returned)
    high_head = jnp.where(xl == 0, returned, out[0])
    heads = jnp.concatenate([low_head, out[1], high_head], axis=1)
    h_oc = flip(heads, "c", 1)
    h_far = flip(heads, "yh", 1)
    h_foc = flip(h_far, "c", 1)

    extra = [jnp.ones((WID, 1), BF16), jnp.zeros((WID, HD - 65), BF16)]
    wf = jnp.concatenate([w_final, *extra], 1)
    parts = (near_own, part_yl, part_far, part_both)
    new_state, stats = finished(state, gate, wf, top, parts, (heads, h_oc, h_far, h_foc), wout)

    got_rows = exchange(stats, Y8)
    request_pick = jnp.arange(REQ, dtype=jnp.int32) == xh
    guide_scale = jnp.sum(jnp.where(request_pick, guidance, 0)).astype(F32) / 2.0
    own_step = jnp.sum(jnp.where(request_pick, step_size, 0.0))
    guide = jnp.stack([own_step, guide_scale])
    every = exchange(block_sums(got_rows), XZ)
    next_latent = next_latents(guide, got_rows, latent)
    every = every.reshape(2, 16, HD)
    state_norm = jnp.sqrt(jnp.sum(every[:, :, 66], axis=1) / (2.0 * SEQ_LEN * D))
    top_score = jnp.max(every[:, :, 67], axis=1)
    return (new_state, next_latent, state_norm, top_score)


def solution(mesh):
    split = Mesh(mesh.devices.reshape(2, 2, 8, 2, 2, 2), ALL)
    return jax.shard_map(
        body,
        mesh=split,
        in_specs=(
            P(SEQ, TP),
            P(SEQ, None),
            P(TP, SEQ),
            P(None, None, TP),
            P(SEQ, TP),
            P(TP, None),
            P(TP, None),
            P(TP, None),
            P(SEQ, TP),
            P(TP, None),
            P(),
            P(None, SEQ),
            P(),
            P(),
        ),
        out_specs=(P(SEQ, TP), P(SEQ, None), P(), P()),
        check_vma=False,
    )
```
